32 devices in a mesh: dir: 2 (over x), slab: 8 (over z, y), tile: 2 (over core).
Axes of the slice: x: 2, y: 2, z: 4, core: 2. Of those that a mesh axis runs over, the one named last changes fastest.
Arguments:
- voxels: float32 [4, 64, 64, 512], P(None, 'slab', 'tile'), may hold values from -2.5 to 2.5
- offsets: int32 [2, 64, 512], P('dir', 'tile'), may hold values from 0 to 511
- heading: int32 [2, 64, 512], P('dir', 'tile'), may hold values from 0 to 1
- cotangent: float32 [2, 3, 64, 512], P('dir', None, 'tile'), may hold values from -6 to 6
Outputs:
- image: float32 [2, 3, 64, 512], P('dir', None, 'tile', 'slab')
- voxel_grad: float32 [4, 64, 64, 512], P(None, 'slab', 'tile', 'dir')
The draws below stay inside these ranges and needn't reach their ends.
Inputs may be any that keep to these rules, and one draw needn't show every extreme that they name: `offsets`: A code packs three sub-cell positions as p + 8 * m + 8 * 8 * n (p along depth, m along rows, n along columns).
All inputs are finite; a program needn't handle non-finite values.
Results may differ from the reference program's by a relative error of at most 0.0003.
Values sent between devices are 32-bit elements; how exact they have to be, the bound alone decides.
No kernel may reach another device: no remote copies, remote signals or barrier semaphores. Data moves between devices by JAX's collectives and lax.ppermute only.
A program may use at most 64 MiB of HBM per device.

```python
import jax
import jax.numpy as jnp
from jax import lax

CHANNELS = 4
LEVELS = 8
NX = 512
GROUPS = 2
NZ = 64
NY = 64


def with_ends(drawn, stream_key, smallest, high):
    longest = drawn.shape.index(max(drawn.shape))
    spots = []
    for shift in (0, 1):
        where = [jax.random.randint(jax.random.fold_in(stream_key, axis), (), 0, length) for axis, length in enumerate(drawn.shape)]
        where[longest] = (where[longest] + shift) % drawn.shape[longest]
        spots.append(tuple(where))
    return drawn.at[spots[0]].set(smallest).at[spots[1]].set(high)


def level_of(key, shape, cuts, least, top_value):
    level = 1.0
    for dim, shards_of in cuts:
        steps = jax.random.uniform(jax.random.fold_in(jax.random.fold_in(key, 6), dim), (shards_of,), jnp.float32, least / len(cuts), top_value / len(cuts))
        level = level * jnp.repeat(jnp.exp(steps), shape[dim] // shards_of).reshape((-1,) + (1,) * (len(shape) - 1 - dim))
    return level


def bell_draw(rng, extent, width, bound, cuts=(), kind=jnp.bfloat16):
    loudness = level_of(rng, extent, cuts, -0.22, 0.18) if cuts else 1.0
    entries = jax.random.normal(rng, extent, jnp.float32) * width * loudness
    return jnp.minimum(jnp.maximum(entries, -bound), bound).astype(kind)


def setup_inputs(seed: int = 0) -> dict:
    seeds = jax.random.split(jax.random.key(seed), 5)
    return {
        "voxels": jnp.clip(jax.random.uniform(seeds[0], (CHANNELS, NZ, NY, NX), jnp.float32, -2.5, 2.5) * level_of(seeds[0], (CHANNELS, NZ, NY, NX), ((1, 8), (2, 2)), -0.4, 0.0), -2.5, 2.5),
        "offsets": with_ends(jax.random.randint(seeds[1], (GROUPS, NY, NX), 0, LEVELS * LEVELS * LEVELS), jax.random.fold_in(seeds[1], 1), 0, (LEVELS * LEVELS * LEVELS) - 1).astype(jnp.int32),
        "heading": with_ends(jax.random.randint(seeds[2], (GROUPS, NY, NX), 0, 2), jax.random.fold_in(seeds[2], 1), 0, 1).astype(jnp.int32),
        "cotangent": bell_draw(seeds[3], (GROUPS, 3, NY, NX), 1.0, 6.0, ((0, 2), (2, 2)), jnp.float32),
    }


def tap_weights(codes):
    level = LEVELS
    fz = (codes % level).astype(jnp.float32)
    fy = (codes // level % level).astype(jnp.float32)
    fx = (codes // (level * level)).astype(jnp.float32)

    def three(raw):
        f = (raw + 0.5) / level - 0.5
        return (jnp.maximum(-f, 0.0), 1.0 - jnp.abs(f), jnp.maximum(f, 0.0))
    return (three(fz), three(fy), three(fx))

def sample(vox, weights):
    wz, wy, wx = weights
    depth, rows, cols = (vox.shape[1], vox.shape[2], vox.shape[3])
    padded = jnp.pad(vox, ((0, 0), (1, 1), (1, 1), (1, 1)))
    plane = None
    for b in range(3):
        for e in range(3):
            term = wy[b] * wx[e] * padded[:, :, b:b + rows, e:e + cols]
            plane = term if plane is None else plane + term
    values = None
    for a in range(3):
        term = wz[a] * plane[:, a:a + depth]
        values = term if values is None else values + term
    return values

def render(vox, weights, head):
    values = sample(vox, weights)
    scale = 2.0 / NZ
    sigma = jax.nn.softplus(values[0]) * scale
    colour = jax.nn.sigmoid(values[1:])
    alpha = 1.0 - jnp.exp(-sigma)
    ahead = jnp.cumsum(sigma, axis=0) - sigma
    total = lax.optimization_barrier(jnp.sum(sigma, axis=0))
    front = jnp.where(head == 0, ahead, total - ahead - sigma)
    return lax.optimization_barrier(jnp.sum(jnp.exp(-front) * alpha * colour, axis=1))

def reference(voxels, offsets, heading, cotangent):

    def one(carry, items):
        codes, head, cot = items
        weights = tap_weights(codes)
        image, pull = jax.vjp(lambda grid: render(grid, weights, head), voxels)
        grad, = pull(cot * NZ)
        return (carry + grad, image)
    total, images = lax.scan(one, jnp.zeros_like(voxels), (offsets, heading, cotangent))
    return (images, total)
```

```python
import functools

import jax
import jax.numpy as jnp
from jax import lax
from jax.experimental import pallas as pl
from jax.experimental.pallas import tpu as pltpu
from jax.sharding import PartitionSpec as P

LEVELS = 8
BITS = LEVELS.bit_length() - 1
LANES = 128
SUB = 8
F32 = jnp.float32
VMEM = pl.BlockSpec(memory_space=pltpu.VMEM)
SMEM = pl.BlockSpec(memory_space=pltpu.SMEM)


def call(body, outs, scratch=(), aliases=None, flops=10**7, inputs=(), name=None):
    return pl.pallas_call(
        body,
        out_shape=outs,
        in_specs=list(inputs),
        out_specs=jax.tree.map(lambda _: VMEM, outs),
        scratch_shapes=list(scratch),
        input_output_aliases=aliases or {},
        cost_estimate=pl.CostEstimate(
            flops=flops, bytes_accessed=4 * 10**6, transcendentals=0
        ),
        compiler_params=pltpu.CompilerParams(vmem_limit_bytes=56 * 2**20),
        name=name,
    )


def shape(*dims):
    return jax.ShapeDtypeStruct(dims, F32)


def iota(dims, axis):
    return lax.broadcasted_iota(jnp.int32, dims, axis)


def three(raw):
    f = (raw.astype(F32) + 0.5) / LEVELS - 0.5
    return (jnp.maximum(-f, 0.0), 1.0 - jnp.abs(f), jnp.maximum(f, 0.0))


def taps_z(code):
    return three(code.astype(jnp.int32) & (LEVELS - 1))


def taps_yx(code):
    q = code.astype(jnp.int32)
    return (three((q >> BITS) & (LEVELS - 1)), three(q >> (2 * BITS)))


def message_rows(channels, rows, width):
    tiles = channels * (width // LANES)
    extra = -(-tiles // SUB) * SUB
    return tiles * rows, tiles * rows + extra, tiles * rows + extra + rows


def edge_column(tile, h):
    return jnp.where(h == 0, tile[:, :1], tile[:, LANES - 1 :])


def pack_body(info, first, last, second, penult, beside, a1, b1, a2, b2, *, width):
    h, _, s = (info[0], info[1], info[2])
    even = s % 2 == 0
    channels, _, rows, _ = first.shape
    tiles = width // LANES
    at_row, at_edge, _ = message_rows(channels, rows, width)
    planes = beside.shape[1]
    lane = iota((rows, LANES), 1)
    base = pl.multiple_of(h * width, LANES)
    side = pl.multiple_of(width - LANES * h, LANES)
    jobs = (
        (a1, last, planes - 1, first, 0),
        (b1, first, 0, last, planes - 1),
        (a2, penult, planes - 2, second, 1),
        (b2, second, 1, penult, planes - 2),
    )
    for out, when_even, k_even, when_odd, k_odd in jobs:

        def fill(block, k, out=out):
            edge = jnp.zeros((rows, LANES), F32)
            for c in range(channels):
                for j in range(tiles):
                    at = c * tiles + j
                    cols = pl.ds(base + j * LANES, LANES)
                    out[at * rows : (at + 1) * rows, :] = block[c, 0, :, cols]
                    out[at_row + at : at_row + at + 1, :] = beside[c, k : k + 1, cols]
                column = edge_column(block[c, 0, :, pl.ds(side, LANES)], h)
                corner = edge_column(beside[c, k : k + 1, pl.ds(side, LANES)], h)
                edge = jnp.where(lane == c, column, edge)
                edge = jnp.where(lane == channels + c, corner, edge)
            out[at_edge : at_edge + rows, :] = edge

        @pl.when(even)
        def _():
            fill(when_even, k_even)

        @pl.when(jnp.logical_not(even))
        def _():
            fill(when_odd, k_odd)


def shifts(window, column, h):
    dims = window.shape
    width = dims[1]
    lane = iota(dims, 1)
    left = jnp.where(h == 1, column, 0.0)
    right = jnp.where(h == 0, column, 0.0)
    minus = jnp.where(lane == 0, left, pltpu.roll(window, 1, 1))
    plus = jnp.where(lane == width - 1, right, pltpu.roll(window, width - 1, 1))
    return (minus, window, plus)


def spread_message(msg, grid, plane, h, channels, rows, width):
    tiles = width // LANES
    at_row, at_edge, _ = message_rows(channels, rows, width)
    edge = msg[at_edge : at_edge + rows, :]
    for c in range(channels):
        first = c * tiles
        window = jnp.concatenate(
            [msg[(first + j) * rows : (first + j + 1) * rows, :] for j in range(tiles)],
            axis=1,
        )
        beyond = jnp.concatenate(
            [msg[at_row + first + j : at_row + first + j + 1, :] for j in range(tiles)],
            axis=1,
        )
        beyond = jnp.broadcast_to(beyond, (SUB, width))
        corner = edge[:SUB, channels + c : channels + c + 1]
        for e, x in enumerate(shifts(window, edge[:, c : c + 1], h)):
            grid[e, c, plane, SUB : SUB + rows, :] = x
        for e, x in enumerate(shifts(beyond, corner, h)):
            grid[e, c, plane, 0:SUB, :] = x
            grid[e, c, plane, SUB + rows : 2 * SUB + rows, :] = x


def bilinear_weights(code, row0, t, rows):
    dims = code.shape
    wy, wx = taps_yx(code)
    row = iota(dims, 0) + row0
    low = jnp.where((row == 0) & (t == 0), 0.0, wy[0])
    high = jnp.where((row == rows - 1) & (t == 1), 0.0, wy[2])
    return [[y * x for x in wx] for y in (low, wy[1], high)]


def bilinear(weights, grid, c, plane, row0, cols):
    total = [None for _ in weights]
    for b in range(3):
        for e in range(3):
            v = grid[e, c, plane, row0 + b + SUB - 1 : row0 + b + 2 * SUB - 1, cols]
            for q, w in enumerate(weights):
                term = w[b][e] * v
                total[q] = term if total[q] is None else total[q] + term
    return total


def logistic(v):
    return 0.5 * jnp.tanh(0.5 * v) + 0.5


def forward_body(info, vox, beside, zlo, zhi, own, other, pay, vals, ends, grid, *, width, scale):
    h, t, s = (info[0], info[1], info[2])
    channels, planes, rows, _ = vox.shape
    base = pl.multiple_of(h * width, LANES)
    side = pl.multiple_of(width - LANES * h, LANES)
    even = s % 2 == 0
    rays = (own, other)

    def place(at, carry):
        c = at // planes
        k = at % planes
        window = vox[c, k, :, pl.ds(base, width)]
        column = edge_column(vox[c, k, :, pl.ds(side, LANES)], h)
        for e, x in enumerate(shifts(window, column, h)):
            grid[e, c, k + 1, SUB : SUB + rows, :] = x
        return carry

    lax.fori_loop(0, channels * planes, place, 0)
    for c in range(channels):
        window = beside[c, :, pl.ds(base, width)]
        column = edge_column(beside[c, :, pl.ds(side, LANES)], h)
        for e, x in enumerate(shifts(window, column, h)):
            for k in range(planes):
                grid[e, c, k + 1, SUB - 1 : SUB, :] = x[k : k + 1]
                grid[e, c, k + 1, SUB + rows : SUB + rows + 1, :] = x[k : k + 1]
    spread_message(zlo, grid, jnp.where(even, planes + 1, 0), h, channels, rows, width)
    spread_message(zhi, grid, jnp.where(even, 0, planes + 1), h, channels, rows, width)

    for i in range(rows // SUB):
        for j in range(width // LANES):
            row0 = i * SUB
            cols = slice(j * LANES, (j + 1) * LANES)
            codes = [r[0, row0 : row0 + SUB, cols] for r in rays]
            weights = [bilinear_weights(q, row0, t, rows) for q in codes]
            wz = [taps_z(q) for q in codes]

            def channel(c, carry, row0=row0, cols=cols, weights=weights, wz=wz):
                old = [None, None]
                for p in range(planes + 2):
                    new = bilinear(weights, grid, c, p, row0, cols)
                    for q in range(2):
                        if p == 1:
                            ends[q, c, 0, row0 : row0 + SUB, cols] = (
                                wz[q][1] * old[1][q] + wz[q][2] * new[q]
                            )
                        if p == planes + 1:
                            ends[q, c, 1, row0 : row0 + SUB, cols] = (
                                wz[q][0] * old[1][q] + wz[q][1] * new[q]
                            )
                        if p >= 2:
                            vals[q, c, p - 2, row0 : row0 + SUB, cols] = (
                                wz[q][0] * old[0][q]
                                + wz[q][1] * old[1][q]
                                + wz[q][2] * new[q]
                            )
                    old = [old[1], new]
                return carry

            lax.fori_loop(0, channels, channel, 0)

    tiles = width // LANES
    for q in range(2):

        def shade(at, carry, q=q):
            row = pl.ds(pl.multiple_of((at // tiles) * SUB, SUB), SUB)
            col = pl.ds(pl.multiple_of((at % tiles) * LANES, LANES), LANES)
            ahead = rays[q][1, row, col] == 0.0
            sigma = []
            for k in range(planes):
                v = vals[q, 0, k, row, col]
                sigma.append((jnp.maximum(v, 0.0) + jnp.log(1.0 + jnp.exp(-jnp.abs(v)))) * scale)
            total = functools.reduce(lambda a, b: a + b, sigma)
            run = jnp.zeros_like(total)
            light = [jnp.zeros_like(total) for _ in range(channels - 1)]
            for k in range(planes):
                front = jnp.where(ahead, run, total - run - sigma[k])
                glow = jnp.exp(-front) * (1.0 - jnp.exp(-sigma[k]))
                for c in range(channels - 1):
                    light[c] = light[c] + glow * logistic(vals[q, c + 1, k, row, col])
                run = run + sigma[k]
            pay[0, q, row, col] = total
            for c in range(channels - 1):
                pay[c + 1, q, row, col] = light[c]
            return carry

        lax.fori_loop(0, (rows // SUB) * tiles, shade, 0)


def column_body(info, zlo, zhi, own, other, vals, ends, out, grid, edge, *, width, scale, slabs):
    h, t, s = (info[0], info[1], info[2])
    _, channels, planes, rows, _ = vals.shape
    even = s % 2 == 0
    rays = (own, other)
    tiles = width // LANES
    spread_message(zlo, grid, jnp.where(even, 1, 0), h, channels, rows, width)
    spread_message(zhi, grid, jnp.where(even, 0, 1), h, channels, rows, width)
    for i in range(rows // SUB):
        for j in range(tiles):
            row0 = i * SUB
            cols = slice(j * LANES, (j + 1) * LANES)
            codes = [r[0, row0 : row0 + SUB, cols] for r in rays]
            weights = [bilinear_weights(q, row0, t, rows) for q in codes]
            wz = [taps_z(q) for q in codes]

            def channel(c, carry, row0=row0, cols=cols, weights=weights, wz=wz):
                at = slice(row0, row0 + SUB)
                for p in range(2):
                    new = bilinear(weights, grid, c, p, row0, cols)
                    for q in range(2):
                        edge[q, c, p, at, cols] = ends[q, c, p, at, cols] + wz[q][2 * p] * new[q]
                return carry

            lax.fori_loop(0, channels, channel, 0)

    for q in range(2):

        def shade(at, carry, q=q):
            row = pl.ds(pl.multiple_of((at // tiles) * SUB, SUB), SUB)
            col = pl.ds(pl.multiple_of((at % tiles) * LANES, LANES), LANES)
            ahead = rays[q][1, row, col] == 0.0
            wz = taps_z(rays[q][0, row, col])
            pull = [rays[q][2 + c, row, col] for c in range(channels - 1)]
            live = {-1: jnp.where(s > 0, 1.0, 0.0), planes: jnp.where(s < slabs - 1, 1.0, 0.0)}

            def value(c, k):
                if k < 0:
                    return edge[q, c, 0, row, col]
                if k == planes:
                    return edge[q, c, 1, row, col]
                return vals[q, c, k, row, col]

            ks = range(-1, planes + 1)
            sigma, slope = ({}, {})
            for k in ks:
                v = value(0, k)
                u = jnp.exp(-jnp.abs(v))
                sigma[k] = (jnp.maximum(v, 0.0) + jnp.log(1.0 + u)) * scale
                slope[k] = logistic(v) * scale
                if k in live:
                    slope[k] = slope[k] * live[k]
            total = functools.reduce(lambda a, b: a + b, [sigma[k] for k in range(planes)])
            run = -sigma[-1]
            share, after = ({}, {})
            tint = [{} for _ in range(channels - 1)]
            for k in ks:
                front = jnp.where(ahead, run, total - run - sigma[k])
                reach = jnp.exp(-front)
                left = jnp.exp(-sigma[k])
                glow = reach * (1.0 - left)
                if k in live:
                    glow = glow * live[k]
                hue = None
                for c in range(channels - 1):
                    colour = logistic(value(c + 1, k))
                    term = pull[c] * colour
                    hue = term if hue is None else hue + term
                    tint[c][k] = glow * term * (1.0 - colour)
                share[k] = glow * hue
                after[k] = reach * left * hue
                run = run + sigma[k]
            whole = functools.reduce(lambda a, b: a + b, [share[k] for k in range(planes)])
            run = -share[-1]
            pushed = {}
            for k in ks:
                before = jnp.where(ahead, run, whole - run - share[k])
                pushed[k] = (after[k] + before + share[k]) * slope[k]
                run = run + share[k]
            for at, field in enumerate([pushed, slope] + tint):
                for p in range(planes):
                    out[at, q, p, row, col] = (
                        wz[2] * field[p - 1] + wz[1] * field[p] + wz[0] * field[p + 1]
                    )
            return carry

        lax.fori_loop(0, (rows // SUB) * tiles, shade, 0)


def scatter_body(info, cols5, own, other, reach, rest, grad, ymsg, xmsg, weights, *, channels):
    h, t = (info[0], info[1])
    _, _, planes, rows, width = cols5.shape
    lane = iota((rows, width), 1)
    row = iota((rows, width), 0)
    tall = rows + SUB
    lane_tall = iota((tall, width), 1)
    lane_pack = iota((tall, LANES), 1)
    for q, r in enumerate((own, other)):
        wy, wx = taps_yx(r[0])
        for b in range(3):
            for e in range(3):
                weights[q, b * 3 + e] = wy[b] * wx[e]
    xmsg[...] = jnp.zeros(xmsg.shape, F32)

    def plane(p, carry):
        for c in range(channels):
            col = []
            for q in range(2):
                if c == 0:
                    col.append(reach[q] * cols5[0, q, p] - rest[q] * cols5[1, q, p])
                else:
                    col.append(reach[q] * cols5[c + 1, q, p])
            summed = []
            for e in range(3):
                part = [
                    weights[0, b * 3 + e] * col[0] + weights[1, b * 3 + e] * col[1]
                    for b in range(3)
                ]
                down = pltpu.roll(part[2], 1, 0)
                up = pltpu.roll(part[0], rows - 1, 0)
                main = part[1] + jnp.where(row == 0, 0.0, down) + jnp.where(row == rows - 1, 0.0, up)
                tail = jnp.where(t == 0, down[:SUB], pltpu.roll(up[rows - SUB :], 1, 0))
                summed.append(jnp.concatenate([main, tail], axis=0))
            right = pltpu.roll(summed[2], 1, 1)
            left = pltpu.roll(summed[0], width - 1, 1)
            both = (
                summed[1]
                + jnp.where(lane_tall == 0, 0.0, right)
                + jnp.where(lane_tall == width - 1, 0.0, left)
            )
            grad[c, p] = both[:rows]
            at = c * planes + p
            ymsg[pl.ds(at, 1), :] = both[rows : rows + 1]
            out = jnp.where(h == 0, right[:, :1], left[:, width - 1 :])
            xmsg[...] = jnp.where(lane_pack == at, out, xmsg[...])
        return carry

    lax.fori_loop(0, planes, plane, 0)
    ymsg[channels * planes : channels * planes + 1, :LANES] = xmsg[rows : rows + 1, :]


def finish_body(info, grad_in, yrow, xcol, grad):
    h, t = (info[0], info[1])
    channels, planes, rows, width = grad.shape
    row = iota((rows, width), 0)
    lane = iota((rows, width), 1)
    lane_pack = iota((rows, LANES), 1)
    at_row = row == jnp.where(t == 0, rows - 1, 0)
    at_lane = lane == jnp.where(h == 0, width - 1, 0)
    packed = xcol[...]
    for c in range(channels):
        for p in range(planes):
            at = c * planes + p
            both = jnp.where(at_row, yrow[at : at + 1, :], 0.0)
            both = both + jnp.where(at_lane, packed[:, at : at + 1], 0.0)
            grad[c, p] = grad_in[c, p] + both


def per_device(voxels, offsets, heading, cotangent):
    channels, planes, rows, total = voxels.shape
    colours = channels - 1
    dirs, slabs, cores = (lax.axis_size(a) for a in ("dir", "slab", "tile"))
    if dirs != 2 or cores != 2 or slabs & (slabs - 1):
        raise ValueError("mesh")
    width = total // dirs
    depth = planes * slabs
    scale = 2.0 / depth
    h, s, t = (lax.axis_index(a) for a in ("dir", "slab", "tile"))
    info = jnp.stack([h, t, s]).astype(jnp.int32)
    swap = [(0, 1), (1, 0)]
    tiles = width // LANES

    line = lax.dynamic_slice_in_dim(voxels, jnp.where(t == 0, rows - 1, 0), 1, axis=2)
    beside = lax.ppermute(line[:, :, 0], "tile", swap)

    _, _, height = message_rows(channels, rows, width)
    ks = (0, planes - 1, 1, planes - 2)

    def block(k):
        return pl.BlockSpec((channels, 1, rows, total), lambda i: (0, k, 0, 0))

    packed = pl.pallas_call(
        functools.partial(pack_body, width=width),
        grid=(1,),
        in_specs=[SMEM] + [block(k) for k in ks] + [VMEM],
        out_specs=[VMEM] * 4,
        out_shape=[shape(height, LANES)] * 4,
        name="pack",
    )(info, voxels, voxels, voxels, voxels, beside)
    pairs_a = [(i, i ^ 1) for i in range(slabs)]
    pairs_b = [(i, i + 1) for i in range(1, slabs - 1, 2)]
    pairs_b = pairs_b + [(b, a) for a, b in pairs_b]
    near_a = lax.ppermute(packed[0], "slab", pairs_a)
    near_b = lax.ppermute(packed[1], "slab", pairs_b)

    codes = jnp.concatenate(
        [offsets.astype(F32), heading.astype(F32), cotangent[0] * depth], axis=0
    )
    own = lax.dynamic_slice_in_dim(codes, h * width, width, axis=2)
    sent = lax.dynamic_slice_in_dim(codes, (1 - h) * width, width, axis=2)
    other = lax.ppermute(sent, "dir", swap)

    far_a = lax.ppermute(packed[2], "slab", pairs_a)
    far_b = lax.ppermute(packed[3], "slab", pairs_b)

    pay, vals, ends = call(
        functools.partial(forward_body, width=width, scale=scale),
        [
            shape(channels, 2, rows, width),
            shape(2, channels, planes, rows, width),
            shape(2, channels, 2, rows, width),
        ],
        scratch=[pltpu.VMEM((3, channels, planes + 2, rows + 2 * SUB, width), F32)],
        inputs=[SMEM] + [VMEM] * 6,
        name="forward",
    )(info, voxels, beside, near_a, near_b, own, other)

    cols5 = call(
        functools.partial(column_body, width=width, scale=scale, slabs=slabs),
        shape(channels + 1, 2, planes, rows, width),
        scratch=[
            pltpu.VMEM((3, channels, 2, rows + 2 * SUB, width), F32),
            pltpu.VMEM((2, channels, 2, rows, width), F32),
        ],
        inputs=[SMEM] + [VMEM] * 6,
        name="column",
    )(info, far_a, far_b, own, other, vals, ends)

    rays = jnp.stack([own, other], axis=1)
    forward = rays[1] == 0.0
    pull = rays[2:]
    before = jnp.zeros_like(pay[0])
    lead = jnp.zeros_like(pay[0])
    block_all = pay
    for bit in range(slabs.bit_length() - 1):
        theirs = lax.ppermute(block_all, "slab", [(i, i ^ (1 << bit)) for i in range(slabs)])
        lower = ((s >> bit) & 1) == 1
        earlier = lower == forward
        fade_theirs = jnp.exp(-theirs[0])
        fade_mine = jnp.exp(-block_all[0])
        light = jnp.where(
            earlier,
            theirs[1:] + fade_theirs * block_all[1:],
            block_all[1:] + fade_mine * theirs[1:],
        )
        weighted = jnp.sum(pull * theirs[1:], axis=0)
        lead = jnp.where(earlier, weighted + fade_theirs * lead, lead)
        before = jnp.where(earlier, before + theirs[0], before)
        block_all = jnp.concatenate([(block_all[0] + theirs[0])[None], light], axis=0)
    reach = jnp.exp(-before)
    rest = jnp.sum(pull * block_all[1:], axis=0) - lead

    grad, ymsg, xmsg = call(
        functools.partial(scatter_body, channels=channels),
        [
            shape(channels, planes, rows, width),
            shape(channels * planes + SUB, width),
            shape(rows + SUB, LANES),
        ],
        scratch=[pltpu.VMEM((2, 9, rows, width), F32)],
        inputs=[SMEM] + [VMEM] * 5,
        name="scatter",
    )(info, cols5, own, other, reach, rest)
    yrow = lax.ppermute(ymsg, "tile", swap)
    corner = yrow[channels * planes : channels * planes + 1, :LANES]
    at = jnp.arange(rows)[:, None] == jnp.where(t == 0, rows - 1, 0)
    xcol = lax.ppermute(xmsg[:rows] + jnp.where(at, corner, 0.0), "dir", swap)
    voxel_grad = call(
        finish_body,
        shape(channels, planes, rows, width),
        inputs=[SMEM] + [VMEM] * 3,
        aliases={1: 0},
        name="finish",
    )(info, grad, yrow, xcol)

    share = total // slabs
    half = slabs // dirs
    start = (s % half) * share
    mine = lax.dynamic_slice_in_dim(block_all[1:, 0], start, share, axis=2)
    sent = lax.dynamic_slice_in_dim(block_all[1:, 1], start, share, axis=2)
    got = lax.ppermute(sent, "dir", swap)
    image = jnp.where(s // half == h, mine, got)
    return (image[None], voxel_grad)


def solution(mesh):
    return jax.shard_map(
        per_device,
        mesh=mesh,
        in_specs=(
            P(None, "slab", "tile", None),
            P("dir", "tile", None),
            P("dir", "tile", None),
            P("dir", None, "tile", None),
        ),
        out_specs=(P("dir", None, "tile", "slab"), P(None, "slab", "tile", "dir")),
        check_vma=False,
    )
```

```python
import functools

import jax
import jax.numpy as jnp
from jax import lax
from jax.experimental import pallas as pl
from jax.experimental.pallas import tpu as pltpu
from jax.sharding import PartitionSpec as P

LEVELS = 8
BITS = LEVELS.bit_length() - 1
LANES = 128
SUB = 8
F32 = jnp.float32
VMEM = pl.BlockSpec(memory_space=pltpu.VMEM)
SMEM = pl.BlockSpec(memory_space=pltpu.SMEM)
MIB = 2**20


def call(body, name, outs, args, scratch=(), limit=16, flops=10**7, specs=None, **statics):
    inputs = [SMEM] + [VMEM] * (len(args) - 1)
    return pl.pallas_call(
        functools.partial(body, **statics),
        out_shape=outs,
        grid=() if specs is None else (1,),
        in_specs=specs or inputs,
        out_specs=jax.tree.map(lambda _: VMEM, outs),
        scratch_shapes=list(scratch),
        cost_estimate=pl.CostEstimate(
            flops=flops, bytes_accessed=2 * 10**6, transcendentals=0
        ),
        compiler_params=pltpu.CompilerParams(vmem_limit_bytes=limit * MIB),
        name=name,
    )(*args)


def shape(*dims):
    return jax.ShapeDtypeStruct(dims, F32)


def iota(dims, axis):
    return lax.broadcasted_iota(jnp.int32, dims, axis)


def fraction(raw):
    return (raw.astype(F32) + 0.5) / LEVELS - 0.5


def three(raw):
    f = fraction(raw)
    return (jnp.maximum(-f, 0.0), 1.0 - jnp.abs(f), jnp.maximum(f, 0.0))


def split_code(code):
    q = code.astype(jnp.int32)
    return (q & (LEVELS - 1), (q >> BITS) & (LEVELS - 1), q >> (2 * BITS))


def logistic(v):
    return 0.5 * jnp.tanh(0.5 * v) + 0.5


def total_of(terms):
    return functools.reduce(lambda a, b: a + b, terms)


def log_soft(v):
    return jnp.maximum(v, 0.0) + jnp.log(1.0 + jnp.exp(-jnp.abs(v)))


def shifts(tiles, beside, h):
    lane = iota(tiles[0].shape, 1)
    last = LANES - 1
    zero = jnp.zeros_like(beside)
    right = [pltpu.roll(x, 1, 1) for x in tiles]
    left = [pltpu.roll(x, last, 1) for x in tiles]
    below = [jnp.where(h == 1, beside, zero)] + right[:-1]
    above = left[1:] + [jnp.where(h == 0, beside, zero)]
    minus = [jnp.where(lane == 0, b, r) for b, r in zip(below, right)]
    plus = [jnp.where(lane == last, a, x) for a, x in zip(above, left)]
    return (minus, tiles, plus)


def beside_shift(source, h):
    target = jnp.where(h == 1, 0, LANES - 1)
    return lax.rem(target - source + LANES, LANES)


def window_parts(h, width):
    base = pl.multiple_of(h * width, LANES)
    side = pl.multiple_of(width - LANES * h, LANES)
    source = jnp.where(h == 0, 0, LANES - 1)
    return base, side, source


def pack_body(info, first, last, out_a, out_b, diag_a, diag_b, *, width):
    h, t, s = (info[0], info[1], info[2])
    even = s % 2 == 0
    channels, _, rows, _ = first.shape
    count = width // LANES
    base, side, source = window_parts(h, width)
    lane = iota((rows, LANES), 1)
    row = pl.multiple_of(jnp.where(t == 0, rows - SUB, 0), SUB)
    pick = iota((SUB, LANES), 0) == jnp.where(t == 0, SUB - 1, 0)
    lane8 = iota((SUB, LANES), 1)

    def fill(block, out, diag):
        edge = jnp.zeros((rows, LANES), F32)
        corner = jnp.zeros((SUB, LANES), F32)
        for c in range(channels):
            for j in range(count):
                at = c * count + j
                cols = pl.ds(base + j * LANES, LANES)
                out[at * rows : (at + 1) * rows, :] = block[c, 0, :, cols]
                line = jnp.where(pick, block[c, 0, pl.ds(row, SUB), cols], 0.0)
                diag[at : at + 1, :] = jnp.sum(line, axis=0, keepdims=True)
            turn = lax.rem(c - source + LANES, LANES)
            cols = pl.ds(side, LANES)
            edge = jnp.where(lane == c, pltpu.roll(block[c, 0, :, cols], turn, 1), edge)
            line = jnp.where(pick, block[c, 0, pl.ds(row, SUB), cols], 0.0)
            line = jnp.sum(line, axis=0, keepdims=True)
            line = pltpu.roll(jnp.broadcast_to(line, (SUB, LANES)), turn, 1)
            corner = jnp.where(lane8 == c, line, corner)
        out[channels * count * rows :, :] = edge
        diag[channels * count :, :] = corner

    @pl.when(even)
    def _():
        fill(last, out_a, diag_a)
        fill(first, out_b, diag_b)

    @pl.when(jnp.logical_not(even))
    def _():
        fill(first, out_a, diag_a)
        fill(last, out_b, diag_b)


def code_body(info, offsets, heading, cotangent, own, sent, *, width, depth):
    h = info[0]
    for out, at in ((own, h), (sent, 1 - h)):
        cols = pl.ds(pl.multiple_of(at * width, LANES), width)
        out[0] = offsets[0, :, cols].astype(F32)
        out[1] = heading[0, :, cols].astype(F32)
        for c in range(cotangent.shape[1]):
            out[2 + c] = cotangent[0, c, :, cols] * depth


def spread_message(msg, diag, grid, plane, info, channels, rows, count):
    h, t = (info[0], info[1])
    body = channels * count
    edge = msg[body * rows :, :]
    corner = diag[body:, :]
    beyond = pl.ds(pl.multiple_of(jnp.where(t == 0, SUB + rows, 0), SUB), SUB)
    for c in range(channels):
        turn = beside_shift(c, h)
        first = c * count
        tiles = [msg[(first + j) * rows : (first + j + 1) * rows, :] for j in range(count)]
        lines = [
            jnp.broadcast_to(diag[first + j : first + j + 1, :], (SUB, LANES))
            for j in range(count)
        ]
        for e, xs in enumerate(shifts(tiles, pltpu.roll(edge, turn, 1), h)):
            for j, x in enumerate(xs):
                grid[e, c, plane, SUB : SUB + rows, j * LANES : (j + 1) * LANES] = x
        for e, xs in enumerate(shifts(lines, pltpu.roll(corner, turn, 1), h)):
            for j, x in enumerate(xs):
                grid[e, c, plane, beyond, j * LANES : (j + 1) * LANES] = x


def taps(code, row0, t, rows):
    _, m, n = split_code(code)
    fy, fx = (fraction(m), fraction(n))
    row = iota(code.shape, 0) + row0
    low = (row == 0) & (t == 0)
    high = (row == rows - 1) & (t == 1)
    up = ((fy > 0.0) & jnp.logical_not(high)) | low
    ay, ax = (jnp.abs(fy), jnp.abs(fx))
    gone = (low & (fy < 0.0)) | (high & (fy > 0.0))
    by = jnp.where(gone, 0.0, ay)
    return (up, fx > 0.0, (1.0 - ay) * (1.0 - ax), (1.0 - ay) * ax, by * (1.0 - ax), by * ax)


def bilinear(rays, grid, c, plane, row0, cols):
    v = [
        [grid[e, c, plane, row0 + b + SUB - 1 : row0 + b + 2 * SUB - 1, cols] for e in range(3)]
        for b in range(3)
    ]
    out = []
    for up, right, centre, across, along, diagonal in rays:
        row = [jnp.where(up, v[2][e], v[0][e]) for e in range(3)]
        out.append(
            centre * v[1][1]
            + across * jnp.where(right, v[1][2], v[1][0])
            + along * row[1]
            + diagonal * jnp.where(right, row[2], row[0])
        )
    return out


def ray_tiles(rays, rows, width, t):
    for i in range(rows // SUB):
        for j in range(width // LANES):
            at = slice(i * SUB, (i + 1) * SUB)
            cols = slice(j * LANES, (j + 1) * LANES)
            codes = [r[0, at, cols] for r in rays]
            yield (
                i * SUB,
                at,
                cols,
                [taps(q, i * SUB, t, rows) for q in codes],
                [three(split_code(q)[0]) for q in codes],
            )


def each_tile(rows, width, body):
    count = width // LANES

    def step(n, carry):
        row = pl.ds(pl.multiple_of((n // count) * SUB, SUB), SUB)
        col = pl.ds(pl.multiple_of((n % count) * LANES, LANES), LANES)
        body(row, col)
        return carry

    lax.fori_loop(0, (rows // SUB) * count, step, 0)


def products(left):
    ones = jnp.ones_like(left[0])
    rising, falling = ([ones], [ones])
    for x in left[:-1]:
        rising.append(rising[-1] * x)
    for x in left[:0:-1]:
        falling.append(falling[-1] * x)
    return rising, falling[::-1]


def inner_body(info, vox, line, own, other, vals, part, ends, inner, grid, *, width, scale):
    h, t = (info[0], info[1])
    channels, planes, rows, _ = vox.shape
    count = width // LANES
    base, side, source = window_parts(h, width)
    turn = beside_shift(source, h)
    rays = (own, other)

    def place(k, carry):
        for c in range(channels):
            tiles = [vox[c, k, :, pl.ds(base + j * LANES, LANES)] for j in range(count)]
            beside = pltpu.roll(vox[c, k, :, pl.ds(side, LANES)], turn, 1)
            for e, xs in enumerate(shifts(tiles, beside, h)):
                for j, x in enumerate(xs):
                    grid[e, c, k, SUB : SUB + rows, j * LANES : (j + 1) * LANES] = x
        return carry

    lax.fori_loop(0, planes, place, 0)
    beyond = pl.ds(pl.multiple_of(jnp.where(t == 0, SUB + rows, 0), SUB), SUB)
    for c in range(channels):
        tiles = [line[c, :, pl.ds(base + j * LANES, LANES)] for j in range(count)]
        beside = pltpu.roll(line[c, :, pl.ds(side, LANES)], turn, 1)
        for e, xs in enumerate(shifts(tiles, beside, h)):
            for j, x in enumerate(xs):
                for k in range(planes):
                    grid[e, c, k, beyond, j * LANES : (j + 1) * LANES] = jnp.broadcast_to(
                        x[k : k + 1], (SUB, LANES)
                    )

    for row0, at, cols, yx, wz in ray_tiles(rays, rows, width, t):

        def channel(c, carry, row0=row0, at=at, cols=cols, yx=yx, wz=wz):
            old = [None, None]
            for p in range(planes):
                new = bilinear(yx, grid, c, p, row0, cols)
                for q in range(2):
                    w = wz[q]
                    if p == 0:
                        ends[q, c, 0, at, cols] = w[2] * new[q]
                    elif p == 1:
                        part[q, c, 0, at, cols] = w[1] * old[1][q] + w[2] * new[q]
                    else:
                        vals[q, c, p - 2, at, cols] = (
                            w[0] * old[0][q] + w[1] * old[1][q] + w[2] * new[q]
                        )
                    if p == planes - 1:
                        part[q, c, 1, at, cols] = w[0] * old[1][q] + w[1] * new[q]
                        ends[q, c, 1, at, cols] = w[0] * new[q]
                old = [old[1], new]
            return carry

        lax.fori_loop(0, channels, channel, 0)

    for q in range(2):

        def shade(row, col, q=q):
            ahead = rays[q][1, row, col] == 0.0
            sigma = [log_soft(vals[q, 0, k, row, col]) * scale for k in range(planes - 2)]
            left = [jnp.exp(-x) for x in sigma]
            rising, falling = products(left)
            light = [None] * (channels - 1)
            for k in range(planes - 2):
                glow = jnp.where(ahead, rising[k], falling[k]) * (1.0 - left[k])
                for c in range(channels - 1):
                    term = glow * logistic(vals[q, c + 1, k, row, col])
                    light[c] = term if k == 0 else light[c] + term
            inner[0, q, row, col] = total_of(sigma)
            for c in range(channels - 1):
                inner[c + 1, q, row, col] = light[c]

        each_tile(rows, width, shade)


def rim_body(info, near_a, near_b, diag_a, diag_b, own, other, part, ends, inner, pay, rim, ends_out, grid, *, scale):
    t, s = (info[1], info[2])
    _, channels, _, rows, width = part.shape
    count = width // LANES
    even = s % 2 == 0
    rays = (own, other)
    spread_message(near_a, diag_a, grid, jnp.where(even, 1, 0), info, channels, rows, count)
    spread_message(near_b, diag_b, grid, jnp.where(even, 0, 1), info, channels, rows, count)
    for row0, at, cols, yx, wz in ray_tiles(rays, rows, width, t):

        def channel(c, carry, row0=row0, at=at, cols=cols, yx=yx, wz=wz):
            for p in range(2):
                new = bilinear(yx, grid, c, p, row0, cols)
                for q in range(2):
                    rim[q, c, p, at, cols] = part[q, c, p, at, cols] + wz[q][2 * p] * new[q]
                    ends_out[q, c, p, at, cols] = ends[q, c, p, at, cols] + wz[q][1] * new[q]
            return carry

        lax.fori_loop(0, channels, channel, 0)
    for q in range(2):

        def shade(row, col, q=q):
            ahead = rays[q][1, row, col] == 0.0
            sigma = [log_soft(rim[q, 0, p, row, col]) * scale for p in range(2)]
            left = [jnp.exp(-x) for x in sigma]
            middle = inner[0, q, row, col]
            through = jnp.exp(-middle)
            first = jnp.where(ahead, left[0], left[1])
            last = first * through
            pay[0, q, row, col] = sigma[0] + middle + sigma[1]
            low = jnp.where(ahead, 1.0, last) * (1.0 - left[0])
            high = jnp.where(ahead, last, 1.0) * (1.0 - left[1])
            for c in range(channels - 1):
                pay[c + 1, q, row, col] = (
                    low * logistic(rim[q, c + 1, 0, row, col])
                    + first * inner[c + 1, q, row, col]
                    + high * logistic(rim[q, c + 1, 1, row, col])
                )

        each_tile(rows, width, shade)


def column_body(own, other, vals, rim, cols5, tail, *, scale):
    _, channels, inside, rows, width = vals.shape
    planes = inside + 2
    rays = (own, other)
    for q in range(2):

        def shade(row, col, q=q):
            ahead = rays[q][1, row, col] == 0.0
            wz = three(split_code(rays[q][0, row, col])[0])
            pull = [rays[q][2 + c, row, col] for c in range(channels - 1)]

            def value(c, k):
                if k == 0 or k == planes - 1:
                    return rim[q, c, 1 if k else 0, row, col]
                return vals[q, c, k - 1, row, col]

            ks = range(planes)
            sigma = [log_soft(value(0, k)) * scale for k in ks]
            slope = [logistic(value(0, k)) * scale for k in ks]
            left = [jnp.exp(-x) for x in sigma]
            rising, falling = products(left)
            share, after = ([], [])
            tint = [[] for _ in range(channels - 1)]
            for k in ks:
                reach = jnp.where(ahead, rising[k], falling[k])
                glow = reach * (1.0 - left[k])
                hue = []
                for c in range(channels - 1):
                    colour = logistic(value(c + 1, k))
                    hue.append(pull[c] * colour)
                    tint[c].append(glow * hue[-1] * (1.0 - colour))
                hue = total_of(hue)
                share.append(glow * hue)
                after.append(reach * left[k] * hue)
            whole = total_of(share)
            run = jnp.zeros_like(whole)
            pushed = []
            for k in ks:
                upto = run + share[k]
                pushed.append((after[k] + jnp.where(ahead, upto, whole - run)) * slope[k])
                run = upto
            tail[0, q, row, col] = rising[-1] * left[-1]
            tail[1, q, row, col] = whole
            for n, field in enumerate([pushed, slope] + tint):
                for p in range(planes):
                    x = wz[1] * field[p]
                    if p > 0:
                        x = x + wz[2] * field[p - 1]
                    if p < planes - 1:
                        x = x + wz[0] * field[p + 1]
                    cols5[n, q, p, row, col] = x

        each_tile(rows, width, shade)


def outer_body(info, far_a, far_b, diag_a, diag_b, own, other, ends, tail, outer, grid, value, *, scale, slabs):
    t, s = (info[1], info[2])
    _, channels, _, rows, width = ends.shape
    count = width // LANES
    even = s % 2 == 0
    rays = (own, other)
    spread_message(far_a, diag_a, grid, jnp.where(even, 1, 0), info, channels, rows, count)
    spread_message(far_b, diag_b, grid, jnp.where(even, 0, 1), info, channels, rows, count)
    for row0, at, cols, yx, wz in ray_tiles(rays, rows, width, t):

        def channel(c, carry, row0=row0, at=at, cols=cols, yx=yx, wz=wz):
            for p in range(2):
                new = bilinear(yx, grid, c, p, row0, cols)
                for q in range(2):
                    value[q, c, p, at, cols] = ends[q, c, p, at, cols] + wz[q][2 * p] * new[q]
            return carry

        lax.fori_loop(0, channels, channel, 0)
    live = (jnp.where(s > 0, 1.0, 0.0), jnp.where(s < slabs - 1, 1.0, 0.0))
    for q in range(2):

        def shade(row, col, q=q):
            ahead = rays[q][1, row, col] == 0.0
            wz = three(split_code(rays[q][0, row, col])[0])
            pull = [rays[q][2 + c, row, col] for c in range(channels - 1)]
            through = tail[0, q, row, col]
            whole = tail[1, q, row, col]
            for p in range(2):
                v = value[q, 0, p, row, col]
                sigma = log_soft(v) * scale
                slope = logistic(v) * (scale * live[p])
                enters = ahead if p == 0 else jnp.logical_not(ahead)
                left = jnp.exp(-sigma)
                reach = jnp.where(enters, jnp.exp(sigma), through)
                glow = reach * (1.0 - left) * live[p]
                hue = []
                fields = []
                for c in range(channels - 1):
                    colour = logistic(value[q, c + 1, p, row, col])
                    hue.append(pull[c] * colour)
                    fields.append(glow * hue[-1] * (1.0 - colour))
                hue = total_of(hue)
                share = glow * hue
                upto = jnp.where(enters, 0.0, whole + share)
                pushed = (reach * left * hue + upto) * slope
                for n, field in enumerate([pushed, slope] + fields):
                    outer[n, q, p, row, col] = wz[2 - 2 * p] * field

        each_tile(rows, width, shade)


def merge_body(cols5, outer, reach, rest, columns, *, channels):
    _, _, planes, rows, width = cols5.shape

    def ray(row, col):
        for q in range(2):
            near, far = (reach[q, row, col], rest[q, row, col])
            for p in range(planes):
                side = None if 0 < p < planes - 1 else (0 if p == 0 else 1)

                def field(n):
                    x = cols5[n, q, p, row, col]
                    return x if side is None else x + outer[n, q, side, row, col]

                columns[0, q, p, row, col] = near * field(0) - far * field(1)
                for c in range(1, channels):
                    columns[c, q, p, row, col] = near * field(c + 1)

    each_tile(rows, width, ray)


def border_body(info, columns, own, other, line, edge):
    h, t = (info[0], info[1])
    channels, _, planes, rows, width = columns.shape
    count = width // LANES
    last = LANES - 1
    rays = (own, other)
    row0 = pl.multiple_of(jnp.where(t == 0, rows - SUB, 0), SUB)
    near = pl.ds(row0, SUB)
    take = jnp.where(t == 0, SUB - 1, 0)
    lane8 = iota((SUB, LANES), 1)
    pick = iota((SUB, LANES), 0) == take
    side = pl.ds(pl.multiple_of(jnp.where(h == 0, width - LANES, 0), LANES), LANES)
    down, across = ([], [])
    for r in rays:
        _, wy, wx = [three(x) for x in split_code(r[0, near, :])]
        y = jnp.where(t == 0, wy[2], wy[0])
        down.append([y * x for x in wx])
        _, wy, wx = [three(x) for x in split_code(r[0, :, side])]
        x = jnp.where(h == 0, wx[2], wx[0])
        across.append([y * x for y in wy])
    row = iota((rows, LANES), 0)
    lane = iota((rows, LANES), 1)
    source = jnp.where(h == 0, last, 0)
    edge[...] = jnp.zeros(edge.shape, F32)

    def channel(c, carry):
        for p in range(planes):
            at = c * planes + p
            strip = [columns[c, q, p, near, :] for q in range(2)]
            sums = []
            for e in range(3):
                x = total_of([down[q][e] * strip[q] for q in range(2)])
                x = jnp.sum(jnp.where(jnp.concatenate([pick] * count, axis=1), x, 0.0), axis=0, keepdims=True)
                sums.append(jnp.broadcast_to(x, (SUB, width)))
            plus = [sums[2][:, j * LANES : (j + 1) * LANES] for j in range(count)]
            minus = [sums[0][:, j * LANES : (j + 1) * LANES] for j in range(count)]
            plus = [pltpu.roll(x, 1, 1) for x in plus]
            minus = [pltpu.roll(x, last, 1) for x in minus]
            zero = jnp.zeros_like(plus[0])
            for j in range(count):
                x = sums[1][:, j * LANES : (j + 1) * LANES]
                x = x + jnp.where(lane8 == 0, plus[j - 1] if j else zero, plus[j])
                x = x + jnp.where(lane8 == last, minus[j + 1] if j < count - 1 else zero, minus[j])
                line[c, p : p + 1, j * LANES : (j + 1) * LANES] = x[:1]
            strip = [columns[c, q, p, :, side] for q in range(2)]
            part = [total_of([across[q][b] * strip[q] for q in range(2)]) for b in range(3)]
            lower = pltpu.roll(part[2], 1, 0)
            upper = pltpu.roll(part[0], rows - 1, 0)
            main = part[1] + jnp.where(row == 0, 0.0, lower) + jnp.where(row == rows - 1, 0.0, upper)
            over = jnp.where(t == 0, lower[:SUB], pltpu.roll(upper[rows - SUB :], 1, 0))
            turn = lax.rem(at - source + LANES, LANES)
            edge[:rows, :] = jnp.where(lane == at, pltpu.roll(main, turn, 1), edge[:rows, :])
            edge[rows:, :] = jnp.where(lane8 == at, pltpu.roll(over, turn, 1), edge[rows:, :])
        return carry

    lax.fori_loop(0, channels, channel, 0)


def scatter_body(columns, own, other, grad, weights):
    channels, _, planes, rows, width = columns.shape
    lane = iota((rows, width), 1)
    row = iota((rows, width), 0)
    for q, r in enumerate((own, other)):
        _, wy, wx = [three(x) for x in split_code(r[0])]
        for b in range(3):
            for e in range(3):
                weights[q, b * 3 + e] = wy[b] * wx[e]

    def plane(p, carry):
        for c in range(channels):
            col = [columns[c, q, p] for q in range(2)]
            summed = []
            for e in range(3):
                part = [
                    weights[0, b * 3 + e] * col[0] + weights[1, b * 3 + e] * col[1]
                    for b in range(3)
                ]
                down = pltpu.roll(part[2], 1, 0)
                up = pltpu.roll(part[0], rows - 1, 0)
                summed.append(
                    part[1] + jnp.where(row == 0, 0.0, down) + jnp.where(row == rows - 1, 0.0, up)
                )
            right = pltpu.roll(summed[2], 1, 1)
            left = pltpu.roll(summed[0], width - 1, 1)
            grad[c, p] = (
                summed[1]
                + jnp.where(lane == 0, 0.0, right)
                + jnp.where(lane == width - 1, 0.0, left)
            )
        return carry

    lax.fori_loop(0, planes, plane, 0)


def finish_body(info, grad_in, line, edge, corner, grad):
    h, t = (info[0], info[1])
    channels, planes, rows, width = grad.shape
    row = iota((rows, width), 0)
    lane = iota((rows, width), 1)
    last = jnp.where(t == 0, rows - 1, 0)
    at_row = row == last
    at_lane = lane == jnp.where(h == 0, width - 1, 0)
    packed = edge[...] + jnp.where(iota((rows, LANES), 0) == last, corner[:1], 0.0)

    for c in range(channels):
        for p in range(planes):
            at = c * planes + p
            both = jnp.where(at_row, line[c, p : p + 1, :], 0.0)
            both = both + jnp.where(at_lane, packed[:, at : at + 1], 0.0)
            grad[c, p] = grad_in[c, p] + both


def per_device(voxels, offsets, heading, cotangent):
    channels, planes, rows, total = voxels.shape
    dirs, slabs, cores = (lax.axis_size(a) for a in ("dir", "slab", "tile"))
    if dirs != 2 or cores != 2 or slabs & (slabs - 1):
        raise ValueError("mesh")
    width = total // dirs
    depth = planes * slabs
    scale = 2.0 / depth
    h, s, t = (lax.axis_index(a) for a in ("dir", "slab", "tile"))
    info = jnp.stack([h, t, s]).astype(jnp.int32)
    swap = [(0, 1), (1, 0)]
    count = width // LANES
    grid = lambda n: pltpu.VMEM((3, channels, n, rows + 2 * SUB, width), F32)

    pairs_a = [(i, i ^ 1) for i in range(slabs)]
    pairs_b = [(i, i + 1) for i in range(1, slabs - 1, 2)]
    pairs_b = pairs_b + [(b, a) for a, b in pairs_b]
    cross = lambda pairs: [
        (a * cores + i, b * cores + 1 - i) for a, b in pairs for i in range(cores)
    ]

    def halo(level):
        def block(k):
            return pl.BlockSpec((channels, 1, rows, total), lambda i: (0, k, 0, 0))

        big = shape(channels * count * rows + rows, LANES)
        small = shape(channels * count + SUB, LANES)
        packed = call(
            pack_body,
            f"pack{level}",
            [big, big, small, small],
            (info, voxels, voxels),
            specs=[SMEM, block(level), block(planes - 1 - level)],
            width=width,
        )
        with jax.named_scope(f"halo{level}"):
            return (
                lax.ppermute(packed[0], "slab", pairs_a),
                lax.ppermute(packed[1], "slab", pairs_b),
                lax.ppermute(packed[2], ("slab", "tile"), cross(pairs_a)),
                lax.ppermute(packed[3], ("slab", "tile"), cross(pairs_b)),
            )

    near = halo(0)
    own, sent = call(
        code_body,
        "codes",
        [shape(channels + 1, rows, width)] * 2,
        (info, offsets, heading, cotangent),
        width=width,
        depth=depth,
    )
    other = lax.ppermute(sent, "dir", swap)
    line = lax.dynamic_slice_in_dim(voxels, jnp.where(t == 0, rows - 1, 0), 1, axis=2)
    line = lax.ppermute(line[:, :, 0], "tile", swap)

    two = shape(2, channels, 2, rows, width)
    four = shape(channels, 2, rows, width)
    vals, part, ends, inner = call(
        inner_body,
        "inner",
        [shape(2, channels, planes - 2, rows, width), two, two, four],
        (info, voxels, line, own, other),
        scratch=[grid(planes)],
        limit=20,
        width=width,
        scale=scale,
    )
    pay, rim, ends = call(
        rim_body,
        "rim",
        [four, two, two],
        (info, *near, own, other, part, ends, inner),
        scratch=[grid(2)],
        scale=scale,
    )
    far = halo(1)

    cols5, tail = pl.pallas_call(
        functools.partial(column_body, scale=scale),
        out_shape=[shape(channels + 1, 2, planes, rows, width), shape(2, 2, rows, width)],
        in_specs=[VMEM] * 4,
        out_specs=[VMEM] * 2,
        cost_estimate=pl.CostEstimate(flops=10**7, bytes_accessed=2 * 10**6, transcendentals=0),
        compiler_params=pltpu.CompilerParams(vmem_limit_bytes=16 * MIB),
        name="column",
    )(own, other, vals, rim)
    outer = call(
        outer_body,
        "outer",
        shape(channels + 1, 2, 2, rows, width),
        (info, *far, own, other, ends, tail),
        scratch=[grid(2), pltpu.VMEM((2, channels, 2, rows, width), F32)],
        scale=scale,
        slabs=slabs,
    )

    rays = jnp.stack([own, other], axis=1)
    forward = rays[1] == 0.0
    pull = rays[2:]
    before = jnp.zeros_like(pay[0])
    lead = jnp.zeros_like(pay[0])
    block_all = pay
    for bit in range(slabs.bit_length() - 1):
        with jax.named_scope(f"scan{bit}"):
            theirs = lax.ppermute(block_all, "slab", [(i, i ^ (1 << bit)) for i in range(slabs)])
        lower = ((s >> bit) & 1) == 1
        earlier = lower == forward
        fade_theirs = jnp.exp(-theirs[0])
        fade_mine = jnp.exp(-block_all[0])
        light = jnp.where(
            earlier,
            theirs[1:] + fade_theirs * block_all[1:],
            block_all[1:] + fade_mine * theirs[1:],
        )
        weighted = jnp.sum(pull * theirs[1:], axis=0)
        lead = jnp.where(earlier, weighted + fade_theirs * lead, lead)
        before = jnp.where(earlier, before + theirs[0], before)
        block_all = jnp.concatenate([(block_all[0] + theirs[0])[None], light], axis=0)
    reach = jnp.exp(-before)
    rest = jnp.sum(pull * block_all[1:], axis=0) - lead

    plain = dict(
        compiler_params=pltpu.CompilerParams(vmem_limit_bytes=16 * MIB),
        cost_estimate=pl.CostEstimate(flops=10**7, bytes_accessed=2 * 10**6, transcendentals=0),
    )
    columns = pl.pallas_call(
        functools.partial(merge_body, channels=channels),
        out_shape=shape(channels, 2, planes, rows, width),
        in_specs=[VMEM] * 4,
        out_specs=VMEM,
        name="merge",
        **plain,
    )(cols5, outer, reach, rest)
    line, edge = call(
        border_body,
        "border",
        [shape(channels, planes, width), shape(rows + SUB, LANES)],
        (info, columns, own, other),
    )
    line = lax.ppermute(line, "tile", swap)
    corner = lax.ppermute(edge[rows:], ("dir", "tile"), [(i, 3 - i) for i in range(4)])
    edge = lax.ppermute(edge[:rows], "dir", swap)
    grad = pl.pallas_call(
        scatter_body,
        out_shape=shape(channels, planes, rows, width),
        in_specs=[VMEM] * 3,
        out_specs=VMEM,
        scratch_shapes=[pltpu.VMEM((2, 9, rows, width), F32)],
        name="scatter",
        **plain,
    )(columns, own, other)
    voxel_grad = call(
        finish_body,
        "finish",
        shape(channels, planes, rows, width),
        (info, grad, line, edge, corner),
    )

    share = total // slabs
    half = slabs // dirs
    start = (s % half) * share
    mine = lax.dynamic_slice_in_dim(block_all[1:, 0], start, share, axis=2)
    sent = lax.dynamic_slice_in_dim(block_all[1:, 1], start, share, axis=2)
    got = lax.ppermute(sent, "dir", swap)
    image = jnp.where(s // half == h, mine, got)
    return (image[None], voxel_grad)


def solution(mesh):
    return jax.shard_map(
        per_device,
        mesh=mesh,
        in_specs=(
            P(None, "slab", "tile", None),
            P("dir", "tile", None),
            P("dir", "tile", None),
            P("dir", None, "tile", None),
        ),
        out_specs=(P("dir", None, "tile", "slab"), P(None, "slab", "tile", "dir")),
        check_vma=False,
    )
```

```python
import functools

import jax
import jax.numpy as jnp
from jax import lax
from jax.experimental import pallas as pl
from jax.experimental.pallas import tpu as pltpu
from jax.sharding import PartitionSpec as P


LEVELS = 8
BITS = LEVELS.bit_length() - 1
LANES = 128
SUB = 8
F32 = jnp.float32
VMEM = pl.BlockSpec(memory_space=pltpu.VMEM)
SMEM = pl.BlockSpec(memory_space=pltpu.SMEM)
MIB = 2**20


def call(body, outs, args, scratch=(), limit=16, flops=10**7, specs=None, **statics):
    inputs = [SMEM] + [VMEM] * (len(args) - 1)
    return pl.pallas_call(
        functools.partial(body, **statics),
        out_shape=outs,
        grid=() if specs is None else (1,),
        in_specs=specs or inputs,
        out_specs=jax.tree.map(lambda _: VMEM, outs),
        scratch_shapes=list(scratch),
        cost_estimate=pl.CostEstimate(
            flops=flops, bytes_accessed=2 * 10**6, transcendentals=0
        ),
        compiler_params=pltpu.CompilerParams(vmem_limit_bytes=limit * MIB),
    )(*args)


def shape(*dims):
    return jax.ShapeDtypeStruct(dims, F32)


def iota(dims, axis):
    return lax.broadcasted_iota(jnp.int32, dims, axis)


def fraction(raw):
    return (raw.astype(F32) + 0.5) / LEVELS - 0.5


def three(raw):
    f = fraction(raw)
    return (jnp.maximum(-f, 0.0), 1.0 - jnp.abs(f), jnp.maximum(f, 0.0))


def split_code(code):
    q = code.astype(jnp.int32)
    return (q & (LEVELS - 1), (q >> BITS) & (LEVELS - 1), q >> (2 * BITS))


def logistic(v):
    return 0.5 * jnp.tanh(0.5 * v) + 0.5


def total_of(terms):
    return functools.reduce(lambda a, b: a + b, terms)


def log_soft(v):
    return jnp.maximum(v, 0.0) + jnp.log(1.0 + jnp.exp(-jnp.abs(v)))


def shifts(tiles, beside, h):
    lane = iota(tiles[0].shape, 1)
    last = LANES - 1
    zero = jnp.zeros_like(beside)
    right = [pltpu.roll(x, 1, 1) for x in tiles]
    left = [pltpu.roll(x, last, 1) for x in tiles]
    below = [jnp.where(h == 1, beside, zero)] + right[:-1]
    above = left[1:] + [jnp.where(h == 0, beside, zero)]
    minus = [jnp.where(lane == 0, b, r) for b, r in zip(below, right)]
    plus = [jnp.where(lane == last, a, x) for a, x in zip(above, left)]
    return (minus, tiles, plus)


def beside_shift(source, h):
    target = jnp.where(h == 1, 0, LANES - 1)
    return lax.rem(target - source + LANES, LANES)


def window_parts(h, width):
    base = pl.multiple_of(h * width, LANES)
    side = pl.multiple_of(width - LANES * h, LANES)
    source = jnp.where(h == 0, 0, LANES - 1)
    return base, side, source


def first_body(info, offsets, heading, cotangent, voxels, own, sent, line, code, head, cot, strip, sems, *, width, depth):
    h, t = (info[0], info[1])
    channels, planes, rows, _ = voxels.shape
    row = pl.multiple_of(jnp.where(t == 0, rows - SUB, 0), SUB)
    copies = [
        pltpu.make_async_copy(voxels.at[:, :, pl.ds(row, SUB), :], strip, sems.at[0]),
        pltpu.make_async_copy(offsets, code, sems.at[1]),
        pltpu.make_async_copy(heading, head, sems.at[2]),
        pltpu.make_async_copy(cotangent, cot, sems.at[3]),
    ]
    for copy in copies:
        copy.start()
    copies[0].wait()
    for c in range(channels):
        for k in range(planes):
            line[c, k : k + 1, :] = jnp.where(
                t == 0, strip[c, k, SUB - 1 : SUB, :], strip[c, k, :1, :]
            )
    for copy in copies[1:]:
        copy.wait()
    for out, at in ((own, h), (sent, 1 - h)):
        cols = pl.ds(pl.multiple_of(at * width, LANES), width)
        out[0] = code[0, :, cols].astype(F32)
        out[1] = head[0, :, cols].astype(F32)
        for c in range(channels - 1):
            out[2 + c] = cot[0, c, :, cols] * depth


def message_rows(channels, rows, count):
    body = channels * count * rows
    lines = -(-channels * count // SUB) * SUB
    return body, body + lines, body + lines + rows


def pack_body(info, first, last, line, out_a, out_b, *, width):
    h, s = (info[0], info[2])
    channels, _, rows, _ = first.shape
    planes = line.shape[1]
    count = width // LANES
    base, side, source = window_parts(h, width)
    at_line, at_edge, _ = message_rows(channels, rows, count)
    lane = iota((rows, LANES), 1)

    def fill(block, k, out):
        edge = jnp.zeros((rows, LANES), F32)
        for c in range(channels):
            for j in range(count):
                at = c * count + j
                cols = pl.ds(base + j * LANES, LANES)
                out[at * rows : (at + 1) * rows, :] = block[c, 0, :, cols]
                out[at_line + at : at_line + at + 1, :] = line[c, k : k + 1, cols]
            cols = pl.ds(side, LANES)
            turn = lax.rem(c - source + LANES, LANES)
            edge = jnp.where(lane == c, pltpu.roll(block[c, 0, :, cols], turn, 1), edge)
            turn = lax.rem(channels + c - source + LANES, LANES)
            corner = jnp.broadcast_to(line[c, k : k + 1, cols], (SUB, LANES))
            corner = pltpu.roll(corner, turn, 1)[:1]
            edge = jnp.where(lane == channels + c, corner, edge)
        out[at_edge:, :] = edge

    @pl.when(s % 2 == 0)
    def _():
        fill(last, planes - 1, out_a)
        fill(first, 0, out_b)

    @pl.when(s % 2 == 1)
    def _():
        fill(first, 0, out_a)
        fill(last, planes - 1, out_b)


def spread_message(msg, grid, plane, info, channels, rows, count):
    h, t = (info[0], info[1])
    at_line, at_edge, _ = message_rows(channels, rows, count)
    edge = msg[at_edge:, :]
    beyond = pl.ds(pl.multiple_of(jnp.where(t == 0, SUB + rows, 0), SUB), SUB)
    for c in range(channels):
        first = c * count
        tiles = [msg[(first + j) * rows : (first + j + 1) * rows, :] for j in range(count)]
        lines = [
            jnp.broadcast_to(msg[at_line + first + j : at_line + first + j + 1, :], (SUB, LANES))
            for j in range(count)
        ]
        side = pltpu.roll(edge, beside_shift(c, h), 1)
        corner = pltpu.roll(edge[:SUB], beside_shift(channels + c, h), 1)
        for e, xs in enumerate(shifts(tiles, side, h)):
            for j, x in enumerate(xs):
                grid[e, c, plane, SUB : SUB + rows, j * LANES : (j + 1) * LANES] = x
        for e, xs in enumerate(shifts(lines, corner, h)):
            for j, x in enumerate(xs):
                grid[e, c, plane, beyond, j * LANES : (j + 1) * LANES] = x


def taps(code, row0, t, rows):
    _, m, n = split_code(code)
    fy, fx = (fraction(m), fraction(n))
    row = iota(code.shape, 0) + row0
    low = (row == 0) & (t == 0)
    high = (row == rows - 1) & (t == 1)
    up = ((fy > 0.0) & jnp.logical_not(high)) | low
    ay, ax = (jnp.abs(fy), jnp.abs(fx))
    gone = (low & (fy < 0.0)) | (high & (fy > 0.0))
    by = jnp.where(gone, 0.0, ay)
    return (up, fx > 0.0, (1.0 - ay) * (1.0 - ax), (1.0 - ay) * ax, by * (1.0 - ax), by * ax)


def bilinear(rays, grid, c, plane, row0, cols):
    v = [
        [grid[e, c, plane, row0 + b + SUB - 1 : row0 + b + 2 * SUB - 1, cols] for e in range(3)]
        for b in range(3)
    ]
    out = []
    for up, right, centre, across, along, diagonal in rays:
        row = [jnp.where(up, v[2][e], v[0][e]) for e in range(3)]
        out.append(
            centre * v[1][1]
            + across * jnp.where(right, v[1][2], v[1][0])
            + along * row[1]
            + diagonal * jnp.where(right, row[2], row[0])
        )
    return out


def ray_tiles(rays, rows, width, t):
    for i in range(rows // SUB):
        for j in range(width // LANES):
            at = slice(i * SUB, (i + 1) * SUB)
            cols = slice(j * LANES, (j + 1) * LANES)
            codes = [r[0, at, cols] for r in rays]
            yield (
                i * SUB,
                at,
                cols,
                [taps(q, i * SUB, t, rows) for q in codes],
                [three(split_code(q)[0]) for q in codes],
            )


def each_tile(rows, width, body):
    count = width // LANES

    def step(n, carry):
        row = pl.ds(pl.multiple_of((n // count) * SUB, SUB), SUB)
        col = pl.ds(pl.multiple_of((n % count) * LANES, LANES), LANES)
        body(row, col)
        return carry

    lax.fori_loop(0, (rows // SUB) * count, step, 0)


def products(left):
    ones = jnp.ones_like(left[0])
    rising, falling = ([ones], [ones])
    for x in left[:-1]:
        rising.append(rising[-1] * x)
    for x in left[:0:-1]:
        falling.append(falling[-1] * x)
    return rising, falling[::-1]


def inner_body(info, vox, line, own, other, vals, part, ends, inner, grid, *, width, scale):
    h, t = (info[0], info[1])
    channels, planes, rows, _ = vox.shape
    count = width // LANES
    base, side, source = window_parts(h, width)
    turn = beside_shift(source, h)
    rays = (own, other)

    def place(k, carry):
        for c in range(channels):
            tiles = [vox[c, k, :, pl.ds(base + j * LANES, LANES)] for j in range(count)]
            beside = pltpu.roll(vox[c, k, :, pl.ds(side, LANES)], turn, 1)
            for e, xs in enumerate(shifts(tiles, beside, h)):
                for j, x in enumerate(xs):
                    grid[e, c, k, SUB : SUB + rows, j * LANES : (j + 1) * LANES] = x
        return carry

    lax.fori_loop(0, planes, place, 0)
    beyond = pl.ds(pl.multiple_of(jnp.where(t == 0, SUB + rows, 0), SUB), SUB)
    for c in range(channels):
        tiles = [line[c, :, pl.ds(base + j * LANES, LANES)] for j in range(count)]
        beside = pltpu.roll(line[c, :, pl.ds(side, LANES)], turn, 1)
        for e, xs in enumerate(shifts(tiles, beside, h)):
            for j, x in enumerate(xs):
                for k in range(planes):
                    grid[e, c, k, beyond, j * LANES : (j + 1) * LANES] = jnp.broadcast_to(
                        x[k : k + 1], (SUB, LANES)
                    )

    for row0, at, cols, yx, wz in ray_tiles(rays, rows, width, t):

        def channel(c, carry, row0=row0, at=at, cols=cols, yx=yx, wz=wz):
            old = [None, None]
            for p in range(planes):
                new = bilinear(yx, grid, c, p, row0, cols)
                for q in range(2):
                    w = wz[q]
                    if p == 0:
                        ends[q, c, 0, at, cols] = w[2] * new[q]
                    elif p == 1:
                        part[q, c, 0, at, cols] = w[1] * old[1][q] + w[2] * new[q]
                    else:
                        vals[q, c, p - 2, at, cols] = (
                            w[0] * old[0][q] + w[1] * old[1][q] + w[2] * new[q]
                        )
                    if p == planes - 1:
                        part[q, c, 1, at, cols] = w[0] * old[1][q] + w[1] * new[q]
                        ends[q, c, 1, at, cols] = w[0] * new[q]
                old = [old[1], new]
            return carry

        lax.fori_loop(0, channels, channel, 0)

    for q in range(2):

        def shade(row, col, q=q):
            ahead = rays[q][1, row, col] == 0.0
            sigma = [log_soft(vals[q, 0, k, row, col]) * scale for k in range(planes - 2)]
            left = [jnp.exp(-x) for x in sigma]
            rising, falling = products(left)
            light = [None] * (channels - 1)
            for k in range(planes - 2):
                glow = jnp.where(ahead, rising[k], falling[k]) * (1.0 - left[k])
                for c in range(channels - 1):
                    term = glow * logistic(vals[q, c + 1, k, row, col])
                    light[c] = term if k == 0 else light[c] + term
            inner[0, q, row, col] = total_of(sigma)
            for c in range(channels - 1):
                inner[c + 1, q, row, col] = light[c]

        each_tile(rows, width, shade)


def chunk_mask(s, chunk):
    bit = (iota((SUB, LANES), 1) >> (chunk.bit_length() - 1)) & 1
    mine = s & 1
    return bit == mine, jnp.where(mine == 1, LANES - chunk, chunk)


def rim_body(info, near_a, near_b, own, other, part, ends, inner, pay, rim, ends_out, keep, send, grid, *, scale, chunk):
    t, s = (info[1], info[2])
    _, channels, _, rows, width = part.shape
    count = width // LANES
    even = s % 2 == 0
    rays = (own, other)
    spread_message(near_a, grid, jnp.where(even, 1, 0), info, channels, rows, count)
    spread_message(near_b, grid, jnp.where(even, 0, 1), info, channels, rows, count)
    for row0, at, cols, yx, wz in ray_tiles(rays, rows, width, t):

        def channel(c, carry, row0=row0, at=at, cols=cols, yx=yx, wz=wz):
            for p in range(2):
                new = bilinear(yx, grid, c, p, row0, cols)
                for q in range(2):
                    rim[q, c, p, at, cols] = part[q, c, p, at, cols] + wz[q][2 * p] * new[q]
                    ends_out[q, c, p, at, cols] = ends[q, c, p, at, cols] + wz[q][1] * new[q]
            return carry

        lax.fori_loop(0, channels, channel, 0)
    kept, turn = chunk_mask(s, chunk)

    def shade(row, col):
        lights = []
        for q in range(2):
            ahead = rays[q][1, row, col] == 0.0
            sigma = [log_soft(rim[q, 0, p, row, col]) * scale for p in range(2)]
            left = [jnp.exp(-x) for x in sigma]
            middle = inner[0, q, row, col]
            through = jnp.exp(-middle)
            first = jnp.where(ahead, left[0], left[1])
            last = first * through
            pay[0, q, row, col] = sigma[0] + middle + sigma[1]
            low = jnp.where(ahead, 1.0, last) * (1.0 - left[0])
            high = jnp.where(ahead, last, 1.0) * (1.0 - left[1])
            light = [
                low * logistic(rim[q, c + 1, 0, row, col])
                + first * inner[c + 1, q, row, col]
                + high * logistic(rim[q, c + 1, 1, row, col])
                for c in range(channels - 1)
            ]
            pay[1, q, row, col] = total_of([rays[q][2 + c, row, col] * x for c, x in enumerate(light)])
            lights.append(light)
        for c, (a, b) in enumerate(zip(*lights)):
            keep[c, row, col] = jnp.where(kept, a, pltpu.roll(b, turn, 1))
            send[c, row, col] = jnp.where(kept, pltpu.roll(b, LANES - turn, 1), a)

    each_tile(rows, width, shade)


def column_body(info, own, other, vals, rim, ends, cols5, *, scale, slabs):
    s = info[2]
    _, channels, inside, rows, width = vals.shape
    planes = inside + 2
    rays = (own, other)
    live = {-1: jnp.where(s > 0, 1.0, 0.0), planes: jnp.where(s < slabs - 1, 1.0, 0.0)}
    for q in range(2):

        def shade(row, col, q=q):
            ahead = rays[q][1, row, col] == 0.0
            wz = three(split_code(rays[q][0, row, col])[0])
            pull = [rays[q][2 + c, row, col] for c in range(channels - 1)]

            def value(c, k):
                if k in live:
                    return ends[q, c, 1 if k > 0 else 0, row, col]
                if k == 0 or k == planes - 1:
                    return rim[q, c, 1 if k else 0, row, col]
                return vals[q, c, k - 1, row, col]

            ks = range(planes)
            every = range(-1, planes + 1)
            sigma = {k: log_soft(value(0, k)) * scale for k in every}
            slope = {k: logistic(value(0, k)) * scale for k in every}
            left = {k: jnp.exp(-sigma[k]) for k in every}
            rising, falling = products([left[k] for k in ks])
            through = rising[-1] * left[planes - 1]
            share, after = ({}, {})
            tint = [{} for _ in range(channels - 1)]
            for k in every:
                if k == -1:
                    reach = jnp.where(ahead, jnp.exp(sigma[k]), through)
                elif k == planes:
                    reach = jnp.where(ahead, through, jnp.exp(sigma[k]))
                else:
                    reach = jnp.where(ahead, rising[k], falling[k])
                glow = reach * (1.0 - left[k])
                if k in live:
                    glow = glow * live[k]
                    slope[k] = slope[k] * live[k]
                hue = []
                for c in range(channels - 1):
                    colour = logistic(value(c + 1, k))
                    hue.append(pull[c] * colour)
                    tint[c][k] = glow * hue[-1] * (1.0 - colour)
                hue = total_of(hue)
                share[k] = glow * hue
                after[k] = reach * left[k] * hue
            whole = total_of([share[k] for k in ks])
            run = -share[-1]
            pushed = {}
            for k in every:
                upto = run + share[k]
                pushed[k] = (after[k] + jnp.where(ahead, upto, whole - run)) * slope[k]
                run = upto
            for n, field in enumerate([pushed, slope] + tint):
                for p in ks:
                    cols5[n, q, p, row, col] = (
                        wz[1] * field[p] + wz[2] * field[p - 1] + wz[0] * field[p + 1]
                    )

        each_tile(rows, width, shade)


def ray_order(info, bit, heading):
    lower = ((info[2] >> bit) & 1) == 1
    return heading == jnp.where(lower, 0.0, 1.0)


def scan_body(info, own, other, block, theirs, *refs, bit, rounds, chunk, tile_bit):
    first = bit == 0
    last = bit == rounds - 1
    refs = list(refs)
    state = None if first else refs.pop(0)
    out_state = refs.pop(0)
    out_block = None if last else refs.pop(0)
    out_final = refs.pop(0) if bit == rounds - 2 else None
    mine_scale, their_scale = refs
    rays = (own, other)
    _, rows, width = own.shape
    kept, turn = chunk_mask(info[2], chunk)
    halved = tile_bit is not None and bit >= tile_bit
    my_tile = (info[2] >> (tile_bit or 0)) & 1

    def ray(row, col):
        scales = []
        for q in range(2):
            heading = rays[q][1, row, col]
            earlier = ray_order(info, bit, heading)
            depth = block[0, q, row, col]
            before = jnp.zeros_like(depth) if first else state[0, q, row, col]
            rest = block[1, q, row, col] if first else state[1, q, row, col]
            if last:
                their_depth = their_light = theirs[q, row, col]
            else:
                their_depth, their_light = (theirs[n, q, row, col] for n in range(2))
            fade = jnp.exp(-depth)
            their_fade = jnp.exp(-their_depth)
            later = fade if first else jnp.exp(before - depth)
            out_rest = rest + jnp.where(earlier, 0.0, later * their_light)
            out_before = before + jnp.where(earlier, their_depth, 0.0)
            if last:
                reach = jnp.exp(-out_before)
                out_state[0, q, row, col] = reach
                out_state[1, q, row, col] = reach * out_rest
            else:
                out_state[0, q, row, col] = out_before
                out_state[1, q, row, col] = out_rest
                light = block[1, q, row, col]
                out_depth = depth + their_depth
                out_light = jnp.where(
                    earlier, their_light + their_fade * light, light + fade * their_light
                )
                out_block[0, q, row, col] = out_depth
                out_block[1, q, row, col] = out_light
                if out_final is not None:
                    out_final[q, row, col] = jnp.where(
                        ray_order(info, bit + 1, heading), out_light, out_depth
                    )
            scales.append((jnp.where(earlier, their_fade, 1.0), jnp.where(earlier, 1.0, fade)))
        packed = [jnp.where(kept, a, pltpu.roll(b, turn, 1)) for a, b in zip(*scales)]
        for out, x in zip((mine_scale, their_scale), packed):
            if not halved:
                out[row, col] = x
            else:

                @pl.when(col.start == my_tile * LANES)
                def _(out=out, x=x):
                    out[row, :] = x

    each_tile(rows, width, ray)


def light_body(info, keep, got, mine_scale, their_scale, *outs, tile_bit):
    mine, theirs = (mine_scale[...], their_scale[...])
    if tile_bit is None:
        for c in range(keep.shape[0]):
            outs[0][c] = mine * keep[c] + theirs * got[c]
        return
    tile = (info[2] >> tile_bit) & 1
    for c in range(keep.shape[0]):
        both = mine * keep[c] + theirs * got[c]
        low, high = (both[:, :LANES], both[:, LANES:])
        outs[0][c] = jnp.where(tile == 0, low, high)
        outs[1][c] = jnp.where(tile == 0, high, low)


def merge_body(reach_rest, cols5, columns, *, channels):
    _, _, planes, rows, width = cols5.shape

    def ray(row, col):
        for q in range(2):
            near, far = (reach_rest[0, q, row, col], reach_rest[1, q, row, col])
            for p in range(planes):
                columns[0, q, p, row, col] = (
                    near * cols5[0, q, p, row, col] - far * cols5[1, q, p, row, col]
                )
                for c in range(1, channels):
                    columns[c, q, p, row, col] = near * cols5[c + 1, q, p, row, col]

    each_tile(rows, width, ray)


def border_body(info, columns, own, other, line, edge):
    h, t = (info[0], info[1])
    channels, _, planes, rows, width = columns.shape
    count = width // LANES
    last = LANES - 1
    rays = (own, other)
    row0 = pl.multiple_of(jnp.where(t == 0, rows - SUB, 0), SUB)
    near = pl.ds(row0, SUB)
    take = jnp.where(t == 0, SUB - 1, 0)
    lane8 = iota((SUB, LANES), 1)
    pick = iota((SUB, LANES), 0) == take
    side = pl.ds(pl.multiple_of(jnp.where(h == 0, width - LANES, 0), LANES), LANES)
    down, across = ([], [])
    for r in rays:
        _, wy, wx = [three(x) for x in split_code(r[0, near, :])]
        y = jnp.where(t == 0, wy[2], wy[0])
        down.append([y * x for x in wx])
        _, wy, wx = [three(x) for x in split_code(r[0, :, side])]
        x = jnp.where(h == 0, wx[2], wx[0])
        across.append([y * x for y in wy])
    row = iota((rows, LANES), 0)
    lane = iota((rows, LANES), 1)
    source = jnp.where(h == 0, last, 0)
    edge[...] = jnp.zeros(edge.shape, F32)

    def channel(c, carry):
        for p in range(planes):
            at = c * planes + p
            strip = [columns[c, q, p, near, :] for q in range(2)]
            sums = []
            for e in range(3):
                x = total_of([down[q][e] * strip[q] for q in range(2)])
                x = jnp.sum(jnp.where(jnp.concatenate([pick] * count, axis=1), x, 0.0), axis=0, keepdims=True)
                sums.append(jnp.broadcast_to(x, (SUB, width)))
            plus = [sums[2][:, j * LANES : (j + 1) * LANES] for j in range(count)]
            minus = [sums[0][:, j * LANES : (j + 1) * LANES] for j in range(count)]
            plus = [pltpu.roll(x, 1, 1) for x in plus]
            minus = [pltpu.roll(x, last, 1) for x in minus]
            zero = jnp.zeros_like(plus[0])
            for j in range(count):
                x = sums[1][:, j * LANES : (j + 1) * LANES]
                x = x + jnp.where(lane8 == 0, plus[j - 1] if j else zero, plus[j])
                x = x + jnp.where(lane8 == last, minus[j + 1] if j < count - 1 else zero, minus[j])
                line[c, p : p + 1, j * LANES : (j + 1) * LANES] = x[:1]
            strip = [columns[c, q, p, :, side] for q in range(2)]
            part = [total_of([across[q][b] * strip[q] for q in range(2)]) for b in range(3)]
            lower = pltpu.roll(part[2], 1, 0)
            upper = pltpu.roll(part[0], rows - 1, 0)
            main = part[1] + jnp.where(row == 0, 0.0, lower) + jnp.where(row == rows - 1, 0.0, upper)
            over = jnp.where(t == 0, lower[:SUB], pltpu.roll(upper[rows - SUB :], 1, 0))
            turn = lax.rem(at - source + LANES, LANES)
            edge[:rows, :] = jnp.where(lane == at, pltpu.roll(main, turn, 1), edge[:rows, :])
            edge[rows:, :] = jnp.where(lane8 == at, pltpu.roll(over, turn, 1), edge[rows:, :])
        return carry

    lax.fori_loop(0, channels, channel, 0)


def scatter_body(columns, own, other, grad, weights):
    channels, _, planes, rows, width = columns.shape
    lane = iota((rows, width), 1)
    row = iota((rows, width), 0)
    for q, r in enumerate((own, other)):
        _, wy, wx = [three(x) for x in split_code(r[0])]
        for b in range(3):
            for e in range(3):
                weights[q, b * 3 + e] = wy[b] * wx[e]

    def plane(p, carry):
        for c in range(channels):
            col = [columns[c, q, p] for q in range(2)]
            summed = []
            for e in range(3):
                part = [
                    weights[0, b * 3 + e] * col[0] + weights[1, b * 3 + e] * col[1]
                    for b in range(3)
                ]
                down = pltpu.roll(part[2], 1, 0)
                up = pltpu.roll(part[0], rows - 1, 0)
                summed.append(
                    part[1] + jnp.where(row == 0, 0.0, down) + jnp.where(row == rows - 1, 0.0, up)
                )
            right = pltpu.roll(summed[2], 1, 1)
            left = pltpu.roll(summed[0], width - 1, 1)
            grad[c, p] = (
                summed[1]
                + jnp.where(lane == 0, 0.0, right)
                + jnp.where(lane == width - 1, 0.0, left)
            )
        return carry

    lax.fori_loop(0, planes, plane, 0)


def finish_body(info, grad_in, line, edge, corner, grad):
    h, t = (info[0], info[1])
    _, planes, rows, width = grad.shape
    c = pl.program_id(0)
    source = jnp.where(h == 0, LANES - 1, 0)
    side = pl.ds(pl.multiple_of(jnp.where(h == 0, width - LANES, 0), LANES), LANES)
    last = jnp.where(t == 0, rows - 1, 0)
    at_row = iota((rows, width), 0) == last
    at_lane = iota((rows, LANES), 1) == source
    packed = edge[...] + jnp.where(iota((rows, LANES), 0) == last, corner[:1], 0.0)
    for p in range(planes):
        grad[0, p] = grad_in[0, p] + jnp.where(at_row, line[0, p : p + 1, :], 0.0)
        turn = lax.rem(source - (c * planes + p) + LANES, LANES)
        grad[0, p, :, side] += jnp.where(at_lane, pltpu.roll(packed, turn, 1), 0.0)


def per_device(voxels, offsets, heading, cotangent):
    channels, planes, rows, total = voxels.shape
    dirs, slabs, cores = (lax.axis_size(a) for a in ("dir", "slab", "tile"))
    if dirs != 2 or cores != 2 or slabs & (slabs - 1):
        raise ValueError("mesh")
    width = total // dirs
    depth = planes * slabs
    scale = 2.0 / depth
    h, s, t = (lax.axis_index(a) for a in ("dir", "slab", "tile"))
    info = jnp.stack([h, t, s]).astype(jnp.int32)
    swap = [(0, 1), (1, 0)]
    count = width // LANES
    grid = lambda n: pltpu.VMEM((3, channels, n, rows + 2 * SUB, width), F32)
    colours = channels - 1
    half = slabs // dirs
    chunk = total // slabs
    rounds = slabs.bit_length() - 1
    tile_bit = (LANES // chunk).bit_length() - 1
    tile_bit = tile_bit if 0 < tile_bit < rounds - 1 else None

    pairs_a = [(i, i ^ 1) for i in range(slabs)]
    pairs_b = [(i, i + 1) for i in range(1, slabs - 1, 2)]
    pairs_b = pairs_b + [(b, a) for a, b in pairs_b]

    hbm = pl.BlockSpec(memory_space=pltpu.HBM)
    ray = shape(channels + 1, rows, width)
    own, sent, line = pl.pallas_call(
        functools.partial(first_body, width=width, depth=depth),
        out_shape=[ray, ray, shape(channels, planes, total)],
        in_specs=[SMEM] + [hbm] * 4,
        out_specs=[VMEM] * 3,
        scratch_shapes=[
            pltpu.VMEM(offsets.shape, jnp.int32),
            pltpu.VMEM(heading.shape, jnp.int32),
            pltpu.VMEM(cotangent.shape, F32),
            pltpu.VMEM((channels, planes, SUB, total), F32),
            pltpu.SemaphoreType.DMA((4,)),
        ],
        compiler_params=pltpu.CompilerParams(vmem_limit_bytes=8 * MIB),
        name="first",
    )(info, offsets, heading, cotangent, voxels)
    line = lax.ppermute(line, "tile", swap)
    other = lax.ppermute(sent, "dir", swap)

    def block(k):
        return pl.BlockSpec((channels, 1, rows, total), lambda i: (0, k, 0, 0))

    near = call(
        pack_body,
        [shape(message_rows(channels, rows, count)[2], LANES)] * 2,
        (info, voxels, voxels, line),
        specs=[SMEM, block(0), block(planes - 1), VMEM],
        width=width,
    )
    near = [lax.ppermute(x, "slab", p) for x, p in zip(near, (pairs_a, pairs_b))]

    two = shape(2, channels, 2, rows, width)
    pair = shape(2, 2, rows, width)
    vals, part, ends, inner = call(
        inner_body,
        [shape(2, channels, planes - 2, rows, width), two, two, shape(channels, 2, rows, width)],
        (info, voxels, line, own, other),
        scratch=[grid(planes)],
        limit=20,
        width=width,
        scale=scale,
    )
    light = shape(colours, rows, width)
    pay, rim, ends, keep, send = call(
        rim_body,
        [pair, two, two, light, light],
        (info, *near, own, other, part, ends, inner),
        scratch=[grid(2)],
        scale=scale,
        chunk=chunk,
    )
    cols5 = call(
        column_body,
        shape(channels + 1, 2, planes, rows, width),
        (info, own, other, vals, rim, ends),
        scale=scale,
        slabs=slabs,
    )

    message, state = (pay, ())
    for bit in range(rounds):
        pairs = [(i, i ^ (1 << bit)) for i in range(slabs)]
        if bit == 1:
            message, cols5 = lax.optimization_barrier((message, cols5))
        last = bit == rounds - 1
        theirs = lax.ppermute(message, "slab", pairs)
        got = lax.ppermute(send, "slab", pairs)
        halved = tile_bit is not None and bit >= tile_bit
        factor = shape(rows, LANES if halved else width)
        outs = [pair] + ([] if last else [pair])
        outs = outs + ([shape(2, rows, width)] if bit == rounds - 2 else []) + [factor] * 2
        state, *others, mine_scale, their_scale = call(
            scan_body,
            outs,
            (info, own, other, pay, theirs) + tuple(state),
            bit=bit,
            rounds=rounds,
            chunk=chunk,
            tile_bit=tile_bit,
        )
        if not last:
            pay, message = (others[0], others[-1])
            state = (state,)
        if last:
            break
        split = tile_bit if bit + 1 == tile_bit else None
        kept = shape(colours, rows, LANES) if split is not None else shape(*keep.shape)
        pieces = call(
            light_body,
            [kept] * (1 if split is None else 2),
            (info, keep, got, mine_scale, their_scale),
            tile_bit=split,
        )
        keep, send = (pieces[0], pieces[-1])

    plain = dict(
        compiler_params=pltpu.CompilerParams(vmem_limit_bytes=16 * MIB),
        cost_estimate=pl.CostEstimate(flops=10**7, bytes_accessed=2 * 10**6, transcendentals=0),
    )
    columns = pl.pallas_call(
        functools.partial(merge_body, channels=channels),
        out_shape=shape(channels, 2, planes, rows, width),
        in_specs=[VMEM] * 2,
        out_specs=VMEM,
        name="merge",
        **plain,
    )(state, cols5)
    line, edge = call(
        border_body,
        [shape(channels, planes, width), shape(rows + SUB, LANES)],
        (info, columns, own, other),
    )
    line, got = lax.optimization_barrier((line, got))
    edge, corner = (edge[:rows], edge[rows:])
    edge = lax.ppermute(edge, "dir", swap)
    corner = lax.ppermute(corner, ("dir", "tile"), [(i, 3 - i) for i in range(4)])
    line = lax.ppermute(line, "tile", swap)
    grad = pl.pallas_call(
        scatter_body,
        out_shape=shape(channels, planes, rows, width),
        in_specs=[VMEM] * 3,
        out_specs=VMEM,
        scratch_shapes=[pltpu.VMEM((2, 9, rows, width), F32)],
        name="scatter",
        **plain,
    )(columns, own, other)
    quarter = pl.BlockSpec((1, planes, rows, width), lambda c: (c, 0, 0, 0))
    voxel_grad = pl.pallas_call(
        finish_body,
        out_shape=shape(channels, planes, rows, width),
        grid=(channels,),
        in_specs=[SMEM, quarter, pl.BlockSpec((1, planes, width), lambda c: (c, 0, 0)), VMEM, VMEM],
        out_specs=quarter,
        name="finish",
        **plain,
    )(info, grad, line, edge, corner)

    keep = call(
        light_body, shape(*keep.shape), (info, keep, got, mine_scale, their_scale), tile_bit=None
    )
    start = (s % half) * chunk
    start = lax.rem(start, LANES) if tile_bit is not None else start
    there = jnp.where(s % 2 == 1, start - chunk, start + chunk)
    mine = lax.dynamic_slice_in_dim(keep, start, chunk, axis=2)
    sent = lax.dynamic_slice_in_dim(keep, there, chunk, axis=2)
    got = lax.ppermute(sent, "dir", swap)
    image = jnp.where(s // half == h, mine, got)
    return (image[None], voxel_grad)


def solution(mesh):
    return jax.shard_map(
        per_device,
        mesh=mesh,
        in_specs=(
            P(None, "slab", "tile", None),
            P("dir", "tile", None),
            P("dir", "tile", None),
            P("dir", None, "tile", None),
        ),
        out_specs=(P("dir", None, "tile", "slab"), P(None, "slab", "tile", "dir")),
        check_vma=False,
    )
```

```python
import functools

import jax
import jax.numpy as jnp
from jax import lax
from jax.experimental import pallas as pl
from jax.experimental.pallas import tpu as pltpu
from jax.sharding import PartitionSpec as P


LEVELS = 8
BITS = LEVELS.bit_length() - 1
LANES = 128
SUB = 8
F32 = jnp.float32
VMEM = pl.BlockSpec(memory_space=pltpu.VMEM)
SMEM = pl.BlockSpec(memory_space=pltpu.SMEM)
MIB = 2**20


def call(body, outs, args, scratch=(), limit=16, flops=10**7, specs=None, **statics):
    inputs = [SMEM] + [VMEM] * (len(args) - 1)
    return pl.pallas_call(
        functools.partial(body, **statics),
        out_shape=outs,
        grid=() if specs is None else (1,),
        in_specs=specs or inputs,
        out_specs=jax.tree.map(lambda _: VMEM, outs),
        scratch_shapes=list(scratch),
        cost_estimate=pl.CostEstimate(
            flops=flops, bytes_accessed=2 * 10**6, transcendentals=0
        ),
        compiler_params=pltpu.CompilerParams(vmem_limit_bytes=limit * MIB),
    )(*args)


def shape(*dims):
    return jax.ShapeDtypeStruct(dims, F32)


def iota(dims, axis):
    return lax.broadcasted_iota(jnp.int32, dims, axis)


def fraction(raw):
    return (raw.astype(F32) + 0.5) / LEVELS - 0.5


def three(raw):
    f = fraction(raw)
    return (jnp.maximum(-f, 0.0), 1.0 - jnp.abs(f), jnp.maximum(f, 0.0))


def split_code(code):
    q = code.astype(jnp.int32)
    return (q & (LEVELS - 1), (q >> BITS) & (LEVELS - 1), q >> (2 * BITS))


def logistic(v):
    return 0.5 * jnp.tanh(0.5 * v) + 0.5


def total_of(terms):
    return functools.reduce(lambda a, b: a + b, terms)


def log_soft(v):
    return jnp.maximum(v, 0.0) + jnp.log(1.0 + jnp.exp(-jnp.abs(v)))


def shifts(tiles, beside, h):
    lane = iota(tiles[0].shape, 1)
    last = LANES - 1
    zero = jnp.zeros_like(beside)
    right = [pltpu.roll(x, 1, 1) for x in tiles]
    left = [pltpu.roll(x, last, 1) for x in tiles]
    below = [jnp.where(h == 1, beside, zero)] + right[:-1]
    above = left[1:] + [jnp.where(h == 0, beside, zero)]
    minus = [jnp.where(lane == 0, b, r) for b, r in zip(below, right)]
    plus = [jnp.where(lane == last, a, x) for a, x in zip(above, left)]
    return (minus, tiles, plus)


def beside_shift(source, h):
    target = jnp.where(h == 1, 0, LANES - 1)
    return lax.rem(target - source + LANES, LANES)


def window_parts(h, width):
    base = pl.multiple_of(h * width, LANES)
    side = pl.multiple_of(width - LANES * h, LANES)
    source = jnp.where(h == 0, 0, LANES - 1)
    return base, side, source


def first_body(info, offsets, heading, cotangent, voxels, own, sent, line, code, head, cot, strip, sems, *, width, depth):
    h, t = (info[0], info[1])
    channels, planes, rows, _ = voxels.shape
    row = pl.multiple_of(jnp.where(t == 0, rows - SUB, 0), SUB)
    copies = [
        pltpu.make_async_copy(voxels.at[:, :, pl.ds(row, SUB), :], strip, sems.at[0]),
        pltpu.make_async_copy(offsets, code, sems.at[1]),
        pltpu.make_async_copy(heading, head, sems.at[2]),
        pltpu.make_async_copy(cotangent, cot, sems.at[3]),
    ]
    for copy in copies:
        copy.start()
    copies[0].wait()
    for c in range(channels):
        for k in range(planes):
            line[c, k : k + 1, :] = jnp.where(
                t == 0, strip[c, k, SUB - 1 : SUB, :], strip[c, k, :1, :]
            )
    for copy in copies[1:]:
        copy.wait()
    for out, at in ((own, h), (sent, 1 - h)):
        cols = pl.ds(pl.multiple_of(at * width, LANES), width)
        out[0] = code[0, :, cols].astype(F32)
        out[1] = head[0, :, cols].astype(F32)
        for c in range(channels - 1):
            out[2 + c] = cot[0, c, :, cols] * depth


def message_rows(channels, rows, count):
    body = channels * count * rows
    lines = -(-channels * count // SUB) * SUB
    return body, body + lines, body + lines + rows


def pack_body(info, first, last, line, out_a, out_b, *, width):
    h, s = (info[0], info[2])
    channels, _, rows, _ = first.shape
    planes = line.shape[1]
    count = width // LANES
    base, side, source = window_parts(h, width)
    at_line, at_edge, _ = message_rows(channels, rows, count)
    lane = iota((rows, LANES), 1)

    def fill(block, k, out):
        edge = jnp.zeros((rows, LANES), F32)
        for c in range(channels):
            for j in range(count):
                at = c * count + j
                cols = pl.ds(base + j * LANES, LANES)
                out[at * rows : (at + 1) * rows, :] = block[c, 0, :, cols]
                out[at_line + at : at_line + at + 1, :] = line[c, k : k + 1, cols]
            cols = pl.ds(side, LANES)
            turn = lax.rem(c - source + LANES, LANES)
            edge = jnp.where(lane == c, pltpu.roll(block[c, 0, :, cols], turn, 1), edge)
            turn = lax.rem(channels + c - source + LANES, LANES)
            corner = jnp.broadcast_to(line[c, k : k + 1, cols], (SUB, LANES))
            corner = pltpu.roll(corner, turn, 1)[:1]
            edge = jnp.where(lane == channels + c, corner, edge)
        out[at_edge:, :] = edge

    @pl.when(s % 2 == 0)
    def _():
        fill(last, planes - 1, out_a)
        fill(first, 0, out_b)

    @pl.when(s % 2 == 1)
    def _():
        fill(first, 0, out_a)
        fill(last, planes - 1, out_b)


def spread_message(msg, grid, plane, info, channels, rows, count):
    h, t = (info[0], info[1])
    at_line, at_edge, _ = message_rows(channels, rows, count)
    edge = msg[at_edge:, :]
    beyond = pl.ds(pl.multiple_of(jnp.where(t == 0, SUB + rows, 0), SUB), SUB)
    for c in range(channels):
        first = c * count
        tiles = [msg[(first + j) * rows : (first + j + 1) * rows, :] for j in range(count)]
        lines = [
            jnp.broadcast_to(msg[at_line + first + j : at_line + first + j + 1, :], (SUB, LANES))
            for j in range(count)
        ]
        side = pltpu.roll(edge, beside_shift(c, h), 1)
        corner = pltpu.roll(edge[:SUB], beside_shift(channels + c, h), 1)
        for e, xs in enumerate(shifts(tiles, side, h)):
            for j, x in enumerate(xs):
                grid[e, c, plane, SUB : SUB + rows, j * LANES : (j + 1) * LANES] = x
        for e, xs in enumerate(shifts(lines, corner, h)):
            for j, x in enumerate(xs):
                grid[e, c, plane, beyond, j * LANES : (j + 1) * LANES] = x


def taps(code, row0, t, rows):
    _, m, n = split_code(code)
    fy, fx = (fraction(m), fraction(n))
    row = iota(code.shape, 0) + row0
    low = (row == 0) & (t == 0)
    high = (row == rows - 1) & (t == 1)
    up = ((fy > 0.0) & jnp.logical_not(high)) | low
    ay, ax = (jnp.abs(fy), jnp.abs(fx))
    gone = (low & (fy < 0.0)) | (high & (fy > 0.0))
    by = jnp.where(gone, 0.0, ay)
    return (up, fx > 0.0, (1.0 - ay) * (1.0 - ax), (1.0 - ay) * ax, by * (1.0 - ax), by * ax)


def bilinear(rays, grid, c, plane, row0, cols):
    v = [
        [grid[e, c, plane, row0 + b + SUB - 1 : row0 + b + 2 * SUB - 1, cols] for e in range(3)]
        for b in range(3)
    ]
    out = []
    for up, right, centre, across, along, diagonal in rays:
        row = [jnp.where(up, v[2][e], v[0][e]) for e in range(3)]
        out.append(
            centre * v[1][1]
            + across * jnp.where(right, v[1][2], v[1][0])
            + along * row[1]
            + diagonal * jnp.where(right, row[2], row[0])
        )
    return out


def ray_tiles(rays, rows, width, t):
    for i in range(rows // SUB):
        for j in range(width // LANES):
            at = slice(i * SUB, (i + 1) * SUB)
            cols = slice(j * LANES, (j + 1) * LANES)
            codes = [r[0, at, cols] for r in rays]
            yield (
                i * SUB,
                at,
                cols,
                [taps(q, i * SUB, t, rows) for q in codes],
                [three(split_code(q)[0]) for q in codes],
            )


def each_tile(rows, width, body, unroll=False):
    count = width // LANES
    if unroll:
        for i in range(rows // SUB):
            for j in range(count):
                body(pl.ds(i * SUB, SUB), pl.ds(j * LANES, LANES))
        return

    def step(n, carry):
        row = pl.ds(pl.multiple_of((n // count) * SUB, SUB), SUB)
        col = pl.ds(pl.multiple_of((n % count) * LANES, LANES), LANES)
        body(row, col)
        return carry

    lax.fori_loop(0, (rows // SUB) * count, step, 0)


def products(left):
    ones = jnp.ones_like(left[0])
    rising, falling = ([ones], [ones])
    for x in left[:-1]:
        rising.append(rising[-1] * x)
    for x in left[:0:-1]:
        falling.append(falling[-1] * x)
    return rising, falling[::-1]


def inner_body(info, vox, line, own, other, vals, part, ends, inner, grid, *, width, scale):
    h, t = (info[0], info[1])
    channels, planes, rows, _ = vox.shape
    count = width // LANES
    base, side, source = window_parts(h, width)
    turn = beside_shift(source, h)
    rays = (own, other)

    def place(k, carry):
        for c in range(channels):
            tiles = [vox[c, k, :, pl.ds(base + j * LANES, LANES)] for j in range(count)]
            beside = pltpu.roll(vox[c, k, :, pl.ds(side, LANES)], turn, 1)
            for e, xs in enumerate(shifts(tiles, beside, h)):
                for j, x in enumerate(xs):
                    grid[e, c, k, SUB : SUB + rows, j * LANES : (j + 1) * LANES] = x
        return carry

    lax.fori_loop(0, planes, place, 0)
    beyond = pl.ds(pl.multiple_of(jnp.where(t == 0, SUB + rows, 0), SUB), SUB)
    for c in range(channels):
        tiles = [line[c, :, pl.ds(base + j * LANES, LANES)] for j in range(count)]
        beside = pltpu.roll(line[c, :, pl.ds(side, LANES)], turn, 1)
        for e, xs in enumerate(shifts(tiles, beside, h)):
            for j, x in enumerate(xs):
                for k in range(planes):
                    grid[e, c, k, beyond, j * LANES : (j + 1) * LANES] = jnp.broadcast_to(
                        x[k : k + 1], (SUB, LANES)
                    )

    for row0, at, cols, yx, wz in ray_tiles(rays, rows, width, t):

        def channel(c, carry, row0=row0, at=at, cols=cols, yx=yx, wz=wz):
            old = [None, None]
            for p in range(planes):
                new = bilinear(yx, grid, c, p, row0, cols)
                for q in range(2):
                    w = wz[q]
                    if p == 0:
                        ends[q, c, 0, at, cols] = w[2] * new[q]
                    elif p == 1:
                        part[q, c, 0, at, cols] = w[1] * old[1][q] + w[2] * new[q]
                    else:
                        vals[q, c, p - 2, at, cols] = (
                            w[0] * old[0][q] + w[1] * old[1][q] + w[2] * new[q]
                        )
                    if p == planes - 1:
                        part[q, c, 1, at, cols] = w[0] * old[1][q] + w[1] * new[q]
                        ends[q, c, 1, at, cols] = w[0] * new[q]
                old = [old[1], new]
            return carry

        lax.fori_loop(0, channels, channel, 0)

    for q in range(2):

        def shade(row, col, q=q):
            ahead = rays[q][1, row, col] == 0.0
            sigma = [log_soft(vals[q, 0, k, row, col]) * scale for k in range(planes - 2)]
            left = [jnp.exp(-x) for x in sigma]
            rising, falling = products(left)
            light = [None] * (channels - 1)
            for k in range(planes - 2):
                glow = jnp.where(ahead, rising[k], falling[k]) * (1.0 - left[k])
                for c in range(channels - 1):
                    term = glow * logistic(vals[q, c + 1, k, row, col])
                    light[c] = term if k == 0 else light[c] + term
            inner[0, q, row, col] = total_of(sigma)
            for c in range(channels - 1):
                inner[c + 1, q, row, col] = light[c]

        each_tile(rows, width, shade)


def chunk_mask(s, chunk):
    bit = (iota((SUB, LANES), 1) >> (chunk.bit_length() - 1)) & 1
    mine = s & 1
    return bit == mine, jnp.where(mine == 1, LANES - chunk, chunk)


def rim_body(info, near_a, near_b, own, other, part, ends, inner, pay, rim, ends_out, keep, send, grid, *, scale, chunk):
    t, s = (info[1], info[2])
    _, channels, _, rows, width = part.shape
    count = width // LANES
    even = s % 2 == 0
    rays = (own, other)
    spread_message(near_a, grid, jnp.where(even, 1, 0), info, channels, rows, count)
    spread_message(near_b, grid, jnp.where(even, 0, 1), info, channels, rows, count)
    for row0, at, cols, yx, wz in ray_tiles(rays, rows, width, t):

        def channel(c, carry, row0=row0, at=at, cols=cols, yx=yx, wz=wz):
            for p in range(2):
                new = bilinear(yx, grid, c, p, row0, cols)
                for q in range(2):
                    rim[q, c, p, at, cols] = part[q, c, p, at, cols] + wz[q][2 * p] * new[q]
                    ends_out[q, c, p, at, cols] = ends[q, c, p, at, cols] + wz[q][1] * new[q]
            return carry

        lax.fori_loop(0, channels, channel, 0)
    kept, turn = chunk_mask(s, chunk)

    def shade(row, col):
        lights = []
        for q in range(2):
            ahead = rays[q][1, row, col] == 0.0
            sigma = [log_soft(rim[q, 0, p, row, col]) * scale for p in range(2)]
            left = [jnp.exp(-x) for x in sigma]
            middle = inner[0, q, row, col]
            through = jnp.exp(-middle)
            first = jnp.where(ahead, left[0], left[1])
            last = first * through
            pay[0, q, row, col] = sigma[0] + middle + sigma[1]
            low = jnp.where(ahead, 1.0, last) * (1.0 - left[0])
            high = jnp.where(ahead, last, 1.0) * (1.0 - left[1])
            light = [
                low * logistic(rim[q, c + 1, 0, row, col])
                + first * inner[c + 1, q, row, col]
                + high * logistic(rim[q, c + 1, 1, row, col])
                for c in range(channels - 1)
            ]
            pay[1, q, row, col] = total_of([rays[q][2 + c, row, col] * x for c, x in enumerate(light)])
            lights.append(light)
        for c, (a, b) in enumerate(zip(*lights)):
            keep[c, row, col] = jnp.where(kept, a, pltpu.roll(b, turn, 1))
            send[c, row, col] = jnp.where(kept, pltpu.roll(b, LANES - turn, 1), a)

    each_tile(rows, width, shade)


def column_body(info, own, other, vals, rim, ends, cols5, *, scale, slabs):
    s = info[2]
    _, channels, inside, rows, width = vals.shape
    planes = inside + 2
    rays = (own, other)
    live = {-1: jnp.where(s > 0, 1.0, 0.0), planes: jnp.where(s < slabs - 1, 1.0, 0.0)}
    for q in range(2):

        def shade(row, col, q=q):
            ahead = rays[q][1, row, col] == 0.0
            wz = three(split_code(rays[q][0, row, col])[0])
            pull = [rays[q][2 + c, row, col] for c in range(channels - 1)]

            def value(c, k):
                if k in live:
                    return ends[q, c, 1 if k > 0 else 0, row, col]
                if k == 0 or k == planes - 1:
                    return rim[q, c, 1 if k else 0, row, col]
                return vals[q, c, k - 1, row, col]

            ks = range(planes)
            every = range(-1, planes + 1)
            sigma = {k: log_soft(value(0, k)) * scale for k in every}
            slope = {k: logistic(value(0, k)) * scale for k in every}
            left = {k: jnp.exp(-sigma[k]) for k in every}
            rising, falling = products([left[k] for k in ks])
            through = rising[-1] * left[planes - 1]
            share, after = ({}, {})
            tint = [{} for _ in range(channels - 1)]
            for k in every:
                if k == -1:
                    reach = jnp.where(ahead, jnp.exp(sigma[k]), through)
                elif k == planes:
                    reach = jnp.where(ahead, through, jnp.exp(sigma[k]))
                else:
                    reach = jnp.where(ahead, rising[k], falling[k])
                glow = reach * (1.0 - left[k])
                if k in live:
                    glow = glow * live[k]
                    slope[k] = slope[k] * live[k]
                hue = []
                for c in range(channels - 1):
                    colour = logistic(value(c + 1, k))
                    hue.append(pull[c] * colour)
                    tint[c][k] = glow * hue[-1] * (1.0 - colour)
                hue = total_of(hue)
                share[k] = glow * hue
                after[k] = reach * left[k] * hue
            whole = total_of([share[k] for k in ks])
            run = -share[-1]
            pushed = {}
            for k in every:
                upto = run + share[k]
                pushed[k] = (after[k] + jnp.where(ahead, upto, whole - run)) * slope[k]
                run = upto
            for n, field in enumerate([pushed, slope] + tint):
                for p in ks:
                    cols5[n, q, p, row, col] = (
                        wz[1] * field[p] + wz[2] * field[p - 1] + wz[0] * field[p + 1]
                    )

        each_tile(rows, width, shade)


def ray_order(info, bit, heading):
    lower = ((info[2] >> bit) & 1) == 1
    return heading == jnp.where(lower, 0.0, 1.0)


def scan_body(info, own, other, block, theirs, *refs, bit, rounds, chunk, tile_bit):
    first = bit == 0
    last = bit == rounds - 1
    refs = list(refs)
    state = None if first else refs.pop(0)
    out_state = refs.pop(0)
    out_block = None if last else refs.pop(0)
    out_final = refs.pop(0) if bit == rounds - 2 else None
    mine_scale, their_scale = refs
    rays = (own, other)
    _, rows, width = own.shape
    kept, turn = chunk_mask(info[2], chunk)
    halved = tile_bit is not None and bit >= tile_bit
    my_tile = (info[2] >> (tile_bit or 0)) & 1

    def ray(row, col):
        scales = []
        for q in range(2):
            heading = rays[q][1, row, col]
            earlier = ray_order(info, bit, heading)
            depth = block[0, q, row, col]
            before = jnp.zeros_like(depth) if first else state[0, q, row, col]
            rest = block[1, q, row, col] if first else state[1, q, row, col]
            if last:
                their_depth = their_light = theirs[q, row, col]
            else:
                their_depth, their_light = (theirs[n, q, row, col] for n in range(2))
            fade = jnp.exp(-depth)
            their_fade = jnp.exp(-their_depth)
            later = fade if first else jnp.exp(before - depth)
            out_rest = rest + jnp.where(earlier, 0.0, later * their_light)
            out_before = before + jnp.where(earlier, their_depth, 0.0)
            if last:
                reach = jnp.exp(-out_before)
                out_state[0, q, row, col] = reach
                out_state[1, q, row, col] = reach * out_rest
            else:
                out_state[0, q, row, col] = out_before
                out_state[1, q, row, col] = out_rest
                light = block[1, q, row, col]
                out_depth = depth + their_depth
                out_light = jnp.where(
                    earlier, their_light + their_fade * light, light + fade * their_light
                )
                out_block[0, q, row, col] = out_depth
                out_block[1, q, row, col] = out_light
                if out_final is not None:
                    out_final[q, row, col] = jnp.where(
                        ray_order(info, bit + 1, heading), out_light, out_depth
                    )
            scales.append((jnp.where(earlier, their_fade, 1.0), jnp.where(earlier, 1.0, fade)))
        packed = [jnp.where(kept, a, pltpu.roll(b, turn, 1)) for a, b in zip(*scales)]
        for out, x in zip((mine_scale, their_scale), packed):
            if not halved:
                out[row, col] = x
            else:

                @pl.when(col.start == my_tile * LANES)
                def _(out=out, x=x):
                    out[row, :] = x

    each_tile(rows, width, ray, unroll=True)


def light_body(info, keep, got, mine_scale, their_scale, *outs, tile_bit):
    mine, theirs = (mine_scale[...], their_scale[...])
    if tile_bit is None:
        for c in range(keep.shape[0]):
            outs[0][c] = mine * keep[c] + theirs * got[c]
        return
    tile = (info[2] >> tile_bit) & 1
    for c in range(keep.shape[0]):
        both = mine * keep[c] + theirs * got[c]
        low, high = (both[:, :LANES], both[:, LANES:])
        outs[0][c] = jnp.where(tile == 0, low, high)
        outs[1][c] = jnp.where(tile == 0, high, low)


def image_body(info, keep, got, mine_scale, their_scale, mine, sent, *, chunk, half, halved):
    s = info[2]
    start = lax.rem(s, half) * chunk
    base = 0 if halved else (start // LANES) * LANES
    cols = pl.ds(pl.multiple_of(base, LANES), LANES)
    start = lax.rem(start, LANES)
    there = jnp.where(lax.rem(s, 2) == 1, start - chunk, start + chunk)
    for c in range(keep.shape[0]):
        both = mine_scale[:, cols] * keep[c, :, cols] + their_scale[:, cols] * got[c, :, cols]
        mine[c] = pltpu.roll(both, lax.rem(LANES - start, LANES), 1)[:, :chunk]
        sent[c] = pltpu.roll(both, lax.rem(LANES - there, LANES), 1)[:, :chunk]


def choose_body(info, mine, got, image, *, half):
    image[0] = jnp.where(info[2] // half == info[0], mine[...], got[...])


def merge_body(info, reach_rest, cols5, own, other, columns, line, edge, corner, strips):
    h, t = (info[0], info[1])
    channels, _, planes, rows, width = columns.shape
    last = LANES - 1
    rays = (own, other)

    def ray(row, col):
        for q in range(2):
            near, far = (reach_rest[0, q, row, col], reach_rest[1, q, row, col])
            for p in range(planes):
                columns[0, q, p, row, col] = (
                    near * cols5[0, q, p, row, col] - far * cols5[1, q, p, row, col]
                )
                for c in range(1, channels):
                    columns[c, q, p, row, col] = near * cols5[c + 1, q, p, row, col]

    each_tile(rows, width, ray)

    down = []
    for r in rays:
        code = jnp.where(t == 0, r[0, rows - 1 : rows, :], r[0, :1, :])
        _, wy, wx = [three(x) for x in split_code(jnp.broadcast_to(code, (planes, width)))]
        y = jnp.where(t == 0, wy[2], wy[0])
        down.append([y * x for x in wx])
    lane = iota((planes, width), 1)
    for c in range(channels):
        for q in range(2):
            for p in range(planes):
                strips[q, p : p + 1, :] = jnp.where(
                    t == 0, columns[c, q, p, rows - 1 : rows, :], columns[c, q, p, :1, :]
                )
        minus, same, plus = [
            down[0][e] * strips[0] + down[1][e] * strips[1] for e in range(3)
        ]
        plus = jnp.where(lane == 0, 0.0, pltpu.roll(plus, 1, 1))
        minus = jnp.where(lane == width - 1, 0.0, pltpu.roll(minus, width - 1, 1))
        line[c] = same + plus + minus

    side = pl.ds(pl.multiple_of(jnp.where(h == 0, width - LANES, 0), LANES), LANES)
    source = jnp.where(h == 0, last, 0)
    lane = iota((rows, LANES), 1)
    row = iota((rows, LANES), 0)
    packed, across = ([], [])
    for q, r in enumerate(rays):
        code = pltpu.roll(r[0, :, side], lax.rem(LANES - source, LANES), 1)
        code = jnp.broadcast_to(code[:, :1], (rows, LANES))
        _, wy, wx = [three(x) for x in split_code(code)]
        x = jnp.where(h == 0, wx[2], wx[0])
        across.append([y * x for y in wy])
        both = jnp.zeros((rows, LANES), F32)
        for c in range(channels):
            for p in range(planes):
                at = c * planes + p
                turn = lax.rem(at - source + LANES, LANES)
                both = jnp.where(lane == at, pltpu.roll(columns[c, q, p, :, side], turn, 1), both)
        packed.append(both)
    part = [across[0][b] * packed[0] + across[1][b] * packed[1] for b in range(3)]
    lower = pltpu.roll(part[2], 1, 0)
    upper = pltpu.roll(part[0], rows - 1, 0)
    edge[...] = (
        part[1] + jnp.where(row == 0, 0.0, lower) + jnp.where(row == rows - 1, 0.0, upper)
    )
    corner[...] = jnp.where(t == 0, lower[:SUB], pltpu.roll(upper[rows - SUB :], 1, 0))


def scatter_body(columns, own, other, grad, weights):
    channels, _, planes, rows, width = columns.shape
    lane = iota((rows, width), 1)
    row = iota((rows, width), 0)
    for q, r in enumerate((own, other)):
        _, wy, wx = [three(x) for x in split_code(r[0])]
        for b in range(3):
            for e in range(3):
                weights[q, b * 3 + e] = wy[b] * wx[e]

    def plane(p, carry):
        for c in range(channels):
            col = [columns[c, q, p] for q in range(2)]
            summed = []
            for e in range(3):
                part = [
                    weights[0, b * 3 + e] * col[0] + weights[1, b * 3 + e] * col[1]
                    for b in range(3)
                ]
                down = pltpu.roll(part[2], 1, 0)
                up = pltpu.roll(part[0], rows - 1, 0)
                summed.append(
                    part[1] + jnp.where(row == 0, 0.0, down) + jnp.where(row == rows - 1, 0.0, up)
                )
            right = pltpu.roll(summed[2], 1, 1)
            left = pltpu.roll(summed[0], width - 1, 1)
            grad[c, p] = (
                summed[1]
                + jnp.where(lane == 0, 0.0, right)
                + jnp.where(lane == width - 1, 0.0, left)
            )
        return carry

    lax.fori_loop(0, planes, plane, 0)


def finish_body(info, grad_in, line, edge, corner, grad, buffer, sems):
    h, t = (info[0], info[1])
    channels, planes, rows, width = buffer.shape
    source = jnp.where(h == 0, LANES - 1, 0)
    side = pl.ds(pl.multiple_of(jnp.where(h == 0, width - LANES, 0), LANES), LANES)
    last = jnp.where(t == 0, rows - 1, 0)
    at_row = iota((rows, width), 0) == last
    at_lane = iota((rows, LANES), 1) == source
    packed = edge[...] + jnp.where(iota((rows, LANES), 0) == last, corner[:1], 0.0)
    copies = []
    for c in range(channels):
        for p in range(planes):
            buffer[c, p] = grad_in[c, p] + jnp.where(at_row, line[c, p : p + 1, :], 0.0)
            turn = lax.rem(source - (c * planes + p) + LANES, LANES)
            buffer[c, p, :, side] += jnp.where(at_lane, pltpu.roll(packed, turn, 1), 0.0)
        copies.append(pltpu.make_async_copy(buffer.at[c], grad.at[c], sems.at[c]))
        copies[-1].start()
    for copy in copies:
        copy.wait()


def per_device(voxels, offsets, heading, cotangent):
    channels, planes, rows, total = voxels.shape
    dirs, slabs, cores = (lax.axis_size(a) for a in ("dir", "slab", "tile"))
    if dirs != 2 or cores != 2 or slabs & (slabs - 1) or 2 * total > slabs * LANES:
        raise ValueError("mesh")
    width = total // dirs
    depth = planes * slabs
    scale = 2.0 / depth
    h, s, t = (lax.axis_index(a) for a in ("dir", "slab", "tile"))
    info = jnp.stack([h, t, s]).astype(jnp.int32)
    swap = [(0, 1), (1, 0)]
    count = width // LANES
    grid = lambda n: pltpu.VMEM((3, channels, n, rows + 2 * SUB, width), F32)
    colours = channels - 1
    half = slabs // dirs
    chunk = total // slabs
    rounds = slabs.bit_length() - 1
    tile_bit = (LANES // chunk).bit_length() - 1
    tile_bit = tile_bit if 0 < tile_bit < rounds - 1 else None

    pairs_a = [(i, i ^ 1) for i in range(slabs)]
    pairs_b = [(i, i + 1) for i in range(1, slabs - 1, 2)]
    pairs_b = pairs_b + [(b, a) for a, b in pairs_b]

    hbm = pl.BlockSpec(memory_space=pltpu.HBM)
    ray = shape(channels + 1, rows, width)
    own, sent, line = pl.pallas_call(
        functools.partial(first_body, width=width, depth=depth),
        out_shape=[ray, ray, shape(channels, planes, total)],
        in_specs=[SMEM] + [hbm] * 4,
        out_specs=[VMEM] * 3,
        scratch_shapes=[
            pltpu.VMEM(offsets.shape, jnp.int32),
            pltpu.VMEM(heading.shape, jnp.int32),
            pltpu.VMEM(cotangent.shape, F32),
            pltpu.VMEM((channels, planes, SUB, total), F32),
            pltpu.SemaphoreType.DMA((4,)),
        ],
        compiler_params=pltpu.CompilerParams(vmem_limit_bytes=62 * MIB),
        name="first",
    )(info, offsets, heading, cotangent, voxels)
    line = lax.ppermute(line, "tile", swap)
    other = lax.ppermute(sent, "dir", swap)

    def block(k):
        return pl.BlockSpec((channels, 1, rows, total), lambda i: (0, k, 0, 0))

    near = call(
        pack_body,
        [shape(message_rows(channels, rows, count)[2], LANES)] * 2,
        (info, voxels, voxels, line),
        specs=[SMEM, block(0), block(planes - 1), VMEM],
        width=width,
    )
    near = [lax.ppermute(x, "slab", p) for x, p in zip(near, (pairs_a, pairs_b))]

    two = shape(2, channels, 2, rows, width)
    pair = shape(2, 2, rows, width)
    vals, part, ends, inner = call(
        inner_body,
        [shape(2, channels, planes - 2, rows, width), two, two, shape(channels, 2, rows, width)],
        (info, voxels, line, own, other),
        scratch=[grid(planes)],
        limit=20,
        width=width,
        scale=scale,
    )
    light = shape(colours, rows, width)
    pay, rim, ends, keep, send = call(
        rim_body,
        [pair, two, two, light, light],
        (info, *near, own, other, part, ends, inner),
        scratch=[grid(2)],
        scale=scale,
        chunk=chunk,
    )
    cols5 = call(
        column_body,
        shape(channels + 1, 2, planes, rows, width),
        (info, own, other, vals, rim, ends),
        scale=scale,
        slabs=slabs,
    )

    message, state = (pay, ())
    for bit in range(rounds):
        pairs = [(i, i ^ (1 << bit)) for i in range(slabs)]
        last = bit == rounds - 1
        theirs = lax.ppermute(message, "slab", pairs)
        got = lax.ppermute(send, "slab", pairs)
        halved = tile_bit is not None and bit >= tile_bit
        factor = shape(rows, LANES if halved else width)
        outs = [pair] + ([] if last else [pair])
        outs = outs + ([shape(2, rows, width)] if bit == rounds - 2 else []) + [factor] * 2
        state, *others, mine_scale, their_scale = call(
            scan_body,
            outs,
            (info, own, other, pay, theirs) + tuple(state),
            bit=bit,
            rounds=rounds,
            chunk=chunk,
            tile_bit=tile_bit,
        )
        if not last:
            pay, message = (others[0], others[-1])
            state = (state,)
        if last:
            break
        split = tile_bit if bit + 1 == tile_bit else None
        kept = shape(colours, rows, LANES) if split is not None else shape(*keep.shape)
        pieces = call(
            light_body,
            [kept] * (1 if split is None else 2),
            (info, keep, got, mine_scale, their_scale),
            tile_bit=split,
        )
        keep, send = (pieces[0], pieces[-1])

    plain = dict(
        compiler_params=pltpu.CompilerParams(vmem_limit_bytes=16 * MIB),
        cost_estimate=pl.CostEstimate(flops=10**7, bytes_accessed=2 * 10**6, transcendentals=0),
    )
    columns, line, edge, corner = call(
        merge_body,
        [
            shape(channels, 2, planes, rows, width),
            shape(channels, planes, width),
            shape(rows, LANES),
            shape(SUB, LANES),
        ],
        (info, state, cols5, own, other),
        scratch=[pltpu.VMEM((2, planes, width), F32)],
    )
    edge = lax.ppermute(edge, "dir", swap)
    corner = lax.ppermute(corner, ("dir", "tile"), [(i, 3 - i) for i in range(4)])
    line = lax.ppermute(line, "tile", swap)
    grad = pl.pallas_call(
        scatter_body,
        out_shape=shape(channels, planes, rows, width),
        in_specs=[VMEM] * 3,
        out_specs=VMEM,
        scratch_shapes=[pltpu.VMEM((2, 9, rows, width), F32)],
        name="scatter",
        **plain,
    )(columns, own, other)
    grad_shape = (channels, planes, rows, width)
    voxel_grad = pl.pallas_call(
        finish_body,
        out_shape=shape(*grad_shape),
        in_specs=[SMEM] + [VMEM] * 4,
        out_specs=hbm,
        scratch_shapes=[pltpu.VMEM(grad_shape, F32), pltpu.SemaphoreType.DMA((channels,))],
        name="finish",
        **plain,
    )(info, grad, line, edge, corner)

    piece = shape(colours, rows, chunk)
    mine, sent = call(
        image_body,
        [piece, piece],
        (info, keep, got, mine_scale, their_scale),
        chunk=chunk,
        half=half,
        halved=tile_bit is not None,
    )
    got = lax.ppermute(sent, "dir", swap)
    image = call(choose_body, shape(1, colours, rows, chunk), (info, mine, got), half=half)
    return (image, voxel_grad)


def solution(mesh):
    return jax.shard_map(
        per_device,
        mesh=mesh,
        in_specs=(
            P(None, "slab", "tile", None),
            P("dir", "tile", None),
            P("dir", "tile", None),
            P("dir", None, "tile", None),
        ),
        out_specs=(P("dir", None, "tile", "slab"), P(None, "slab", "tile", "dir")),
        check_vma=False,
    )
```

```python
import functools

import jax
import jax.numpy as jnp
from jax import lax
from jax.experimental import pallas as pl
from jax.experimental.pallas import tpu as pltpu
from jax.sharding import PartitionSpec as P


LEVELS = 8
BITS = LEVELS.bit_length() - 1
LANES = 128
SUB = 8
F32 = jnp.float32
VMEM = pl.BlockSpec(memory_space=pltpu.VMEM)
MIB = 2**20


def call(body, outs, args, scratch=(), limit=16, specs=None, out_specs=None, **statics):
    def kernel(*refs):
        body(tuple(lax.axis_index(a) for a in ("dir", "tile", "slab")), *refs, **statics)

    grid = {} if specs is None else dict(grid=(1,))
    return pl.pallas_call(
        kernel,
        out_shape=outs,
        in_specs=specs or [VMEM] * len(args),
        out_specs=out_specs or jax.tree.map(lambda _: VMEM, outs),
        scratch_shapes=list(scratch),
        cost_estimate=pl.CostEstimate(flops=10**7, bytes_accessed=2 * 10**6, transcendentals=0),
        compiler_params=pltpu.CompilerParams(vmem_limit_bytes=limit * MIB),
        **grid,
    )(*args)


def shape(*dims):
    return jax.ShapeDtypeStruct(dims, F32)


def iota(dims, axis):
    return lax.broadcasted_iota(jnp.int32, dims, axis)


def fraction(raw):
    return (raw.astype(F32) + 0.5) / LEVELS - 0.5


def three(raw):
    f = fraction(raw)
    return (jnp.maximum(-f, 0.0), 1.0 - jnp.abs(f), jnp.maximum(f, 0.0))


def split_code(code):
    q = code.astype(jnp.int32)
    return (q & (LEVELS - 1), (q >> BITS) & (LEVELS - 1), q >> (2 * BITS))


def logistic(v):
    return 0.5 * jnp.tanh(0.5 * v) + 0.5


def total_of(terms):
    return functools.reduce(lambda a, b: a + b, terms)


def log_soft(v):
    return jnp.maximum(v, 0.0) + jnp.log(1.0 + jnp.exp(-jnp.abs(v)))


def shifts(tiles, beside, h):
    lane = iota(tiles[0].shape, 1)
    last = LANES - 1
    zero = jnp.zeros_like(beside)
    right = [pltpu.roll(x, 1, 1) for x in tiles]
    left = [pltpu.roll(x, last, 1) for x in tiles]
    below = [jnp.where(h == 1, beside, zero)] + right[:-1]
    above = left[1:] + [jnp.where(h == 0, beside, zero)]
    minus = [jnp.where(lane == 0, b, r) for b, r in zip(below, right)]
    plus = [jnp.where(lane == last, a, x) for a, x in zip(above, left)]
    return (minus, tiles, plus)


def beside_shift(source, h):
    target = jnp.where(h == 1, 0, LANES - 1)
    return lax.rem(target - source + LANES, LANES)


def window_parts(h, width):
    base = pl.multiple_of(h * width, LANES)
    side = pl.multiple_of(width - LANES * h, LANES)
    source = jnp.where(h == 0, 0, LANES - 1)
    return base, side, source


def first_body(info, offsets, heading, cotangent, voxels, own, sent, line, code, head, cot, strip, sems, *, width, depth):
    h, t = (info[0], info[1])
    channels, planes, rows, _ = voxels.shape
    row = pl.multiple_of(jnp.where(t == 0, rows - SUB, 0), SUB)
    copies = [
        pltpu.make_async_copy(voxels.at[:, :, pl.ds(row, SUB), :], strip, sems.at[0]),
        pltpu.make_async_copy(offsets, code, sems.at[1]),
        pltpu.make_async_copy(heading, head, sems.at[2]),
        pltpu.make_async_copy(cotangent, cot, sems.at[3]),
    ]
    for copy in copies:
        copy.start()
    copies[0].wait()
    for c in range(channels):
        for k in range(planes):
            line[c, k : k + 1, :] = jnp.where(
                t == 0, strip[c, k, SUB - 1 : SUB, :], strip[c, k, :1, :]
            )
    for copy in copies[1:]:
        copy.wait()
    for out, at in ((own, h), (sent, 1 - h)):
        cols = pl.ds(pl.multiple_of(at * width, LANES), width)
        out[0] = code[0, :, cols].astype(F32)
        out[1] = head[0, :, cols].astype(F32)
        for c in range(channels - 1):
            out[2 + c] = cot[0, c, :, cols] * depth


def message_rows(channels, rows, count):
    body = channels * count * rows
    lines = -(-channels * count // SUB) * SUB
    return body, body + lines, body + lines + rows


def pack_body(info, first, last, line, out_a, out_b, *, width):
    h, s = (info[0], info[2])
    channels, _, rows, _ = first.shape
    planes = line.shape[1]
    count = width // LANES
    base, side, source = window_parts(h, width)
    at_line, at_edge, _ = message_rows(channels, rows, count)
    lane = iota((rows, LANES), 1)

    def fill(block, k, out):
        edge = jnp.zeros((rows, LANES), F32)
        for c in range(channels):
            for j in range(count):
                at = c * count + j
                cols = pl.ds(base + j * LANES, LANES)
                out[at * rows : (at + 1) * rows, :] = block[c, 0, :, cols]
                out[at_line + at : at_line + at + 1, :] = line[c, k : k + 1, cols]
            cols = pl.ds(side, LANES)
            turn = lax.rem(c - source + LANES, LANES)
            edge = jnp.where(lane == c, pltpu.roll(block[c, 0, :, cols], turn, 1), edge)
            turn = lax.rem(channels + c - source + LANES, LANES)
            corner = jnp.broadcast_to(line[c, k : k + 1, cols], (SUB, LANES))
            corner = pltpu.roll(corner, turn, 1)[:1]
            edge = jnp.where(lane == channels + c, corner, edge)
        out[at_edge:, :] = edge

    @pl.when(s % 2 == 0)
    def _():
        fill(last, planes - 1, out_a)
        fill(first, 0, out_b)

    @pl.when(s % 2 == 1)
    def _():
        fill(first, 0, out_a)
        fill(last, planes - 1, out_b)


def spread_message(msg, grid, plane, info, channels, rows, count):
    h, t = (info[0], info[1])
    at_line, at_edge, _ = message_rows(channels, rows, count)
    edge = msg[at_edge:, :]
    beyond = pl.ds(pl.multiple_of(jnp.where(t == 0, SUB + rows, 0), SUB), SUB)
    for c in range(channels):
        first = c * count
        tiles = [msg[(first + j) * rows : (first + j + 1) * rows, :] for j in range(count)]
        lines = [
            jnp.broadcast_to(msg[at_line + first + j : at_line + first + j + 1, :], (SUB, LANES))
            for j in range(count)
        ]
        side = pltpu.roll(edge, beside_shift(c, h), 1)
        corner = pltpu.roll(edge[:SUB], beside_shift(channels + c, h), 1)
        for e, xs in enumerate(shifts(tiles, side, h)):
            for j, x in enumerate(xs):
                grid[e, c, plane, SUB : SUB + rows, j * LANES : (j + 1) * LANES] = x
        for e, xs in enumerate(shifts(lines, corner, h)):
            for j, x in enumerate(xs):
                grid[e, c, plane, beyond, j * LANES : (j + 1) * LANES] = x


def taps(code, row0, t, rows):
    _, m, n = split_code(code)
    fy, fx = (fraction(m), fraction(n))
    row = iota(code.shape, 0) + row0
    low = (row == 0) & (t == 0)
    high = (row == rows - 1) & (t == 1)
    up = ((fy > 0.0) & jnp.logical_not(high)) | low
    ay, ax = (jnp.abs(fy), jnp.abs(fx))
    gone = (low & (fy < 0.0)) | (high & (fy > 0.0))
    by = jnp.where(gone, 0.0, ay)
    return (up, fx > 0.0, (1.0 - ay) * (1.0 - ax), (1.0 - ay) * ax, by * (1.0 - ax), by * ax)


def bilinear(rays, grid, c, plane, row0, cols):
    v = [
        [grid[e, c, plane, row0 + b + SUB - 1 : row0 + b + 2 * SUB - 1, cols] for e in range(3)]
        for b in range(3)
    ]
    out = []
    for up, right, centre, across, along, diagonal in rays:
        row = [jnp.where(up, v[2][e], v[0][e]) for e in range(3)]
        out.append(
            centre * v[1][1]
            + across * jnp.where(right, v[1][2], v[1][0])
            + along * row[1]
            + diagonal * jnp.where(right, row[2], row[0])
        )
    return out


def ray_tiles(rays, rows, width, t):
    for i in range(rows // SUB):
        for j in range(width // LANES):
            at = slice(i * SUB, (i + 1) * SUB)
            cols = slice(j * LANES, (j + 1) * LANES)
            codes = [r[0, at, cols] for r in rays]
            yield (
                i * SUB,
                at,
                cols,
                [taps(q, i * SUB, t, rows) for q in codes],
                [three(split_code(q)[0]) for q in codes],
            )


def each_tile(rows, width, body):
    count = width // LANES

    def step(n, carry):
        row = pl.ds(pl.multiple_of((n // count) * SUB, SUB), SUB)
        col = pl.ds(pl.multiple_of((n % count) * LANES, LANES), LANES)
        body(row, col)
        return carry

    lax.fori_loop(0, (rows // SUB) * count, step, 0)


def products(left):
    ones = jnp.ones_like(left[0])
    rising, falling = ([ones], [ones])
    for x in left[:-1]:
        rising.append(rising[-1] * x)
    for x in left[:0:-1]:
        falling.append(falling[-1] * x)
    return rising, falling[::-1]


def inner_body(info, vox, line, own, other, vals, part, ends, inner, grid, *, width, scale):
    h, t = (info[0], info[1])
    channels, planes, rows, _ = vox.shape
    count = width // LANES
    base, side, source = window_parts(h, width)
    turn = beside_shift(source, h)
    rays = (own, other)

    def place(k, carry):
        for c in range(channels):
            tiles = [vox[c, k, :, pl.ds(base + j * LANES, LANES)] for j in range(count)]
            beside = pltpu.roll(vox[c, k, :, pl.ds(side, LANES)], turn, 1)
            for e, xs in enumerate(shifts(tiles, beside, h)):
                for j, x in enumerate(xs):
                    grid[e, c, k, SUB : SUB + rows, j * LANES : (j + 1) * LANES] = x
        return carry

    lax.fori_loop(0, planes, place, 0)
    beyond = pl.ds(pl.multiple_of(jnp.where(t == 0, SUB + rows, 0), SUB), SUB)
    for c in range(channels):
        tiles = [line[c, :, pl.ds(base + j * LANES, LANES)] for j in range(count)]
        beside = pltpu.roll(line[c, :, pl.ds(side, LANES)], turn, 1)
        for e, xs in enumerate(shifts(tiles, beside, h)):
            for j, x in enumerate(xs):
                for k in range(planes):
                    grid[e, c, k, beyond, j * LANES : (j + 1) * LANES] = jnp.broadcast_to(
                        x[k : k + 1], (SUB, LANES)
                    )

    for row0, at, cols, yx, wz in ray_tiles(rays, rows, width, t):

        def channel(c, carry, row0=row0, at=at, cols=cols, yx=yx, wz=wz):
            old = [None, None]
            for p in range(planes):
                new = bilinear(yx, grid, c, p, row0, cols)
                for q in range(2):
                    w = wz[q]
                    if p == 0:
                        ends[q, c, 0, at, cols] = w[2] * new[q]
                    elif p == 1:
                        part[q, c, 0, at, cols] = w[1] * old[1][q] + w[2] * new[q]
                    else:
                        vals[q, c, p - 2, at, cols] = (
                            w[0] * old[0][q] + w[1] * old[1][q] + w[2] * new[q]
                        )
                    if p == planes - 1:
                        part[q, c, 1, at, cols] = w[0] * old[1][q] + w[1] * new[q]
                        ends[q, c, 1, at, cols] = w[0] * new[q]
                old = [old[1], new]
            return carry

        lax.fori_loop(0, channels, channel, 0)

    for q in range(2):

        def shade(row, col, q=q):
            ahead = rays[q][1, row, col] == 0.0
            sigma = [log_soft(vals[q, 0, k, row, col]) * scale for k in range(planes - 2)]
            left = [jnp.exp(-x) for x in sigma]
            rising, falling = products(left)
            light = [None] * (channels - 1)
            for k in range(planes - 2):
                glow = jnp.where(ahead, rising[k], falling[k]) * (1.0 - left[k])
                for c in range(channels - 1):
                    term = glow * logistic(vals[q, c + 1, k, row, col])
                    light[c] = term if k == 0 else light[c] + term
            inner[0, q, row, col] = total_of(sigma)
            for c in range(channels - 1):
                inner[c + 1, q, row, col] = light[c]

        each_tile(rows, width, shade)


def chunk_mask(s, chunk):
    bit = (iota((SUB, LANES), 1) >> (chunk.bit_length() - 1)) & 1
    mine = s & 1
    return bit == mine, jnp.where(mine == 1, LANES - chunk, chunk)


def rim_body(info, near_a, near_b, own, other, part, ends, inner, pay, rim, ends_out, keep, send, grid, *, scale, chunk):
    t, s = (info[1], info[2])
    _, channels, _, rows, width = part.shape
    count = width // LANES
    even = s % 2 == 0
    rays = (own, other)
    spread_message(near_a, grid, jnp.where(even, 1, 0), info, channels, rows, count)
    spread_message(near_b, grid, jnp.where(even, 0, 1), info, channels, rows, count)
    for row0, at, cols, yx, wz in ray_tiles(rays, rows, width, t):

        def channel(c, carry, row0=row0, at=at, cols=cols, yx=yx, wz=wz):
            for p in range(2):
                new = bilinear(yx, grid, c, p, row0, cols)
                for q in range(2):
                    rim[q, c, p, at, cols] = part[q, c, p, at, cols] + wz[q][2 * p] * new[q]
                    ends_out[q, c, p, at, cols] = ends[q, c, p, at, cols] + wz[q][1] * new[q]
            return carry

        lax.fori_loop(0, channels, channel, 0)
    kept, turn = chunk_mask(s, chunk)

    def shade(row, col):
        lights = []
        for q in range(2):
            ahead = rays[q][1, row, col] == 0.0
            sigma = [log_soft(rim[q, 0, p, row, col]) * scale for p in range(2)]
            left = [jnp.exp(-x) for x in sigma]
            middle = inner[0, q, row, col]
            through = jnp.exp(-middle)
            first = jnp.where(ahead, left[0], left[1])
            last = first * through
            pay[0, q, row, col] = sigma[0] + middle + sigma[1]
            low = jnp.where(ahead, 1.0, last) * (1.0 - left[0])
            high = jnp.where(ahead, last, 1.0) * (1.0 - left[1])
            light = [
                low * logistic(rim[q, c + 1, 0, row, col])
                + first * inner[c + 1, q, row, col]
                + high * logistic(rim[q, c + 1, 1, row, col])
                for c in range(channels - 1)
            ]
            pay[1, q, row, col] = total_of([rays[q][2 + c, row, col] * x for c, x in enumerate(light)])
            lights.append(light)
        for c, (a, b) in enumerate(zip(*lights)):
            keep[c, row, col] = jnp.where(kept, a, pltpu.roll(b, turn, 1))
            send[c, row, col] = jnp.where(kept, pltpu.roll(b, LANES - turn, 1), a)

    each_tile(rows, width, shade)


def column_body(info, own, other, vals, rim, ends, cols5, *, scale, slabs):
    s = info[2]
    _, channels, inside, rows, width = vals.shape
    planes = inside + 2
    rays = (own, other)
    live = {-1: jnp.where(s > 0, 1.0, 0.0), planes: jnp.where(s < slabs - 1, 1.0, 0.0)}
    for q in range(2):

        def shade(row, col, q=q):
            ahead = rays[q][1, row, col] == 0.0
            wz = three(split_code(rays[q][0, row, col])[0])
            pull = [rays[q][2 + c, row, col] for c in range(channels - 1)]

            def value(c, k):
                if k in live:
                    return ends[q, c, 1 if k > 0 else 0, row, col]
                if k == 0 or k == planes - 1:
                    return rim[q, c, 1 if k else 0, row, col]
                return vals[q, c, k - 1, row, col]

            ks = range(planes)
            every = range(-1, planes + 1)
            sigma = {k: log_soft(value(0, k)) * scale for k in every}
            slope = {k: logistic(value(0, k)) * scale for k in every}
            left = {k: jnp.exp(-sigma[k]) for k in every}
            rising, falling = products([left[k] for k in ks])
            through = rising[-1] * left[planes - 1]
            share, after = ({}, {})
            tint = [{} for _ in range(channels - 1)]
            for k in every:
                if k == -1:
                    reach = jnp.where(ahead, jnp.exp(sigma[k]), through)
                elif k == planes:
                    reach = jnp.where(ahead, through, jnp.exp(sigma[k]))
                else:
                    reach = jnp.where(ahead, rising[k], falling[k])
                glow = reach * (1.0 - left[k])
                if k in live:
                    glow = glow * live[k]
                    slope[k] = slope[k] * live[k]
                hue = []
                for c in range(channels - 1):
                    colour = logistic(value(c + 1, k))
                    hue.append(pull[c] * colour)
                    tint[c][k] = glow * hue[-1] * (1.0 - colour)
                hue = total_of(hue)
                share[k] = glow * hue
                after[k] = reach * left[k] * hue
            whole = total_of([share[k] for k in ks])
            run = -share[-1]
            pushed = {}
            for k in every:
                upto = run + share[k]
                pushed[k] = (after[k] + jnp.where(ahead, upto, whole - run)) * slope[k]
                run = upto
            for n, field in enumerate([pushed, slope] + tint):
                for p in ks:
                    cols5[n, q, p, row, col] = (
                        wz[1] * field[p] + wz[2] * field[p - 1] + wz[0] * field[p + 1]
                    )

        each_tile(rows, width, shade)


def ray_order(info, bit, heading):
    lower = ((info[2] >> bit) & 1) == 1
    return heading == jnp.where(lower, 0.0, 1.0)


def scan_body(info, own, other, block, theirs, *refs, bit, rounds, chunk, tile_bit):
    first = bit == 0
    last = bit == rounds - 1
    refs = list(refs)
    state = None if first else refs.pop(0)
    out_state = refs.pop(0)
    out_block = None if last else refs.pop(0)
    out_final = refs.pop(0) if bit == rounds - 2 else None
    mine_scale, their_scale = refs
    rays = (own, other)
    _, rows, width = own.shape
    kept, turn = chunk_mask(info[2], chunk)
    halved = tile_bit is not None and bit >= tile_bit
    my_tile = (info[2] >> (tile_bit or 0)) & 1

    def ray(row, col):
        scales = []
        for q in range(2):
            heading = rays[q][1, row, col]
            earlier = ray_order(info, bit, heading)
            depth = block[0, q, row, col]
            before = jnp.zeros_like(depth) if first else state[0, q, row, col]
            rest = block[1, q, row, col] if first else state[1, q, row, col]
            if last:
                their_depth = their_light = theirs[q, row, col]
            else:
                their_depth, their_light = (theirs[n, q, row, col] for n in range(2))
            fade = jnp.exp(-depth)
            their_fade = jnp.exp(-their_depth)
            later = fade if first else jnp.exp(before - depth)
            out_rest = rest + jnp.where(earlier, 0.0, later * their_light)
            out_before = before + jnp.where(earlier, their_depth, 0.0)
            if last:
                reach = jnp.exp(-out_before)
                out_state[0, q, row, col] = reach
                out_state[1, q, row, col] = reach * out_rest
            else:
                out_state[0, q, row, col] = out_before
                out_state[1, q, row, col] = out_rest
                light = block[1, q, row, col]
                out_depth = depth + their_depth
                out_light = jnp.where(
                    earlier, their_light + their_fade * light, light + fade * their_light
                )
                out_block[0, q, row, col] = out_depth
                out_block[1, q, row, col] = out_light
                if out_final is not None:
                    out_final[q, row, col] = jnp.where(
                        ray_order(info, bit + 1, heading), out_light, out_depth
                    )
            scales.append((jnp.where(earlier, their_fade, 1.0), jnp.where(earlier, 1.0, fade)))
        return [jnp.where(kept, a, pltpu.roll(b, turn, 1)) for a, b in zip(*scales)]

    for i in range(rows // SUB):
        row = pl.ds(i * SUB, SUB)
        packed = [ray(row, pl.ds(j, LANES)) for j in range(0, width, LANES)]
        for n, out in enumerate((mine_scale, their_scale)):
            if halved:
                out[row, :] = jnp.where(my_tile == 0, packed[0][n], packed[1][n])
                continue
            for j, x in enumerate(packed):
                out[row, j * LANES : (j + 1) * LANES] = x[n]


def light_body(info, keep, got, mine_scale, their_scale, *outs, tile_bit):
    mine, theirs = (mine_scale[...], their_scale[...])
    if tile_bit is None:
        for c in range(keep.shape[0]):
            outs[0][c] = mine * keep[c] + theirs * got[c]
        return
    tile = (info[2] >> tile_bit) & 1
    for c in range(keep.shape[0]):
        both = mine * keep[c] + theirs * got[c]
        low, high = (both[:, :LANES], both[:, LANES:])
        outs[0][c] = jnp.where(tile == 0, low, high)
        outs[1][c] = jnp.where(tile == 0, high, low)


def image_body(info, keep, got, mine_scale, their_scale, mine, sent, *, chunk, half, halved):
    s = info[2]
    start = lax.rem(s, half) * chunk
    base = 0 if halved else (start // LANES) * LANES
    cols = pl.ds(pl.multiple_of(base, LANES), LANES)
    start = lax.rem(start, LANES)
    there = jnp.where(lax.rem(s, 2) == 1, start - chunk, start + chunk)
    for c in range(keep.shape[0]):
        both = mine_scale[:, cols] * keep[c, :, cols] + their_scale[:, cols] * got[c, :, cols]
        mine[c] = pltpu.roll(both, lax.rem(LANES - start, LANES), 1)[:, :chunk]
        sent[c] = pltpu.roll(both, lax.rem(LANES - there, LANES), 1)[:, :chunk]


def choose_body(info, mine, got, image, *, half):
    image[0] = jnp.where(info[2] // half == info[0], mine[...], got[...])


def merge_body(info, reach_rest, cols5, own, other, columns, line, edge, corner, strips):
    h, t = (info[0], info[1])
    channels, _, planes, rows, width = columns.shape
    last = LANES - 1
    rays = (own, other)

    def ray(row, col):
        for q in range(2):
            near, far = (reach_rest[0, q, row, col], reach_rest[1, q, row, col])
            for p in range(planes):
                columns[0, q, p, row, col] = (
                    near * cols5[0, q, p, row, col] - far * cols5[1, q, p, row, col]
                )
                for c in range(1, channels):
                    columns[c, q, p, row, col] = near * cols5[c + 1, q, p, row, col]

    each_tile(rows, width, ray)

    down = []
    for r in rays:
        code = jnp.where(t == 0, r[0, rows - 1 : rows, :], r[0, :1, :])
        _, wy, wx = [three(x) for x in split_code(jnp.broadcast_to(code, (planes, width)))]
        y = jnp.where(t == 0, wy[2], wy[0])
        down.append([y * x for x in wx])
    lane = iota((planes, width), 1)
    for c in range(channels):
        for q in range(2):
            for p in range(planes):
                strips[q, p : p + 1, :] = jnp.where(
                    t == 0, columns[c, q, p, rows - 1 : rows, :], columns[c, q, p, :1, :]
                )
        minus, same, plus = [
            down[0][e] * strips[0] + down[1][e] * strips[1] for e in range(3)
        ]
        plus = jnp.where(lane == 0, 0.0, pltpu.roll(plus, 1, 1))
        minus = jnp.where(lane == width - 1, 0.0, pltpu.roll(minus, width - 1, 1))
        line[c] = same + plus + minus

    side = pl.ds(pl.multiple_of(jnp.where(h == 0, width - LANES, 0), LANES), LANES)
    source = jnp.where(h == 0, last, 0)
    lane = iota((rows, LANES), 1)
    row = iota((rows, LANES), 0)
    packed, across = ([], [])
    for q, r in enumerate(rays):
        code = pltpu.roll(r[0, :, side], lax.rem(LANES - source, LANES), 1)
        code = jnp.broadcast_to(code[:, :1], (rows, LANES))
        _, wy, wx = [three(x) for x in split_code(code)]
        x = jnp.where(h == 0, wx[2], wx[0])
        across.append([y * x for y in wy])
        both = jnp.zeros((rows, LANES), F32)
        for c in range(channels):
            for p in range(planes):
                at = c * planes + p
                turn = lax.rem(at - source + LANES, LANES)
                both = jnp.where(lane == at, pltpu.roll(columns[c, q, p, :, side], turn, 1), both)
        packed.append(both)
    part = [across[0][b] * packed[0] + across[1][b] * packed[1] for b in range(3)]
    lower = pltpu.roll(part[2], 1, 0)
    upper = pltpu.roll(part[0], rows - 1, 0)
    edge[...] = (
        part[1] + jnp.where(row == 0, 0.0, lower) + jnp.where(row == rows - 1, 0.0, upper)
    )
    corner[...] = jnp.where(t == 0, lower[:SUB], pltpu.roll(upper[rows - SUB :], 1, 0))


def scatter_body(_, columns, own, other, grad, weights):
    channels, _, planes, rows, width = columns.shape
    lane = iota((rows, width), 1)
    row = iota((rows, width), 0)
    for q, r in enumerate((own, other)):
        _, wy, wx = [three(x) for x in split_code(r[0])]
        for b in range(3):
            for e in range(3):
                weights[q, b * 3 + e] = wy[b] * wx[e]

    def plane(p, carry):
        for c in range(channels):
            col = [columns[c, q, p] for q in range(2)]
            summed = []
            for e in range(3):
                part = [
                    weights[0, b * 3 + e] * col[0] + weights[1, b * 3 + e] * col[1]
                    for b in range(3)
                ]
                down = pltpu.roll(part[2], 1, 0)
                up = pltpu.roll(part[0], rows - 1, 0)
                summed.append(
                    part[1] + jnp.where(row == 0, 0.0, down) + jnp.where(row == rows - 1, 0.0, up)
                )
            right = pltpu.roll(summed[2], 1, 1)
            left = pltpu.roll(summed[0], width - 1, 1)
            grad[c, p] = (
                summed[1]
                + jnp.where(lane == 0, 0.0, right)
                + jnp.where(lane == width - 1, 0.0, left)
            )
        return carry

    lax.fori_loop(0, planes, plane, 0)


def finish_body(info, grad_in, line, edge, corner, grad, buffer, sems):
    h, t = (info[0], info[1])
    channels, planes, rows, width = buffer.shape
    source = jnp.where(h == 0, LANES - 1, 0)
    side = pl.ds(pl.multiple_of(jnp.where(h == 0, width - LANES, 0), LANES), LANES)
    last = jnp.where(t == 0, rows - 1, 0)
    at_row = iota((rows, width), 0) == last
    at_lane = iota((rows, LANES), 1) == source
    packed = edge[...] + jnp.where(iota((rows, LANES), 0) == last, corner[:1], 0.0)
    copies = []
    for c in range(channels):
        for p in range(planes):
            buffer[c, p] = grad_in[c, p] + jnp.where(at_row, line[c, p : p + 1, :], 0.0)
            turn = lax.rem(source - (c * planes + p) + LANES, LANES)
            buffer[c, p, :, side] += jnp.where(at_lane, pltpu.roll(packed, turn, 1), 0.0)
        copies.append(pltpu.make_async_copy(buffer.at[c], grad.at[c], sems.at[c]))
        copies[-1].start()
    for copy in copies:
        copy.wait()


def per_device(voxels, offsets, heading, cotangent):
    channels, planes, rows, total = voxels.shape
    dirs, slabs, cores = (lax.axis_size(a) for a in ("dir", "slab", "tile"))
    if dirs != 2 or cores != 2 or slabs & (slabs - 1) or 2 * total > slabs * LANES:
        raise ValueError("mesh")
    width = total // dirs
    depth = planes * slabs
    scale = 2.0 / depth
    swap = [(0, 1), (1, 0)]
    count = width // LANES
    grid = lambda n: pltpu.VMEM((3, channels, n, rows + 2 * SUB, width), F32)
    colours = channels - 1
    half = slabs // dirs
    chunk = total // slabs
    rounds = slabs.bit_length() - 1
    tile_bit = (LANES // chunk).bit_length() - 1
    tile_bit = tile_bit if 0 < tile_bit < rounds - 1 else None

    pairs_a = [(i, i ^ 1) for i in range(slabs)]
    pairs_b = [(i, i + 1) for i in range(1, slabs - 1, 2)]
    pairs_b = pairs_b + [(b, a) for a, b in pairs_b]

    hbm = pl.BlockSpec(memory_space=pltpu.HBM)
    ray = shape(channels + 1, rows, width)
    own, sent, line = call(
        first_body,
        [ray, ray, shape(channels, planes, total)],
        (offsets, heading, cotangent, voxels),
        specs=[hbm] * 4,
        scratch=[
            pltpu.VMEM(offsets.shape, jnp.int32),
            pltpu.VMEM(heading.shape, jnp.int32),
            pltpu.VMEM(cotangent.shape, F32),
            pltpu.VMEM((channels, planes, SUB, total), F32),
            pltpu.SemaphoreType.DMA((4,)),
        ],
        limit=62,
        width=width,
        depth=depth,
    )
    line = lax.ppermute(line, "tile", swap)
    other = lax.ppermute(sent, "dir", swap)

    def block(k):
        return pl.BlockSpec((channels, 1, rows, total), lambda i: (0, k, 0, 0))

    near = call(
        pack_body,
        [shape(message_rows(channels, rows, count)[2], LANES)] * 2,
        (voxels, voxels, line),
        specs=[block(0), block(planes - 1), VMEM],
        width=width,
    )
    near = [lax.ppermute(x, "slab", p) for x, p in zip(near, (pairs_a, pairs_b))]

    two = shape(2, channels, 2, rows, width)
    pair = shape(2, 2, rows, width)
    vals, part, ends, inner = call(
        inner_body,
        [shape(2, channels, planes - 2, rows, width), two, two, shape(channels, 2, rows, width)],
        (voxels, line, own, other),
        scratch=[grid(planes)],
        limit=20,
        width=width,
        scale=scale,
    )
    light = shape(colours, rows, width)
    pay, rim, ends, keep, send = call(
        rim_body,
        [pair, two, two, light, light],
        (*near, own, other, part, ends, inner),
        scratch=[grid(2)],
        scale=scale,
        chunk=chunk,
    )
    cols5 = call(
        column_body,
        shape(channels + 1, 2, planes, rows, width),
        (own, other, vals, rim, ends),
        scale=scale,
        slabs=slabs,
    )

    message, state = (pay, ())
    for bit in range(rounds):
        pairs = [(i, i ^ (1 << bit)) for i in range(slabs)]
        last = bit == rounds - 1
        theirs = lax.ppermute(message, "slab", pairs)
        got = lax.ppermute(send, "slab", pairs)
        halved = tile_bit is not None and bit >= tile_bit
        factor = shape(rows, LANES if halved else width)
        outs = [pair] + ([] if last else [pair])
        outs = outs + ([shape(2, rows, width)] if bit == rounds - 2 else []) + [factor] * 2
        state, *others, mine_scale, their_scale = call(
            scan_body,
            outs,
            (own, other, pay, theirs) + tuple(state),
            bit=bit,
            rounds=rounds,
            chunk=chunk,
            tile_bit=tile_bit,
        )
        if not last:
            pay, message = (others[0], others[-1])
            state = (state,)
        if last:
            break
        split = tile_bit if bit + 1 == tile_bit else None
        kept = shape(colours, rows, LANES) if split is not None else shape(*keep.shape)
        pieces = call(
            light_body,
            [kept] * (1 if split is None else 2),
            (keep, got, mine_scale, their_scale),
            tile_bit=split,
        )
        keep, send = (pieces[0], pieces[-1])

    columns, line, edge, corner = call(
        merge_body,
        [
            shape(channels, 2, planes, rows, width),
            shape(channels, planes, width),
            shape(rows, LANES),
            shape(SUB, LANES),
        ],
        (state, cols5, own, other),
        scratch=[pltpu.VMEM((2, planes, width), F32)],
    )
    edge = lax.ppermute(edge, "dir", swap)
    corner = lax.ppermute(corner, ("dir", "tile"), [(i, 3 - i) for i in range(4)])
    line = lax.ppermute(line, "tile", swap)
    grad_shape = (channels, planes, rows, width)
    grad = call(
        scatter_body,
        shape(*grad_shape),
        (columns, own, other),
        scratch=[pltpu.VMEM((2, 9, rows, width), F32)],
    )
    voxel_grad = call(
        finish_body,
        shape(*grad_shape),
        (grad, line, edge, corner),
        scratch=[pltpu.VMEM(grad_shape, F32), pltpu.SemaphoreType.DMA((channels,))],
        out_specs=hbm,
    )

    piece = shape(colours, rows, chunk)
    mine, sent = call(
        image_body,
        [piece, piece],
        (keep, got, mine_scale, their_scale),
        chunk=chunk,
        half=half,
        halved=tile_bit is not None,
    )
    got = lax.ppermute(sent, "dir", swap)
    image = call(choose_body, shape(1, colours, rows, chunk), (mine, got), half=half)
    return (image, voxel_grad)


def solution(mesh):
    return jax.shard_map(
        per_device,
        mesh=mesh,
        in_specs=(
            P(None, "slab", "tile", None),
            P("dir", "tile", None),
            P("dir", "tile", None),
            P("dir", None, "tile", None),
        ),
        out_specs=(P("dir", None, "tile", "slab"), P(None, "slab", "tile", "dir")),
        check_vma=False,
    )
```

```python
import functools

import jax
import jax.numpy as jnp
from jax import lax
from jax.experimental import pallas as pl
from jax.experimental.pallas import tpu as pltpu
from jax.sharding import PartitionSpec as P


LEVELS = 8
BITS = LEVELS.bit_length() - 1
LANES = 128
SUB = 8
F32 = jnp.float32
VMEM = pl.BlockSpec(memory_space=pltpu.VMEM)
MIB = 2**20


def call(body, outs, args, scratch=(), limit=16, specs=None, out_specs=None, **statics):
    def kernel(*refs):
        body(tuple(lax.axis_index(a) for a in ("dir", "tile", "slab")), *refs, **statics)

    grid = {} if specs is None else dict(grid=(1,))
    return pl.pallas_call(
        kernel,
        out_shape=outs,
        in_specs=specs or [VMEM] * len(args),
        out_specs=out_specs or jax.tree.map(lambda _: VMEM, outs),
        scratch_shapes=list(scratch),
        cost_estimate=pl.CostEstimate(flops=10**7, bytes_accessed=2 * 10**6, transcendentals=0),
        compiler_params=pltpu.CompilerParams(vmem_limit_bytes=limit * MIB),
        **grid,
    )(*args)


def shape(*dims):
    return jax.ShapeDtypeStruct(dims, F32)


def iota(dims, axis):
    return lax.broadcasted_iota(jnp.int32, dims, axis)


def fraction(raw):
    return (raw.astype(F32) + 0.5) / LEVELS - 0.5


def three(raw):
    f = fraction(raw)
    return (jnp.maximum(-f, 0.0), 1.0 - jnp.abs(f), jnp.maximum(f, 0.0))


def split_code(code):
    q = code.astype(jnp.int32)
    return (q & (LEVELS - 1), (q >> BITS) & (LEVELS - 1), q >> (2 * BITS))


def logistic(v):
    return 0.5 * jnp.tanh(0.5 * v) + 0.5


def total_of(terms):
    return functools.reduce(lambda a, b: a + b, terms)


def log_soft(v):
    return jnp.maximum(v, 0.0) + jnp.log(1.0 + jnp.exp(-jnp.abs(v)))


def shifts(tiles, beside, h):
    lane = iota(tiles[0].shape, 1)
    last = LANES - 1
    zero = jnp.zeros_like(beside)
    right = [pltpu.roll(x, 1, 1) for x in tiles]
    left = [pltpu.roll(x, last, 1) for x in tiles]
    below = [jnp.where(h == 1, beside, zero)] + right[:-1]
    above = left[1:] + [jnp.where(h == 0, beside, zero)]
    minus = [jnp.where(lane == 0, b, r) for b, r in zip(below, right)]
    plus = [jnp.where(lane == last, a, x) for a, x in zip(above, left)]
    return (minus, tiles, plus)


def beside_shift(source, h):
    target = jnp.where(h == 1, 0, LANES - 1)
    return lax.rem(target - source + LANES, LANES)


def window_parts(h, width):
    base = pl.multiple_of(h * width, LANES)
    side = pl.multiple_of(width - LANES * h, LANES)
    source = jnp.where(h == 0, 0, LANES - 1)
    return base, side, source


def first_body(info, offsets, heading, cotangent, voxels, own, sent, line, code, head, cot, strip, sems, *, width, depth):
    h, t = (info[0], info[1])
    channels, planes, rows, _ = voxels.shape
    row = pl.multiple_of(jnp.where(t == 0, rows - SUB, 0), SUB)
    copies = [
        pltpu.make_async_copy(voxels.at[:, :, pl.ds(row, SUB), :], strip, sems.at[0]),
        pltpu.make_async_copy(offsets, code, sems.at[1]),
        pltpu.make_async_copy(heading, head, sems.at[2]),
        pltpu.make_async_copy(cotangent, cot, sems.at[3]),
    ]
    for copy in copies:
        copy.start()
    copies[0].wait()
    for c in range(channels):
        for k in range(planes):
            line[c, k : k + 1, :] = jnp.where(
                t == 0, strip[c, k, SUB - 1 : SUB, :], strip[c, k, :1, :]
            )
    for copy in copies[1:]:
        copy.wait()
    for out, at in ((own, h), (sent, 1 - h)):
        cols = pl.ds(pl.multiple_of(at * width, LANES), width)
        out[0] = code[0, :, cols].astype(F32)
        out[1] = head[0, :, cols].astype(F32)
        for c in range(channels - 1):
            out[2 + c] = cot[0, c, :, cols] * depth


def message_rows(channels, rows, count):
    body = channels * count * rows
    lines = -(-channels * count // SUB) * SUB
    return body, body + lines, body + lines + rows


def pack_body(info, first, last, line, out_a, out_b, *, width):
    h, s = (info[0], info[2])
    channels, _, rows, _ = first.shape
    planes = line.shape[1]
    count = width // LANES
    base, side, source = window_parts(h, width)
    at_line, at_edge, _ = message_rows(channels, rows, count)
    lane = iota((rows, LANES), 1)

    def fill(block, k, out):
        edge = jnp.zeros((rows, LANES), F32)
        for c in range(channels):
            for j in range(count):
                at = c * count + j
                cols = pl.ds(base + j * LANES, LANES)
                out[at * rows : (at + 1) * rows, :] = block[c, 0, :, cols]
                out[at_line + at : at_line + at + 1, :] = line[c, k : k + 1, cols]
            cols = pl.ds(side, LANES)
            turn = lax.rem(c - source + LANES, LANES)
            edge = jnp.where(lane == c, pltpu.roll(block[c, 0, :, cols], turn, 1), edge)
            turn = lax.rem(channels + c - source + LANES, LANES)
            corner = jnp.broadcast_to(line[c, k : k + 1, cols], (SUB, LANES))
            corner = pltpu.roll(corner, turn, 1)[:1]
            edge = jnp.where(lane == channels + c, corner, edge)
        out[at_edge:, :] = edge

    @pl.when(s % 2 == 0)
    def _():
        fill(last, planes - 1, out_a)
        fill(first, 0, out_b)

    @pl.when(s % 2 == 1)
    def _():
        fill(first, 0, out_a)
        fill(last, planes - 1, out_b)


def spread_message(msg, grid, plane, info, channels, rows, count):
    h, t = (info[0], info[1])
    at_line, at_edge, _ = message_rows(channels, rows, count)
    edge = msg[at_edge:, :]
    beyond = pl.ds(pl.multiple_of(jnp.where(t == 0, SUB + rows, 0), SUB), SUB)
    for c in range(channels):
        first = c * count
        tiles = [msg[(first + j) * rows : (first + j + 1) * rows, :] for j in range(count)]
        lines = [
            jnp.broadcast_to(msg[at_line + first + j : at_line + first + j + 1, :], (SUB, LANES))
            for j in range(count)
        ]
        side = pltpu.roll(edge, beside_shift(c, h), 1)
        corner = pltpu.roll(edge[:SUB], beside_shift(channels + c, h), 1)
        for e, xs in enumerate(shifts(tiles, side, h)):
            for j, x in enumerate(xs):
                grid[e, c, plane, SUB : SUB + rows, j * LANES : (j + 1) * LANES] = x
        for e, xs in enumerate(shifts(lines, corner, h)):
            for j, x in enumerate(xs):
                grid[e, c, plane, beyond, j * LANES : (j + 1) * LANES] = x


def taps(code, row0, t, rows):
    _, m, n = split_code(code)
    fy, fx = (fraction(m), fraction(n))
    row = iota(code.shape, 0) + row0
    low = (row == 0) & (t == 0)
    high = (row == rows - 1) & (t == 1)
    up = ((fy > 0.0) & jnp.logical_not(high)) | low
    ay, ax = (jnp.abs(fy), jnp.abs(fx))
    gone = (low & (fy < 0.0)) | (high & (fy > 0.0))
    by = jnp.where(gone, 0.0, ay)
    return (up, fx > 0.0, (1.0 - ay) * (1.0 - ax), (1.0 - ay) * ax, by * (1.0 - ax), by * ax)


def bilinear(rays, grid, c, plane, row0, cols):
    v = [
        [grid[e, c, plane, row0 + b + SUB - 1 : row0 + b + 2 * SUB - 1, cols] for e in range(3)]
        for b in range(3)
    ]
    out = []
    for up, right, centre, across, along, diagonal in rays:
        row = [jnp.where(up, v[2][e], v[0][e]) for e in range(3)]
        out.append(
            centre * v[1][1]
            + across * jnp.where(right, v[1][2], v[1][0])
            + along * row[1]
            + diagonal * jnp.where(right, row[2], row[0])
        )
    return out


def ray_tiles(rays, rows, width, t):
    for i in range(rows // SUB):
        for j in range(width // LANES):
            at = slice(i * SUB, (i + 1) * SUB)
            cols = slice(j * LANES, (j + 1) * LANES)
            codes = [r[0, at, cols] for r in rays]
            yield (
                i * SUB,
                at,
                cols,
                [taps(q, i * SUB, t, rows) for q in codes],
                [three(split_code(q)[0]) for q in codes],
            )


def each_tile(rows, width, body, unroll=False):
    count = width // LANES
    if unroll:
        for i in range(rows // SUB):
            for j in range(count):
                body(pl.ds(i * SUB, SUB), pl.ds(j * LANES, LANES))
        return

    def step(n, carry):
        row = pl.ds(pl.multiple_of((n // count) * SUB, SUB), SUB)
        col = pl.ds(pl.multiple_of((n % count) * LANES, LANES), LANES)
        body(row, col)
        return carry

    lax.fori_loop(0, (rows // SUB) * count, step, 0)


def products(left):
    ones = jnp.ones_like(left[0])
    rising, falling = ([ones], [ones])
    for x in left[:-1]:
        rising.append(rising[-1] * x)
    for x in left[:0:-1]:
        falling.append(falling[-1] * x)
    return rising, falling[::-1]


def place_body(info, vox, line, grid, *, width):
    h, t, _ = info
    channels, planes, rows, _ = vox.shape
    count = width // LANES
    base, side, source = window_parts(h, width)
    turn = beside_shift(source, h)

    for k in range(planes):
        for c in range(channels):
            tiles = [vox[c, k, :, pl.ds(base + j * LANES, LANES)] for j in range(count)]
            beside = pltpu.roll(vox[c, k, :, pl.ds(side, LANES)], turn, 1)
            for e, xs in enumerate(shifts(tiles, beside, h)):
                for j, x in enumerate(xs):
                    grid[e, c, k, SUB : SUB + rows, j * LANES : (j + 1) * LANES] = x
    beyond = pl.ds(pl.multiple_of(jnp.where(t == 0, SUB + rows, 0), SUB), SUB)
    for c in range(channels):
        tiles = [line[c, :, pl.ds(base + j * LANES, LANES)] for j in range(count)]
        beside = pltpu.roll(line[c, :, pl.ds(side, LANES)], turn, 1)
        for e, xs in enumerate(shifts(tiles, beside, h)):
            for j, x in enumerate(xs):
                for k in range(planes):
                    grid[e, c, k, beyond, j * LANES : (j + 1) * LANES] = jnp.broadcast_to(
                        x[k : k + 1], (SUB, LANES)
                    )


def inner_body(info, grid, own, other, vals, part, ends, inner, *, scale):
    t = info[1]
    _, rows, width = own.shape
    channels, planes = grid.shape[1:3]
    rays = (own, other)
    for row0, at, cols, yx, wz in ray_tiles(rays, rows, width, t):

        def channel(c, carry, row0=row0, at=at, cols=cols, yx=yx, wz=wz):
            old = [None, None]
            for p in range(planes):
                new = bilinear(yx, grid, c, p, row0, cols)
                for q in range(2):
                    w = wz[q]
                    if p == 0:
                        ends[q, c, 0, at, cols] = w[2] * new[q]
                    elif p == 1:
                        part[q, c, 0, at, cols] = w[1] * old[1][q] + w[2] * new[q]
                    else:
                        vals[q, c, p - 2, at, cols] = (
                            w[0] * old[0][q] + w[1] * old[1][q] + w[2] * new[q]
                        )
                    if p == planes - 1:
                        part[q, c, 1, at, cols] = w[0] * old[1][q] + w[1] * new[q]
                        ends[q, c, 1, at, cols] = w[0] * new[q]
                old = [old[1], new]
            return carry

        lax.fori_loop(0, channels, channel, 0)

    for q in range(2):

        def shade(row, col, q=q):
            ahead = rays[q][1, row, col] == 0.0
            sigma = [log_soft(vals[q, 0, k, row, col]) * scale for k in range(planes - 2)]
            left = [jnp.exp(-x) for x in sigma]
            rising, falling = products(left)
            light = [None] * (channels - 1)
            for k in range(planes - 2):
                glow = jnp.where(ahead, rising[k], falling[k]) * (1.0 - left[k])
                for c in range(channels - 1):
                    term = glow * logistic(vals[q, c + 1, k, row, col])
                    light[c] = term if k == 0 else light[c] + term
            inner[0, q, row, col] = total_of(sigma)
            for c in range(channels - 1):
                inner[c + 1, q, row, col] = light[c]

        each_tile(rows, width, shade)


def chunk_mask(s, chunk):
    bit = (iota((SUB, LANES), 1) >> (chunk.bit_length() - 1)) & 1
    mine = s & 1
    return bit == mine, jnp.where(mine == 1, LANES - chunk, chunk)


def rim_body(info, near_a, near_b, own, other, part, ends, inner, pay, rim, ends_out, keep, send, grid, *, scale, chunk):
    t, s = (info[1], info[2])
    _, channels, _, rows, width = part.shape
    count = width // LANES
    even = s % 2 == 0
    rays = (own, other)
    spread_message(near_a, grid, jnp.where(even, 1, 0), info, channels, rows, count)
    spread_message(near_b, grid, jnp.where(even, 0, 1), info, channels, rows, count)
    for row0, at, cols, yx, wz in ray_tiles(rays, rows, width, t):

        def channel(c, carry, row0=row0, at=at, cols=cols, yx=yx, wz=wz):
            for p in range(2):
                new = bilinear(yx, grid, c, p, row0, cols)
                for q in range(2):
                    rim[q, c, p, at, cols] = part[q, c, p, at, cols] + wz[q][2 * p] * new[q]
                    ends_out[q, c, p, at, cols] = ends[q, c, p, at, cols] + wz[q][1] * new[q]
            return carry

        lax.fori_loop(0, channels, channel, 0)
    kept, turn = chunk_mask(s, chunk)

    def shade(row, col):
        lights = []
        for q in range(2):
            ahead = rays[q][1, row, col] == 0.0
            sigma = [log_soft(rim[q, 0, p, row, col]) * scale for p in range(2)]
            left = [jnp.exp(-x) for x in sigma]
            middle = inner[0, q, row, col]
            through = jnp.exp(-middle)
            first = jnp.where(ahead, left[0], left[1])
            last = first * through
            pay[0, q, row, col] = sigma[0] + middle + sigma[1]
            low = jnp.where(ahead, 1.0, last) * (1.0 - left[0])
            high = jnp.where(ahead, last, 1.0) * (1.0 - left[1])
            light = [
                low * logistic(rim[q, c + 1, 0, row, col])
                + first * inner[c + 1, q, row, col]
                + high * logistic(rim[q, c + 1, 1, row, col])
                for c in range(channels - 1)
            ]
            pay[1, q, row, col] = total_of([rays[q][2 + c, row, col] * x for c, x in enumerate(light)])
            lights.append(light)
        for c, (a, b) in enumerate(zip(*lights)):
            keep[c, row, col] = jnp.where(kept, a, pltpu.roll(b, turn, 1))
            send[c, row, col] = jnp.where(kept, pltpu.roll(b, LANES - turn, 1), a)

    each_tile(rows, width, shade, unroll=True)


def column_body(info, own, other, vals, rim, ends, cols5, *, scale, slabs):
    s = info[2]
    _, channels, inside, rows, width = vals.shape
    planes = inside + 2
    rays = (own, other)
    live = {-1: jnp.where(s > 0, 1.0, 0.0), planes: jnp.where(s < slabs - 1, 1.0, 0.0)}
    for q in range(2):

        def shade(row, col, q=q):
            ahead = rays[q][1, row, col] == 0.0
            wz = three(split_code(rays[q][0, row, col])[0])
            pull = [rays[q][2 + c, row, col] for c in range(channels - 1)]

            def value(c, k):
                if k in live:
                    return ends[q, c, 1 if k > 0 else 0, row, col]
                if k == 0 or k == planes - 1:
                    return rim[q, c, 1 if k else 0, row, col]
                return vals[q, c, k - 1, row, col]

            ks = range(planes)
            every = range(-1, planes + 1)
            sigma = {k: log_soft(value(0, k)) * scale for k in every}
            slope = {k: logistic(value(0, k)) * scale for k in every}
            left = {k: jnp.exp(-sigma[k]) for k in every}
            rising, falling = products([left[k] for k in ks])
            through = rising[-1] * left[planes - 1]
            share, after = ({}, {})
            tint = [{} for _ in range(channels - 1)]
            for k in every:
                if k == -1:
                    reach = jnp.where(ahead, jnp.exp(sigma[k]), through)
                elif k == planes:
                    reach = jnp.where(ahead, through, jnp.exp(sigma[k]))
                else:
                    reach = jnp.where(ahead, rising[k], falling[k])
                glow = reach * (1.0 - left[k])
                if k in live:
                    glow = glow * live[k]
                    slope[k] = slope[k] * live[k]
                hue = []
                for c in range(channels - 1):
                    colour = logistic(value(c + 1, k))
                    hue.append(pull[c] * colour)
                    tint[c][k] = glow * hue[-1] * (1.0 - colour)
                hue = total_of(hue)
                share[k] = glow * hue
                after[k] = reach * left[k] * hue
            whole = total_of([share[k] for k in ks])
            run = -share[-1]
            pushed = {}
            for k in every:
                upto = run + share[k]
                pushed[k] = (after[k] + jnp.where(ahead, upto, whole - run)) * slope[k]
                run = upto
            for n, field in enumerate([pushed, slope] + tint):
                for p in ks:
                    cols5[n, q, p, row, col] = (
                        wz[1] * field[p] + wz[2] * field[p - 1] + wz[0] * field[p + 1]
                    )

        each_tile(rows, width, shade)


def ray_order(info, bit, heading):
    lower = ((info[2] >> bit) & 1) == 1
    return heading == jnp.where(lower, 0.0, 1.0)


def scan_body(info, own, other, block, theirs, *refs, bit, rounds, chunk, tile_bit):
    first = bit == 0
    last = bit == rounds - 1
    refs = list(refs)
    state = None if first else refs.pop(0)
    out_state = refs.pop(0)
    out_block = None if last else refs.pop(0)
    out_final = refs.pop(0) if bit == rounds - 2 else None
    mine_scale, their_scale = refs
    rays = (own, other)
    _, rows, width = own.shape
    kept, turn = chunk_mask(info[2], chunk)
    halved = tile_bit is not None and bit >= tile_bit
    my_tile = (info[2] >> (tile_bit or 0)) & 1

    def ray(row, col):
        scales = []
        for q in range(2):
            heading = rays[q][1, row, col]
            earlier = ray_order(info, bit, heading)
            depth = block[0, q, row, col]
            before = jnp.zeros_like(depth) if first else state[0, q, row, col]
            rest = block[1, q, row, col] if first else state[1, q, row, col]
            if last:
                their_depth = their_light = theirs[q, row, col]
            else:
                their_depth, their_light = (theirs[n, q, row, col] for n in range(2))
            fade = jnp.exp(-depth)
            their_fade = jnp.exp(-their_depth)
            later = fade if first else jnp.exp(before - depth)
            out_rest = rest + jnp.where(earlier, 0.0, later * their_light)
            out_before = before + jnp.where(earlier, their_depth, 0.0)
            if last:
                reach = jnp.exp(-out_before)
                out_state[0, q, row, col] = reach
                out_state[1, q, row, col] = reach * out_rest
            else:
                out_state[0, q, row, col] = out_before
                out_state[1, q, row, col] = out_rest
                light = block[1, q, row, col]
                out_depth = depth + their_depth
                out_light = jnp.where(
                    earlier, their_light + their_fade * light, light + fade * their_light
                )
                out_block[0, q, row, col] = out_depth
                out_block[1, q, row, col] = out_light
                if out_final is not None:
                    out_final[q, row, col] = jnp.where(
                        ray_order(info, bit + 1, heading), out_light, out_depth
                    )
            scales.append((jnp.where(earlier, their_fade, 1.0), jnp.where(earlier, 1.0, fade)))
        return [jnp.where(kept, a, pltpu.roll(b, turn, 1)) for a, b in zip(*scales)]

    for i in range(rows // SUB):
        row = pl.ds(i * SUB, SUB)
        packed = [ray(row, pl.ds(j, LANES)) for j in range(0, width, LANES)]
        for n, out in enumerate((mine_scale, their_scale)):
            if halved:
                out[row, :] = jnp.where(my_tile == 0, packed[0][n], packed[1][n])
                continue
            for j, x in enumerate(packed):
                out[row, j * LANES : (j + 1) * LANES] = x[n]


def light_body(info, keep, got, mine_scale, their_scale, *outs, tile_bit):
    mine, theirs = (mine_scale[...], their_scale[...])
    if tile_bit is None:
        for c in range(keep.shape[0]):
            outs[0][c] = mine * keep[c] + theirs * got[c]
        return
    tile = (info[2] >> tile_bit) & 1
    for c in range(keep.shape[0]):
        both = mine * keep[c] + theirs * got[c]
        low, high = (both[:, :LANES], both[:, LANES:])
        outs[0][c] = jnp.where(tile == 0, low, high)
        outs[1][c] = jnp.where(tile == 0, high, low)


def gather_body(info, edge, line, keep, got, mine_scale, their_scale, mine, out, *, chunk, half, halved):
    _, t, s = info
    rows = edge.shape[0]
    body = line.shape[0] - SUB
    start = lax.rem(s, half) * chunk
    base = 0 if halved else (start // LANES) * LANES
    cols = pl.ds(pl.multiple_of(base, LANES), LANES)
    start = lax.rem(start, LANES)
    there = jnp.where(lax.rem(s, 2) == 1, start - chunk, start + chunk)
    border = iota((rows, LANES), 0) == jnp.where(t == 0, rows - 1, 0)
    out[:rows, :] = edge[...] + jnp.where(border, line[body : body + 1, :LANES], 0.0)
    for c in range(keep.shape[0]):
        both = mine_scale[:, cols] * keep[c, :, cols] + their_scale[:, cols] * got[c, :, cols]
        mine[c] = pltpu.roll(both, lax.rem(LANES - start, LANES), 1)[:, :chunk]
        out[(c + 1) * rows : (c + 2) * rows, :] = pltpu.roll(
            both, lax.rem(LANES - there, LANES), 1
        )


def merge_body(info, reach_rest, cols5, own, other, columns, line, edge, strips):
    h, t = (info[0], info[1])
    channels, _, planes, rows, width = columns.shape
    last = LANES - 1
    rays = (own, other)

    def ray(row, col):
        for q in range(2):
            near, far = (reach_rest[0, q, row, col], reach_rest[1, q, row, col])
            for p in range(planes):
                columns[0, q, p, row, col] = (
                    near * cols5[0, q, p, row, col] - far * cols5[1, q, p, row, col]
                )
                for c in range(1, channels):
                    columns[c, q, p, row, col] = near * cols5[c + 1, q, p, row, col]

    each_tile(rows, width, ray)

    down = []
    for r in rays:
        code = jnp.where(t == 0, r[0, rows - 1 : rows, :], r[0, :1, :])
        _, wy, wx = [three(x) for x in split_code(jnp.broadcast_to(code, (planes, width)))]
        y = jnp.where(t == 0, wy[2], wy[0])
        down.append([y * x for x in wx])
    lane = iota((planes, width), 1)
    for c in range(channels):
        for q in range(2):
            for p in range(planes):
                strips[q, p : p + 1, :] = jnp.where(
                    t == 0, columns[c, q, p, rows - 1 : rows, :], columns[c, q, p, :1, :]
                )
        minus, same, plus = [
            down[0][e] * strips[0] + down[1][e] * strips[1] for e in range(3)
        ]
        plus = jnp.where(lane == 0, 0.0, pltpu.roll(plus, 1, 1))
        minus = jnp.where(lane == width - 1, 0.0, pltpu.roll(minus, width - 1, 1))
        line[c * planes : (c + 1) * planes, :] = same + plus + minus

    side = pl.ds(pl.multiple_of(jnp.where(h == 0, width - LANES, 0), LANES), LANES)
    source = jnp.where(h == 0, last, 0)
    lane = iota((rows, LANES), 1)
    row = iota((rows, LANES), 0)
    packed, across = ([], [])
    for q, r in enumerate(rays):
        code = pltpu.roll(r[0, :, side], lax.rem(LANES - source, LANES), 1)
        code = jnp.broadcast_to(code[:, :1], (rows, LANES))
        _, wy, wx = [three(x) for x in split_code(code)]
        x = jnp.where(h == 0, wx[2], wx[0])
        across.append([y * x for y in wy])
        both = jnp.zeros((rows, LANES), F32)
        for c in range(channels):
            for p in range(planes):
                at = c * planes + p
                turn = lax.rem(at - source + LANES, LANES)
                both = jnp.where(lane == at, pltpu.roll(columns[c, q, p, :, side], turn, 1), both)
        packed.append(both)
    part = [across[0][b] * packed[0] + across[1][b] * packed[1] for b in range(3)]
    lower = pltpu.roll(part[2], 1, 0)
    upper = pltpu.roll(part[0], rows - 1, 0)
    edge[...] = (
        part[1] + jnp.where(row == 0, 0.0, lower) + jnp.where(row == rows - 1, 0.0, upper)
    )
    line[channels * planes :, :LANES] = jnp.where(t == 0, lower[:SUB], pltpu.roll(upper[rows - SUB :], 1, 0))


def scatter_body(_, columns, own, other, grad, weights):
    channels, _, planes, rows, width = columns.shape
    lane = iota((rows, width), 1)
    row = iota((rows, width), 0)
    for q, r in enumerate((own, other)):
        _, wy, wx = [three(x) for x in split_code(r[0])]
        for b in range(3):
            for e in range(3):
                weights[q, b * 3 + e] = wy[b] * wx[e]

    def plane(p, carry):
        for c in range(channels):
            col = [columns[c, q, p] for q in range(2)]
            summed = []
            for e in range(3):
                part = [
                    weights[0, b * 3 + e] * col[0] + weights[1, b * 3 + e] * col[1]
                    for b in range(3)
                ]
                down = pltpu.roll(part[2], 1, 0)
                up = pltpu.roll(part[0], rows - 1, 0)
                summed.append(
                    part[1] + jnp.where(row == 0, 0.0, down) + jnp.where(row == rows - 1, 0.0, up)
                )
            right = pltpu.roll(summed[2], 1, 1)
            left = pltpu.roll(summed[0], width - 1, 1)
            grad[c, p] = (
                summed[1]
                + jnp.where(lane == 0, 0.0, right)
                + jnp.where(lane == width - 1, 0.0, left)
            )
        return carry

    lax.fori_loop(0, planes, plane, 0)


def finish_body(info, grad_in, line, cross, mine, grad, image, buffer, picture, sems, *, half):
    h, t, s = info
    channels, planes, rows, width = buffer.shape
    source = jnp.where(h == 0, LANES - 1, 0)
    side = pl.ds(pl.multiple_of(jnp.where(h == 0, width - LANES, 0), LANES), LANES)
    last = jnp.where(t == 0, rows - 1, 0)
    at_row = iota((rows, width), 0) == last
    at_lane = iota((rows, LANES), 1) == source
    packed = cross[:rows, :]
    here = s // half == h
    for c in range(channels - 1):
        picture[0, c] = jnp.where(here, mine[c], cross[(c + 1) * rows : (c + 2) * rows, : picture.shape[3]])
    copies = [pltpu.make_async_copy(picture, image, sems.at[channels])]
    copies[0].start()
    for c in range(channels):
        for p in range(planes):
            at = c * planes + p
            buffer[c, p] = grad_in[c, p] + jnp.where(at_row, line[at : at + 1, :], 0.0)
            turn = lax.rem(source - at + LANES, LANES)
            buffer[c, p, :, side] += jnp.where(at_lane, pltpu.roll(packed, turn, 1), 0.0)
        copies.append(pltpu.make_async_copy(buffer.at[c], grad.at[c], sems.at[c]))
        copies[-1].start()
    for copy in copies:
        copy.wait()


def per_device(voxels, offsets, heading, cotangent):
    channels, planes, rows, total = voxels.shape
    dirs, slabs, cores = (lax.axis_size(a) for a in ("dir", "slab", "tile"))
    if dirs != 2 or cores != 2 or slabs & (slabs - 1) or 2 * total > slabs * LANES:
        raise ValueError("mesh")
    width = total // dirs
    depth = planes * slabs
    scale = 2.0 / depth
    swap = [(0, 1), (1, 0)]
    count = width // LANES
    grid = lambda n: pltpu.VMEM((3, channels, n, rows + 2 * SUB, width), F32)
    colours = channels - 1
    half = slabs // dirs
    chunk = total // slabs
    rounds = slabs.bit_length() - 1
    tile_bit = (LANES // chunk).bit_length() - 1
    tile_bit = tile_bit if 0 < tile_bit < rounds - 1 else None

    pairs_a = [(i, i ^ 1) for i in range(slabs)]
    pairs_b = [(i, i + 1) for i in range(1, slabs - 1, 2)]
    pairs_b = pairs_b + [(b, a) for a, b in pairs_b]

    hbm = pl.BlockSpec(memory_space=pltpu.HBM)
    ray = shape(channels + 1, rows, width)
    own, sent, line = call(
        first_body,
        [ray, ray, shape(channels, planes, total)],
        tuple(
            pltpu.with_memory_space_constraint(x, pltpu.HBM)
            for x in (offsets, heading, cotangent, voxels)
        ),
        specs=[hbm] * 4,
        scratch=[
            pltpu.VMEM(offsets.shape, jnp.int32),
            pltpu.VMEM(heading.shape, jnp.int32),
            pltpu.VMEM(cotangent.shape, F32),
            pltpu.VMEM((channels, planes, SUB, total), F32),
            pltpu.SemaphoreType.DMA((4,)),
        ],
        limit=8,
        width=width,
        depth=depth,
    )
    line = lax.ppermute(line, "tile", swap)
    other = lax.ppermute(sent, "dir", swap)

    def block(k):
        return pl.BlockSpec((channels, 1, rows, total), lambda i: (0, k, 0, 0))

    near = call(
        pack_body,
        [shape(message_rows(channels, rows, count)[2], LANES)] * 2,
        (voxels, voxels, line),
        specs=[block(0), block(planes - 1), VMEM],
        width=width,
    )
    near = list(near)
    near[0] = lax.ppermute(near[0], "slab", pairs_a)
    near[1] = lax.ppermute(near[1], "slab", pairs_b)

    two = shape(2, channels, 2, rows, width)
    pair = shape(2, 2, rows, width)
    placed = call(
        place_body, shape(3, channels, planes, rows + 2 * SUB, width), (voxels, line), width=width
    )
    vals, part, ends, inner = call(
        inner_body,
        [shape(2, channels, planes - 2, rows, width), two, two, shape(channels, 2, rows, width)],
        (placed, own, other),
        scale=scale,
    )
    light = shape(colours, rows, width)
    pay, rim, ends, keep, send = call(
        rim_body,
        [pair, two, two, light, light],
        (*near, own, other, part, ends, inner),
        scratch=[grid(2)],
        scale=scale,
        chunk=chunk,
    )
    cols5 = call(
        column_body,
        shape(channels + 1, 2, planes, rows, width),
        (own, other, vals, rim, ends),
        scale=scale,
        slabs=slabs,
    )

    message, state = (pay, ())
    for bit in range(rounds):
        pairs = [(i, i ^ (1 << bit)) for i in range(slabs)]
        last = bit == rounds - 1
        theirs = lax.ppermute(message, "slab", pairs)
        got = lax.ppermute(send, "slab", pairs)
        halved = tile_bit is not None and bit >= tile_bit
        factor = shape(rows, LANES if halved else width)
        outs = [pair] + ([] if last else [pair])
        outs = outs + ([shape(2, rows, width)] if bit == rounds - 2 else []) + [factor] * 2
        state, *others, mine_scale, their_scale = call(
            scan_body,
            outs,
            (own, other, pay, theirs) + tuple(state),
            bit=bit,
            rounds=rounds,
            chunk=chunk,
            tile_bit=tile_bit,
        )
        if not last:
            pay, message = (others[0], others[-1])
            state = (state,)
        if last:
            break
        split = tile_bit if bit + 1 == tile_bit else None
        kept = shape(colours, rows, LANES) if split is not None else shape(*keep.shape)
        pieces = call(
            light_body,
            [kept] * (1 if split is None else 2),
            (keep, got, mine_scale, their_scale),
            tile_bit=split,
        )
        keep, send = (pieces[0], pieces[-1])

    columns, line, edge = call(
        merge_body,
        [
            shape(channels, 2, planes, rows, width),
            shape(channels * planes + SUB, width),
            shape(rows, LANES),
        ],
        (state, cols5, own, other),
        scratch=[pltpu.VMEM((2, planes, width), F32)],
    )
    line = lax.ppermute(line, "tile", swap)
    mine, message = call(
        gather_body,
        [shape(colours, rows, chunk), shape((colours + 1) * rows, LANES)],
        (edge, line, keep, got, mine_scale, their_scale),
        chunk=chunk,
        half=half,
        halved=tile_bit is not None,
    )
    message = lax.ppermute(message, "dir", swap)
    grad_shape = (channels, planes, rows, width)
    grad = call(
        scatter_body,
        shape(*grad_shape),
        (columns, own, other),
        scratch=[pltpu.VMEM((2, 9, rows, width), F32)],
    )
    voxel_grad, image = call(
        finish_body,
        [shape(*grad_shape), shape(1, colours, rows, chunk)],
        (grad, line, message, mine),
        scratch=[
            pltpu.VMEM(grad_shape, F32),
            pltpu.VMEM((1, colours, rows, chunk), F32),
            pltpu.SemaphoreType.DMA((channels + 1,)),
        ],
        out_specs=[hbm, hbm],
        half=half,
    )
    return (image, voxel_grad)


def solution(mesh):
    return jax.shard_map(
        per_device,
        mesh=mesh,
        in_specs=(
            P(None, "slab", "tile", None),
            P("dir", "tile", None),
            P("dir", "tile", None),
            P("dir", None, "tile", None),
        ),
        out_specs=(P("dir", None, "tile", "slab"), P(None, "slab", "tile", "dir")),
        check_vma=False,
    )
```

```python
import functools

import jax
import jax.numpy as jnp
from jax import lax
from jax.experimental import pallas as pl
from jax.experimental.pallas import tpu as pltpu
from jax.sharding import PartitionSpec as P


LEVELS = 8
BITS = LEVELS.bit_length() - 1
LANES = 128
SUB = 8
F32 = jnp.float32
VMEM = pl.BlockSpec(memory_space=pltpu.VMEM)
MIB = 2**20


def call(body, outs, args, scratch=(), limit=16, specs=None, out_specs=None, **statics):
    def kernel(*refs):
        body(tuple(lax.axis_index(a) for a in ("dir", "tile", "slab")), *refs, **statics)

    grid = {} if specs is None else dict(grid=(1,))
    return pl.pallas_call(
        kernel,
        out_shape=outs,
        in_specs=specs or [VMEM] * len(args),
        out_specs=out_specs or jax.tree.map(lambda _: VMEM, outs),
        scratch_shapes=list(scratch),
        cost_estimate=pl.CostEstimate(flops=10**7, bytes_accessed=2 * 10**6, transcendentals=0),
        compiler_params=pltpu.CompilerParams(vmem_limit_bytes=limit * MIB),
        **grid,
    )(*args)


def shape(*dims):
    return jax.ShapeDtypeStruct(dims, F32)


def iota(dims, axis):
    return lax.broadcasted_iota(jnp.int32, dims, axis)


def fraction(raw):
    return (raw.astype(F32) + 0.5) / LEVELS - 0.5


def three(raw):
    f = fraction(raw)
    return (jnp.maximum(-f, 0.0), 1.0 - jnp.abs(f), jnp.maximum(f, 0.0))


def split_code(code):
    q = code.astype(jnp.int32)
    return (q & (LEVELS - 1), (q >> BITS) & (LEVELS - 1), q >> (2 * BITS))


def logistic(v):
    return 0.5 * jnp.tanh(0.5 * v) + 0.5


def total_of(terms):
    return functools.reduce(lambda a, b: a + b, terms)


def log_soft(v):
    return jnp.maximum(v, 0.0) + jnp.log(1.0 + jnp.exp(-jnp.abs(v)))


def shifts(tiles, beside, h):
    lane = iota(tiles[0].shape, 1)
    last = LANES - 1
    zero = jnp.zeros_like(beside)
    right = [pltpu.roll(x, 1, 1) for x in tiles]
    left = [pltpu.roll(x, last, 1) for x in tiles]
    below = [jnp.where(h == 1, beside, zero)] + right[:-1]
    above = left[1:] + [jnp.where(h == 0, beside, zero)]
    minus = [jnp.where(lane == 0, b, r) for b, r in zip(below, right)]
    plus = [jnp.where(lane == last, a, x) for a, x in zip(above, left)]
    return (minus, tiles, plus)


def beside_shift(source, h):
    target = jnp.where(h == 1, 0, LANES - 1)
    return lax.rem(target - source + LANES, LANES)


def window_parts(h, width):
    base = pl.multiple_of(h * width, LANES)
    side = pl.multiple_of(width - LANES * h, LANES)
    source = jnp.where(h == 0, 0, LANES - 1)
    return base, side, source


def first_body(info, offsets, heading, cotangent, voxels, own, sent, line, code, head, cot, strip, sems, *, width, depth):
    h, t = (info[0], info[1])
    channels, planes, rows, _ = voxels.shape
    row = pl.multiple_of(jnp.where(t == 0, rows - SUB, 0), SUB)
    copies = [
        pltpu.make_async_copy(voxels.at[:, :, pl.ds(row, SUB), :], strip, sems.at[0]),
        pltpu.make_async_copy(offsets, code, sems.at[1]),
        pltpu.make_async_copy(heading, head, sems.at[2]),
        pltpu.make_async_copy(cotangent, cot, sems.at[3]),
    ]
    for copy in copies:
        copy.start()
    copies[0].wait()
    for c in range(channels):
        for k in range(planes):
            line[c, k : k + 1, :] = jnp.where(
                t == 0, strip[c, k, SUB - 1 : SUB, :], strip[c, k, :1, :]
            )
    for copy in copies[1:]:
        copy.wait()
    for out, at in ((own, h), (sent, 1 - h)):
        cols = pl.ds(pl.multiple_of(at * width, LANES), width)
        out[0] = code[0, :, cols].astype(F32)
        out[1] = head[0, :, cols].astype(F32)
        for c in range(channels - 1):
            out[2 + c] = cot[0, c, :, cols] * depth


def message_rows(channels, rows, count):
    body = channels * count * rows
    lines = -(-channels * count // SUB) * SUB
    return body, body + lines, body + lines + SUB


def pack_body(info, first, last, line, out_a, out_b, *, width):
    h, s = (info[0], info[2])
    channels, _, rows, _ = first.shape
    planes = line.shape[1]
    count = width // LANES
    base, side, source = window_parts(h, width)
    at_line, at_edge, _ = message_rows(channels, rows, count)
    lane = iota((rows, LANES), 1)

    def fill(block, k, out):
        edge = jnp.zeros((rows, LANES), F32)
        for c in range(channels):
            for j in range(count):
                at = c * count + j
                cols = pl.ds(base + j * LANES, LANES)
                out[at * rows : (at + 1) * rows, :] = block[c, 0, :, cols]
                out[at_line + at : at_line + at + 1, :] = line[c, k : k + 1, cols]
            cols = pl.ds(side, LANES)
            turn = lax.rem(c - source + LANES, LANES)
            edge = jnp.where(lane == c, pltpu.roll(block[c, 0, :, cols], turn, 1), edge)
            turn = lax.rem(channels + c - source + LANES, LANES)
            corner = jnp.broadcast_to(line[c, k : k + 1, cols], (SUB, LANES))
            corner = pltpu.roll(corner, turn, 1)[:1]
            edge = jnp.where(lane == channels + c, corner, edge)
        out[at_edge:, :rows] = jnp.transpose(edge)[:SUB]

    @pl.when(s % 2 == 0)
    def _():
        fill(last, planes - 1, out_a)
        fill(first, 0, out_b)

    @pl.when(s % 2 == 1)
    def _():
        fill(first, 0, out_a)
        fill(last, planes - 1, out_b)


def spread_message(msg, grid, plane, info, channels, rows, count, live):
    h, t = (info[0], info[1])
    at_line, at_edge, _ = message_rows(channels, rows, count)
    edge = jnp.transpose(
        jnp.concatenate([msg[at_edge:, :] * live, jnp.zeros((LANES - SUB, LANES), F32)], axis=0)
    )[:rows]
    beyond = pl.ds(pl.multiple_of(jnp.where(t == 0, SUB + rows, 0), SUB), SUB)
    for c in range(channels):
        first = c * count
        tiles = [
            msg[(first + j) * rows : (first + j + 1) * rows, :] * live for j in range(count)
        ]
        lines = [
            jnp.broadcast_to(
                msg[at_line + first + j : at_line + first + j + 1, :] * live, (SUB, LANES)
            )
            for j in range(count)
        ]
        side = pltpu.roll(edge, beside_shift(c, h), 1)
        corner = pltpu.roll(edge[:SUB], beside_shift(channels + c, h), 1)
        for e, xs in enumerate(shifts(tiles, side, h)):
            for j, x in enumerate(xs):
                grid[e, c, plane, SUB : SUB + rows, j * LANES : (j + 1) * LANES] = x
        for e, xs in enumerate(shifts(lines, corner, h)):
            for j, x in enumerate(xs):
                grid[e, c, plane, beyond, j * LANES : (j + 1) * LANES] = x


def taps(code, row0, t, rows):
    _, m, n = split_code(code)
    fy, fx = (fraction(m), fraction(n))
    row = iota(code.shape, 0) + row0
    low = (row == 0) & (t == 0)
    high = (row == rows - 1) & (t == 1)
    up = ((fy > 0.0) & jnp.logical_not(high)) | low
    ay, ax = (jnp.abs(fy), jnp.abs(fx))
    gone = (low & (fy < 0.0)) | (high & (fy > 0.0))
    by = jnp.where(gone, 0.0, ay)
    return (up, fx > 0.0, (1.0 - ay) * (1.0 - ax), (1.0 - ay) * ax, by * (1.0 - ax), by * ax)


def bilinear(rays, grid, c, plane, row0, cols):
    v = [
        [grid[e, c, plane, row0 + b + SUB - 1 : row0 + b + 2 * SUB - 1, cols] for e in range(3)]
        for b in range(3)
    ]
    out = []
    for up, right, centre, across, along, diagonal in rays:
        row = [jnp.where(up, v[2][e], v[0][e]) for e in range(3)]
        out.append(
            centre * v[1][1]
            + across * jnp.where(right, v[1][2], v[1][0])
            + along * row[1]
            + diagonal * jnp.where(right, row[2], row[0])
        )
    return out


def ray_tiles(rays, rows, width, t):
    for i in range(rows // SUB):
        for j in range(width // LANES):
            at = slice(i * SUB, (i + 1) * SUB)
            cols = slice(j * LANES, (j + 1) * LANES)
            codes = [r[0, at, cols] for r in rays]
            yield (
                i * SUB,
                at,
                cols,
                [taps(q, i * SUB, t, rows) for q in codes],
                [three(split_code(q)[0]) for q in codes],
            )


def each_tile(rows, width, body, unroll=False):
    count = width // LANES
    if unroll:
        for i in range(rows // SUB):
            for j in range(count):
                body(pl.ds(i * SUB, SUB), pl.ds(j * LANES, LANES))
        return

    def step(n, carry):
        row = pl.ds(pl.multiple_of((n // count) * SUB, SUB), SUB)
        col = pl.ds(pl.multiple_of((n % count) * LANES, LANES), LANES)
        body(row, col)
        return carry

    lax.fori_loop(0, (rows // SUB) * count, step, 0)


def products(left):
    ones = jnp.ones_like(left[0])
    rising, falling = ([ones], [ones])
    for x in left[:-1]:
        rising.append(rising[-1] * x)
    for x in left[:0:-1]:
        falling.append(falling[-1] * x)
    return rising, falling[::-1]


def place_body(info, vox, line, grid, *, width):
    h, t, _ = info
    channels, planes, rows, _ = vox.shape
    count = width // LANES
    base, side, source = window_parts(h, width)
    turn = beside_shift(source, h)

    for k in range(planes):
        for c in range(channels):
            tiles = [vox[c, k, :, pl.ds(base + j * LANES, LANES)] for j in range(count)]
            beside = pltpu.roll(vox[c, k, :, pl.ds(side, LANES)], turn, 1)
            for e, xs in enumerate(shifts(tiles, beside, h)):
                for j, x in enumerate(xs):
                    grid[e, c, k, SUB : SUB + rows, j * LANES : (j + 1) * LANES] = x
    beyond = pl.ds(pl.multiple_of(jnp.where(t == 0, SUB + rows, 0), SUB), SUB)
    for c in range(channels):
        tiles = [line[c, :, pl.ds(base + j * LANES, LANES)] for j in range(count)]
        beside = pltpu.roll(line[c, :, pl.ds(side, LANES)], turn, 1)
        for e, xs in enumerate(shifts(tiles, beside, h)):
            for j, x in enumerate(xs):
                for k in range(planes):
                    grid[e, c, k, beyond, j * LANES : (j + 1) * LANES] = jnp.broadcast_to(
                        x[k : k + 1], (SUB, LANES)
                    )


def inner_body(info, grid, own, other, vals, part, ends, inner, *, scale):
    t = info[1]
    _, rows, width = own.shape
    channels, planes = grid.shape[1:3]
    rays = (own, other)
    for row0, at, cols, yx, wz in ray_tiles(rays, rows, width, t):

        def channel(c, carry, row0=row0, at=at, cols=cols, yx=yx, wz=wz):
            old = [None, None]
            for p in range(planes):
                new = bilinear(yx, grid, c, p, row0, cols)
                for q in range(2):
                    w = wz[q]
                    if p == 0:
                        ends[q, c, 0, at, cols] = w[2] * new[q]
                    elif p == 1:
                        part[q, c, 0, at, cols] = w[1] * old[1][q] + w[2] * new[q]
                    else:
                        vals[q, c, p - 2, at, cols] = (
                            w[0] * old[0][q] + w[1] * old[1][q] + w[2] * new[q]
                        )
                    if p == planes - 1:
                        part[q, c, 1, at, cols] = w[0] * old[1][q] + w[1] * new[q]
                        ends[q, c, 1, at, cols] = w[0] * new[q]
                old = [old[1], new]
            return carry

        lax.fori_loop(0, channels, channel, 0)

    for q in range(2):

        def shade(row, col, q=q):
            ahead = rays[q][1, row, col] == 0.0
            sigma = [log_soft(vals[q, 0, k, row, col]) * scale for k in range(planes - 2)]
            left = [jnp.exp(-x) for x in sigma]
            rising, falling = products(left)
            light = [None] * (channels - 1)
            for k in range(planes - 2):
                glow = jnp.where(ahead, rising[k], falling[k]) * (1.0 - left[k])
                for c in range(channels - 1):
                    term = glow * logistic(vals[q, c + 1, k, row, col])
                    light[c] = term if k == 0 else light[c] + term
            inner[0, q, row, col] = total_of(sigma)
            for c in range(channels - 1):
                inner[c + 1, q, row, col] = light[c]

        each_tile(rows, width, shade)


def chunk_mask(s, chunk):
    bit = (iota((SUB, LANES), 1) >> (chunk.bit_length() - 1)) & 1
    mine = s & 1
    return bit == mine, jnp.where(mine == 1, LANES - chunk, chunk)


def rim_body(info, near_a, near_b, own, other, part, ends, inner, pay, rim, ends_out, keep, send, grid, *, scale, chunk, slabs):
    t, s = (info[1], info[2])
    _, channels, _, rows, width = part.shape
    count = width // LANES
    even = s % 2 == 0
    rays = (own, other)
    inside = jnp.where((s == 0) | (s == slabs - 1), 0.0, 1.0)
    spread_message(near_a, grid, jnp.where(even, 1, 0), info, channels, rows, count, 1.0)
    spread_message(near_b, grid, jnp.where(even, 0, 1), info, channels, rows, count, inside)
    for row0, at, cols, yx, wz in ray_tiles(rays, rows, width, t):

        def channel(c, carry, row0=row0, at=at, cols=cols, yx=yx, wz=wz):
            for p in range(2):
                new = bilinear(yx, grid, c, p, row0, cols)
                for q in range(2):
                    rim[q, c, p, at, cols] = part[q, c, p, at, cols] + wz[q][2 * p] * new[q]
                    ends_out[q, c, p, at, cols] = ends[q, c, p, at, cols] + wz[q][1] * new[q]
            return carry

        lax.fori_loop(0, channels, channel, 0)
    kept, turn = chunk_mask(s, chunk)

    def shade(row, col):
        lights = []
        for q in range(2):
            ahead = rays[q][1, row, col] == 0.0
            sigma = [log_soft(rim[q, 0, p, row, col]) * scale for p in range(2)]
            left = [jnp.exp(-x) for x in sigma]
            middle = inner[0, q, row, col]
            through = jnp.exp(-middle)
            first = jnp.where(ahead, left[0], left[1])
            last = first * through
            pay[0, q, row, col] = sigma[0] + middle + sigma[1]
            low = jnp.where(ahead, 1.0, last) * (1.0 - left[0])
            high = jnp.where(ahead, last, 1.0) * (1.0 - left[1])
            light = [
                low * logistic(rim[q, c + 1, 0, row, col])
                + first * inner[c + 1, q, row, col]
                + high * logistic(rim[q, c + 1, 1, row, col])
                for c in range(channels - 1)
            ]
            pay[1, q, row, col] = total_of([rays[q][2 + c, row, col] * x for c, x in enumerate(light)])
            lights.append(light)
        for c, (a, b) in enumerate(zip(*lights)):
            keep[c, row, col] = jnp.where(kept, a, pltpu.roll(b, turn, 1))
            send[c, row, col] = jnp.where(kept, pltpu.roll(b, LANES - turn, 1), a)

    each_tile(rows, width, shade, unroll=True)


def column_body(info, own, other, vals, rim, ends, cols5, *, scale, slabs):
    s = info[2]
    _, channels, inside, rows, width = vals.shape
    planes = inside + 2
    rays = (own, other)
    live = {-1: jnp.where(s > 0, 1.0, 0.0), planes: jnp.where(s < slabs - 1, 1.0, 0.0)}
    for q in range(2):

        def shade(row, col, q=q):
            ahead = rays[q][1, row, col] == 0.0
            wz = three(split_code(rays[q][0, row, col])[0])
            pull = [rays[q][2 + c, row, col] for c in range(channels - 1)]

            def value(c, k):
                if k in live:
                    return ends[q, c, 1 if k > 0 else 0, row, col]
                if k == 0 or k == planes - 1:
                    return rim[q, c, 1 if k else 0, row, col]
                return vals[q, c, k - 1, row, col]

            ks = range(planes)
            every = range(-1, planes + 1)
            sigma = {k: log_soft(value(0, k)) * scale for k in every}
            slope = {k: logistic(value(0, k)) * scale for k in every}
            left = {k: jnp.exp(-sigma[k]) for k in every}
            rising, falling = products([left[k] for k in ks])
            through = rising[-1] * left[planes - 1]
            share, after = ({}, {})
            tint = [{} for _ in range(channels - 1)]
            for k in every:
                if k == -1:
                    reach = jnp.where(ahead, jnp.exp(sigma[k]), through)
                elif k == planes:
                    reach = jnp.where(ahead, through, jnp.exp(sigma[k]))
                else:
                    reach = jnp.where(ahead, rising[k], falling[k])
                glow = reach * (1.0 - left[k])
                if k in live:
                    glow = glow * live[k]
                    slope[k] = slope[k] * live[k]
                hue = []
                for c in range(channels - 1):
                    colour = logistic(value(c + 1, k))
                    hue.append(pull[c] * colour)
                    tint[c][k] = glow * hue[-1] * (1.0 - colour)
                hue = total_of(hue)
                share[k] = glow * hue
                after[k] = reach * left[k] * hue
            whole = total_of([share[k] for k in ks])
            run = -share[-1]
            pushed = {}
            for k in every:
                upto = run + share[k]
                pushed[k] = (after[k] + jnp.where(ahead, upto, whole - run)) * slope[k]
                run = upto
            for n, field in enumerate([pushed, slope] + tint):
                for p in ks:
                    cols5[n, q, p, row, col] = (
                        wz[1] * field[p] + wz[2] * field[p - 1] + wz[0] * field[p + 1]
                    )

        each_tile(rows, width, shade)


def ray_order(info, bit, heading):
    lower = ((info[2] >> bit) & 1) == 1
    return heading == jnp.where(lower, 0.0, 1.0)


def scan_body(info, own, other, block, theirs, *refs, bit, rounds, chunk, tile_bit):
    first = bit == 0
    last = bit == rounds - 1
    refs = list(refs)
    state = None if first else refs.pop(0)
    out_state = refs.pop(0)
    out_block = None if last else refs.pop(0)
    out_final = refs.pop(0) if bit == rounds - 2 else None
    mine_scale, their_scale = refs
    rays = (own, other)
    _, rows, width = own.shape
    kept, turn = chunk_mask(info[2], chunk)
    halved = tile_bit is not None and bit >= tile_bit
    my_tile = (info[2] >> (tile_bit or 0)) & 1

    def ray(row, col):
        scales = []
        for q in range(2):
            heading = rays[q][1, row, col]
            earlier = ray_order(info, bit, heading)
            depth = block[0, q, row, col]
            before = jnp.zeros_like(depth) if first else state[0, q, row, col]
            rest = block[1, q, row, col] if first else state[1, q, row, col]
            if last:
                their_depth = their_light = theirs[q, row, col]
            else:
                their_depth, their_light = (theirs[n, q, row, col] for n in range(2))
            fade = jnp.exp(-depth)
            their_fade = jnp.exp(-their_depth)
            later = fade if first else jnp.exp(before - depth)
            out_rest = rest + jnp.where(earlier, 0.0, later * their_light)
            out_before = before + jnp.where(earlier, their_depth, 0.0)
            if last:
                reach = jnp.exp(-out_before)
                out_state[0, q, row, col] = reach
                out_state[1, q, row, col] = reach * out_rest
            else:
                out_state[0, q, row, col] = out_before
                out_state[1, q, row, col] = out_rest
                light = block[1, q, row, col]
                out_depth = depth + their_depth
                out_light = jnp.where(
                    earlier, their_light + their_fade * light, light + fade * their_light
                )
                out_block[0, q, row, col] = out_depth
                out_block[1, q, row, col] = out_light
                if out_final is not None:
                    out_final[q, row, col] = jnp.where(
                        ray_order(info, bit + 1, heading), out_light, out_depth
                    )
            scales.append((jnp.where(earlier, their_fade, 1.0), jnp.where(earlier, 1.0, fade)))
        return [jnp.where(kept, a, pltpu.roll(b, turn, 1)) for a, b in zip(*scales)]

    for i in range(rows // SUB):
        row = pl.ds(i * SUB, SUB)
        packed = [ray(row, pl.ds(j, LANES)) for j in range(0, width, LANES)]
        for n, out in enumerate((mine_scale, their_scale)):
            if halved:
                out[row, :] = jnp.where(my_tile == 0, packed[0][n], packed[1][n])
                continue
            for j, x in enumerate(packed):
                out[row, j * LANES : (j + 1) * LANES] = x[n]


def light_body(info, keep, got, mine_scale, their_scale, *outs, tile_bit):
    mine, theirs = (mine_scale[...], their_scale[...])
    if tile_bit is None:
        for c in range(keep.shape[0]):
            outs[0][c] = mine * keep[c] + theirs * got[c]
        return
    tile = (info[2] >> tile_bit) & 1
    for c in range(keep.shape[0]):
        both = mine * keep[c] + theirs * got[c]
        low, high = (both[:, :LANES], both[:, LANES:])
        outs[0][c] = jnp.where(tile == 0, low, high)
        outs[1][c] = jnp.where(tile == 0, high, low)


def gather_body(info, edge, line, keep, got, mine_scale, their_scale, mine, out, *, chunk, half, halved):
    _, t, s = info
    rows = edge.shape[0]
    body = line.shape[0] - SUB
    start = lax.rem(s, half) * chunk
    base = 0 if halved else (start // LANES) * LANES
    cols = pl.ds(pl.multiple_of(base, LANES), LANES)
    start = lax.rem(start, LANES)
    there = jnp.where(lax.rem(s, 2) == 1, start - chunk, start + chunk)
    border = iota((rows, LANES), 0) == jnp.where(t == 0, rows - 1, 0)
    out[:rows, :] = edge[...] + jnp.where(border, line[body : body + 1, :LANES], 0.0)
    for c in range(keep.shape[0]):
        both = mine_scale[:, cols] * keep[c, :, cols] + their_scale[:, cols] * got[c, :, cols]
        mine[c] = pltpu.roll(both, lax.rem(LANES - start, LANES), 1)[:, :chunk]
        out[(c + 1) * rows : (c + 2) * rows, :] = pltpu.roll(
            both, lax.rem(LANES - there, LANES), 1
        )


def strips_body(info, cols5, own, other, rows5, packs, down, across):
    h, t, _ = info
    fields, _, planes, rows, width = cols5.shape
    last = LANES - 1
    side = pl.ds(pl.multiple_of(jnp.where(h == 0, width - LANES, 0), LANES), LANES)
    source = jnp.where(h == 0, last, 0)
    lane = iota((rows, LANES), 1)
    for q, r in enumerate((own, other)):
        code = jnp.where(t == 0, r[0, rows - 1 : rows, :], r[0, :1, :])
        _, wy, wx = [three(x) for x in split_code(jnp.broadcast_to(code, (planes, width)))]
        y = jnp.where(t == 0, wy[2], wy[0])
        for e in range(3):
            down[q, e] = y * wx[e]
        code = pltpu.roll(r[0, :, side], lax.rem(LANES - source, LANES), 1)
        _, wy, wx = [three(x) for x in split_code(jnp.broadcast_to(code[:, :1], (rows, LANES)))]
        x = jnp.where(h == 0, wx[2], wx[0])
        for b in range(3):
            across[q, b] = wy[b] * x
        both = [jnp.zeros((rows, LANES), F32) for _ in range(2)]
        for n in range(fields):
            for p in range(planes):
                rows5[q, n, p : p + 1, :] = jnp.where(
                    t == 0, cols5[n, q, p, rows - 1 : rows, :], cols5[n, q, p, :1, :]
                )
                at = p if n < 2 else (n - 1) * planes + p
                turn = lax.rem(at - source + LANES, LANES)
                k = 1 if n == 1 else 0
                both[k] = jnp.where(
                    lane == at, pltpu.roll(cols5[n, q, p, :, side], turn, 1), both[k]
                )
        for k in range(2):
            packs[q, k] = both[k]


def border_body(info, reach_rest, rows5, packs, down, across, line, edge):
    h, t, _ = info
    _, fields, planes, width = rows5.shape
    rows = edge.shape[0]
    last = LANES - 1
    lane = iota((planes, width), 1)
    row = iota((rows, LANES), 0)

    def at_row(n, q):
        x = jnp.where(t == 0, reach_rest[n, q, rows - 1 : rows, :], reach_rest[n, q, :1, :])
        return jnp.broadcast_to(x, (planes, width))

    near = [at_row(0, q) for q in range(2)]
    far = [at_row(1, q) for q in range(2)]
    for c in range(fields - 1):
        strip = [near[q] * rows5[q, c + 1 if c else 0] for q in range(2)]
        if c == 0:
            strip = [strip[q] - far[q] * rows5[q, 1] for q in range(2)]
        minus, same, plus = [
            down[0, e] * strip[0] + down[1, e] * strip[1] for e in range(3)
        ]
        plus = jnp.where(lane == 0, 0.0, pltpu.roll(plus, 1, 1))
        minus = jnp.where(lane == width - 1, 0.0, pltpu.roll(minus, width - 1, 1))
        line[c * planes : (c + 1) * planes, :] = same + plus + minus

    side = pl.ds(pl.multiple_of(jnp.where(h == 0, width - LANES, 0), LANES), LANES)
    turn = lax.rem(LANES - jnp.where(h == 0, last, 0), LANES)

    def at_column(n, q):
        x = pltpu.roll(reach_rest[n, q, :, side], turn, 1)
        return jnp.broadcast_to(x[:, :1], (rows, LANES))

    packed = [
        at_column(0, q) * packs[q, 0] - at_column(1, q) * packs[q, 1] for q in range(2)
    ]
    part = [across[0, b] * packed[0] + across[1, b] * packed[1] for b in range(3)]
    lower = pltpu.roll(part[2], 1, 0)
    upper = pltpu.roll(part[0], rows - 1, 0)
    edge[...] = (
        part[1] + jnp.where(row == 0, 0.0, lower) + jnp.where(row == rows - 1, 0.0, upper)
    )
    line[(fields - 1) * planes :, :LANES] = jnp.where(
        t == 0, lower[:SUB], pltpu.roll(upper[rows - SUB :], 1, 0)
    )


def scatter_body(_, reach_rest, cols5, own, other, grad, weights):
    fields, _, planes, rows, width = cols5.shape
    channels = fields - 1
    lane = iota((rows, width), 1)
    row = iota((rows, width), 0)
    for q, r in enumerate((own, other)):
        _, wy, wx = [three(x) for x in split_code(r[0])]
        for b in range(3):
            for e in range(3):
                weights[q, b * 3 + e] = wy[b] * wx[e]

    def plane(p, carry):
        for c in range(channels):
            col = [reach_rest[0, q] * cols5[c + 1 if c else 0, q, p] for q in range(2)]
            if c == 0:
                col = [col[q] - reach_rest[1, q] * cols5[1, q, p] for q in range(2)]
            summed = []
            for e in range(3):
                part = [
                    weights[0, b * 3 + e] * col[0] + weights[1, b * 3 + e] * col[1]
                    for b in range(3)
                ]
                down = pltpu.roll(part[2], 1, 0)
                up = pltpu.roll(part[0], rows - 1, 0)
                summed.append(
                    part[1] + jnp.where(row == 0, 0.0, down) + jnp.where(row == rows - 1, 0.0, up)
                )
            right = pltpu.roll(summed[2], 1, 1)
            left = pltpu.roll(summed[0], width - 1, 1)
            grad[c, p] = (
                summed[1]
                + jnp.where(lane == 0, 0.0, right)
                + jnp.where(lane == width - 1, 0.0, left)
            )
        return carry

    lax.fori_loop(0, planes, plane, 0)


def finish_body(info, grad_in, line, cross, mine, grad, image, buffer, picture, sems, *, half):
    h, t, s = info
    channels, planes, rows, width = buffer.shape
    source = jnp.where(h == 0, LANES - 1, 0)
    side = pl.ds(pl.multiple_of(jnp.where(h == 0, width - LANES, 0), LANES), LANES)
    last = jnp.where(t == 0, rows - 1, 0)
    at_row = iota((rows, width), 0) == last
    at_lane = iota((rows, LANES), 1) == source
    packed = cross[:rows, :]
    here = s // half == h
    for c in range(channels - 1):
        picture[0, c] = jnp.where(here, mine[c], cross[(c + 1) * rows : (c + 2) * rows, : picture.shape[3]])
    copies = [pltpu.make_async_copy(picture, image, sems.at[channels])]
    copies[0].start()
    for c in range(channels):
        for p in range(planes):
            at = c * planes + p
            buffer[c, p] = grad_in[c, p] + jnp.where(at_row, line[at : at + 1, :], 0.0)
            turn = lax.rem(source - at + LANES, LANES)
            buffer[c, p, :, side] += jnp.where(at_lane, pltpu.roll(packed, turn, 1), 0.0)
        copies.append(pltpu.make_async_copy(buffer.at[c], grad.at[c], sems.at[c]))
        copies[-1].start()
    for copy in copies:
        copy.wait()


def per_device(voxels, offsets, heading, cotangent):
    channels, planes, rows, total = voxels.shape
    dirs, slabs, cores = (lax.axis_size(a) for a in ("dir", "slab", "tile"))
    if dirs != 2 or cores != 2 or slabs & (slabs - 1) or 2 * total > slabs * LANES:
        raise ValueError("mesh")
    if 2 * channels > SUB:
        raise ValueError("channels")
    width = total // dirs
    depth = planes * slabs
    scale = 2.0 / depth
    swap = [(0, 1), (1, 0)]
    count = width // LANES
    grid = lambda n: pltpu.VMEM((3, channels, n, rows + 2 * SUB, width), F32)
    colours = channels - 1
    half = slabs // dirs
    chunk = total // slabs
    rounds = slabs.bit_length() - 1
    tile_bit = (LANES // chunk).bit_length() - 1
    tile_bit = tile_bit if 0 < tile_bit < rounds - 1 else None

    pairs_a = [(i, i ^ 1) for i in range(slabs)]
    pairs_b = [(i, i + 1) for i in range(1, slabs - 1, 2)]
    pairs_b = [(a * cores + i, b * cores + i) for a, b in pairs_b for i in range(cores)]
    pairs_b = pairs_b + [(b, a) for a, b in pairs_b]
    pairs_b = pairs_b + [
        (a * cores + i, a * cores + 1 - i) for a in (0, slabs - 1) for i in range(cores)
    ]

    hbm = pl.BlockSpec(memory_space=pltpu.HBM)
    ray = shape(channels + 1, rows, width)
    own, sent, line = call(
        first_body,
        [ray, ray, shape(channels, planes, total)],
        tuple(
            pltpu.with_memory_space_constraint(x, pltpu.HBM)
            for x in (offsets, heading, cotangent, voxels)
        ),
        specs=[hbm] * 4,
        scratch=[
            pltpu.VMEM(offsets.shape, jnp.int32),
            pltpu.VMEM(heading.shape, jnp.int32),
            pltpu.VMEM(cotangent.shape, F32),
            pltpu.VMEM((channels, planes, SUB, total), F32),
            pltpu.SemaphoreType.DMA((4,)),
        ],
        limit=8,
        width=width,
        depth=depth,
    )
    line = lax.ppermute(line, "tile", swap)
    other = lax.ppermute(sent, "dir", swap)

    def block(k):
        return pl.BlockSpec((channels, 1, rows, total), lambda i: (0, k, 0, 0))

    near = call(
        pack_body,
        [shape(message_rows(channels, rows, count)[2], LANES)] * 2,
        (voxels, voxels, line),
        specs=[block(0), block(planes - 1), VMEM],
        width=width,
    )
    near = list(near)
    near[0] = lax.ppermute(near[0], "slab", pairs_a)
    near[1] = lax.ppermute(near[1], ("slab", "tile"), pairs_b)

    two = shape(2, channels, 2, rows, width)
    pair = shape(2, 2, rows, width)
    placed = call(
        place_body, shape(3, channels, planes, rows + 2 * SUB, width), (voxels, line), width=width
    )
    vals, part, ends, inner = call(
        inner_body,
        [shape(2, channels, planes - 2, rows, width), two, two, shape(channels, 2, rows, width)],
        (placed, own, other),
        scale=scale,
    )
    light = shape(colours, rows, width)
    pay, rim, ends, keep, send = call(
        rim_body,
        [pair, two, two, light, light],
        (*near, own, other, part, ends, inner),
        scratch=[grid(2)],
        scale=scale,
        chunk=chunk,
        slabs=slabs,
    )
    cols5 = call(
        column_body,
        shape(channels + 1, 2, planes, rows, width),
        (own, other, vals, rim, ends),
        scale=scale,
        slabs=slabs,
    )

    strips = call(
        strips_body,
        [
            shape(2, channels + 1, planes, width),
            shape(2, 2, rows, LANES),
            shape(2, 3, planes, width),
            shape(2, 3, rows, LANES),
        ],
        (cols5, own, other),
    )

    message, state = (pay, ())
    for bit in range(rounds):
        pairs = [(i, i ^ (1 << bit)) for i in range(slabs)]
        last = bit == rounds - 1
        theirs = lax.ppermute(message, "slab", pairs)
        got = lax.ppermute(send, "slab", pairs)
        halved = tile_bit is not None and bit >= tile_bit
        factor = shape(rows, LANES if halved else width)
        outs = [pair] + ([] if last else [pair])
        outs = outs + ([shape(2, rows, width)] if bit == rounds - 2 else []) + [factor] * 2
        state, *others, mine_scale, their_scale = call(
            scan_body,
            outs,
            (own, other, pay, theirs) + tuple(state),
            bit=bit,
            rounds=rounds,
            chunk=chunk,
            tile_bit=tile_bit,
        )
        if not last:
            pay, message = (others[0], others[-1])
            state = (state,)
        if last:
            break
        split = tile_bit if bit + 1 == tile_bit else None
        kept = shape(colours, rows, LANES) if split is not None else shape(*keep.shape)
        pieces = call(
            light_body,
            [kept] * (1 if split is None else 2),
            (keep, got, mine_scale, their_scale),
            tile_bit=split,
        )
        keep, send = (pieces[0], pieces[-1])

    line, edge = call(
        border_body, [shape(channels * planes + SUB, width), shape(rows, LANES)], (state, *strips)
    )
    line = lax.ppermute(line, "tile", swap)
    mine, message = call(
        gather_body,
        [shape(colours, rows, chunk), shape((colours + 1) * rows, LANES)],
        (edge, line, keep, got, mine_scale, their_scale),
        chunk=chunk,
        half=half,
        halved=tile_bit is not None,
    )
    message = lax.ppermute(message, "dir", swap)
    grad_shape = (channels, planes, rows, width)
    grad = call(
        scatter_body,
        shape(*grad_shape),
        (state, cols5, own, other),
        scratch=[pltpu.VMEM((2, 9, rows, width), F32)],
    )
    voxel_grad, image = call(
        finish_body,
        [shape(*grad_shape), shape(1, colours, rows, chunk)],
        (grad, line, message, mine),
        scratch=[
            pltpu.VMEM(grad_shape, F32),
            pltpu.VMEM((1, colours, rows, chunk), F32),
            pltpu.SemaphoreType.DMA((channels + 1,)),
        ],
        out_specs=[hbm, hbm],
        half=half,
    )
    return (image, voxel_grad)


def solution(mesh):
    return jax.shard_map(
        per_device,
        mesh=mesh,
        in_specs=(
            P(None, "slab", "tile", None),
            P("dir", "tile", None),
            P("dir", "tile", None),
            P("dir", None, "tile", None),
        ),
        out_specs=(P("dir", None, "tile", "slab"), P(None, "slab", "tile", "dir")),
        check_vma=False,
    )
```

```python
import functools

import jax
import jax.numpy as jnp
from jax import lax
from jax.experimental import pallas as pl
from jax.experimental.pallas import tpu as pltpu
from jax.sharding import PartitionSpec as P


LEVELS = 8
BITS = LEVELS.bit_length() - 1
LANES = 128
SUB = 8
F32 = jnp.float32
VMEM = pl.BlockSpec(memory_space=pltpu.VMEM)
MIB = 2**20


def call(body, outs, args, scratch=(), limit=16, specs=None, out_specs=None, **statics):
    def kernel(*refs):
        body(tuple(lax.axis_index(a) for a in ("dir", "tile", "slab")), *refs, **statics)

    grid = {} if specs is None else dict(grid=(1,))
    return pl.pallas_call(
        kernel,
        out_shape=outs,
        in_specs=specs or [VMEM] * len(args),
        out_specs=out_specs or jax.tree.map(lambda _: VMEM, outs),
        scratch_shapes=list(scratch),
        cost_estimate=pl.CostEstimate(flops=10**7, bytes_accessed=2 * 10**6, transcendentals=0),
        compiler_params=pltpu.CompilerParams(vmem_limit_bytes=limit * MIB),
        **grid,
    )(*args)


def shape(*dims):
    return jax.ShapeDtypeStruct(dims, F32)


def iota(dims, axis):
    return lax.broadcasted_iota(jnp.int32, dims, axis)


def fraction(raw):
    return (raw.astype(F32) + 0.5) / LEVELS - 0.5


def three(raw):
    f = fraction(raw)
    return (jnp.maximum(-f, 0.0), 1.0 - jnp.abs(f), jnp.maximum(f, 0.0))


def split_code(code):
    q = code.astype(jnp.int32)
    return (q & (LEVELS - 1), (q >> BITS) & (LEVELS - 1), q >> (2 * BITS))


def logistic(v):
    return 0.5 * jnp.tanh(0.5 * v) + 0.5


def total_of(terms):
    return functools.reduce(lambda a, b: a + b, terms)


def log_soft(v):
    return jnp.maximum(v, 0.0) + jnp.log(1.0 + jnp.exp(-jnp.abs(v)))


def shifts(tiles, beside, h):
    lane = iota(tiles[0].shape, 1)
    last = LANES - 1
    zero = jnp.zeros_like(beside)
    right = [pltpu.roll(x, 1, 1) for x in tiles]
    left = [pltpu.roll(x, last, 1) for x in tiles]
    below = [jnp.where(h == 1, beside, zero)] + right[:-1]
    above = left[1:] + [jnp.where(h == 0, beside, zero)]
    minus = [jnp.where(lane == 0, b, r) for b, r in zip(below, right)]
    plus = [jnp.where(lane == last, a, x) for a, x in zip(above, left)]
    return (minus, tiles, plus)


def beside_shift(source, h):
    target = jnp.where(h == 1, 0, LANES - 1)
    return lax.rem(target - source + LANES, LANES)


def window_parts(h, width):
    base = pl.multiple_of(h * width, LANES)
    side = pl.multiple_of(width - LANES * h, LANES)
    source = jnp.where(h == 0, 0, LANES - 1)
    return base, side, source


def first_body(info, offsets, heading, cotangent, voxels, own, sent, line, code, head, cot, strip, sems, *, width, depth):
    h, t = (info[0], info[1])
    channels, planes, rows, _ = voxels.shape
    row = pl.multiple_of(jnp.where(t == 0, rows - SUB, 0), SUB)
    copies = [
        pltpu.make_async_copy(voxels.at[:, :, pl.ds(row, SUB), :], strip, sems.at[0]),
        pltpu.make_async_copy(offsets, code, sems.at[1]),
        pltpu.make_async_copy(heading, head, sems.at[2]),
        pltpu.make_async_copy(cotangent, cot, sems.at[3]),
    ]
    for copy in copies:
        copy.start()
    copies[0].wait()
    for c in range(channels):
        for k in range(planes):
            line[c, k : k + 1, :] = jnp.where(
                t == 0, strip[c, k, SUB - 1 : SUB, :], strip[c, k, :1, :]
            )
    for copy in copies[1:]:
        copy.wait()
    for out, at in ((own, h), (sent, 1 - h)):
        cols = pl.ds(pl.multiple_of(at * width, LANES), width)
        out[0] = code[0, :, cols].astype(F32)
        out[1] = head[0, :, cols].astype(F32)
        for c in range(channels - 1):
            out[2 + c] = cot[0, c, :, cols] * depth


def message_rows(channels, rows, count):
    body = channels * count * rows
    lines = -(-channels * count // SUB) * SUB
    return body, body + lines, body + lines + SUB


def pack_body(info, first, last, line, out_a, out_b, *, width):
    h, s = (info[0], info[2])
    channels, _, rows, _ = first.shape
    planes = line.shape[1]
    count = width // LANES
    base, side, source = window_parts(h, width)
    at_line, at_edge, _ = message_rows(channels, rows, count)
    lane = iota((rows, LANES), 1)

    def fill(block, k, out):
        edge = jnp.zeros((rows, LANES), F32)
        for c in range(channels):
            for j in range(count):
                at = c * count + j
                cols = pl.ds(base + j * LANES, LANES)
                out[at * rows : (at + 1) * rows, :] = block[c, 0, :, cols]
                out[at_line + at : at_line + at + 1, :] = line[c, k : k + 1, cols]
            cols = pl.ds(side, LANES)
            turn = lax.rem(c - source + LANES, LANES)
            edge = jnp.where(lane == c, pltpu.roll(block[c, 0, :, cols], turn, 1), edge)
            turn = lax.rem(channels + c - source + LANES, LANES)
            corner = jnp.broadcast_to(line[c, k : k + 1, cols], (SUB, LANES))
            corner = pltpu.roll(corner, turn, 1)[:1]
            edge = jnp.where(lane == channels + c, corner, edge)
        out[at_edge:, :rows] = jnp.transpose(edge)[:SUB]

    @pl.when(s % 2 == 0)
    def _():
        fill(last, planes - 1, out_a)
        fill(first, 0, out_b)

    @pl.when(s % 2 == 1)
    def _():
        fill(first, 0, out_a)
        fill(last, planes - 1, out_b)


def spread_message(msg, grid, plane, info, channels, rows, count, live):
    h, t = (info[0], info[1])
    at_line, at_edge, _ = message_rows(channels, rows, count)
    edge = jnp.transpose(
        jnp.concatenate([msg[at_edge:, :] * live, jnp.zeros((LANES - SUB, LANES), F32)], axis=0)
    )[:rows]
    beyond = pl.ds(pl.multiple_of(jnp.where(t == 0, SUB + rows, 0), SUB), SUB)
    for c in range(channels):
        first = c * count
        tiles = [
            msg[(first + j) * rows : (first + j + 1) * rows, :] * live for j in range(count)
        ]
        lines = [
            jnp.broadcast_to(
                msg[at_line + first + j : at_line + first + j + 1, :] * live, (SUB, LANES)
            )
            for j in range(count)
        ]
        side = pltpu.roll(edge, beside_shift(c, h), 1)
        corner = pltpu.roll(edge[:SUB], beside_shift(channels + c, h), 1)
        for e, xs in enumerate(shifts(tiles, side, h)):
            for j, x in enumerate(xs):
                grid[e, c, plane, SUB : SUB + rows, j * LANES : (j + 1) * LANES] = x
        for e, xs in enumerate(shifts(lines, corner, h)):
            for j, x in enumerate(xs):
                grid[e, c, plane, beyond, j * LANES : (j + 1) * LANES] = x


def taps(code, row0, t, rows):
    _, m, n = split_code(code)
    fy, fx = (fraction(m), fraction(n))
    row = iota(code.shape, 0) + row0
    low = (row == 0) & (t == 0)
    high = (row == rows - 1) & (t == 1)
    up = ((fy > 0.0) & jnp.logical_not(high)) | low
    ay, ax = (jnp.abs(fy), jnp.abs(fx))
    gone = (low & (fy < 0.0)) | (high & (fy > 0.0))
    by = jnp.where(gone, 0.0, ay)
    return (up, fx > 0.0, (1.0 - ay) * (1.0 - ax), (1.0 - ay) * ax, by * (1.0 - ax), by * ax)


def bilinear(rays, grid, c, plane, row0, cols):
    v = [
        [grid[e, c, plane, row0 + b + SUB - 1 : row0 + b + 2 * SUB - 1, cols] for e in range(3)]
        for b in range(3)
    ]
    out = []
    for up, right, centre, across, along, diagonal in rays:
        row = [jnp.where(up, v[2][e], v[0][e]) for e in range(3)]
        out.append(
            centre * v[1][1]
            + across * jnp.where(right, v[1][2], v[1][0])
            + along * row[1]
            + diagonal * jnp.where(right, row[2], row[0])
        )
    return out


def ray_tiles(rays, rows, width, t):
    for i in range(rows // SUB):
        for j in range(width // LANES):
            at = slice(i * SUB, (i + 1) * SUB)
            cols = slice(j * LANES, (j + 1) * LANES)
            codes = [r[0, at, cols] for r in rays]
            yield (
                i * SUB,
                at,
                cols,
                [taps(q, i * SUB, t, rows) for q in codes],
                [three(split_code(q)[0]) for q in codes],
            )


def each_tile(rows, width, body, unroll=False):
    count = width // LANES
    if unroll:
        for i in range(rows // SUB):
            for j in range(count):
                body(pl.ds(i * SUB, SUB), pl.ds(j * LANES, LANES))
        return

    def step(n, carry):
        row = pl.ds(pl.multiple_of((n // count) * SUB, SUB), SUB)
        col = pl.ds(pl.multiple_of((n % count) * LANES, LANES), LANES)
        body(row, col)
        return carry

    lax.fori_loop(0, (rows // SUB) * count, step, 0)


def products(left):
    ones = jnp.ones_like(left[0])
    rising, falling = ([ones], [ones])
    for x in left[:-1]:
        rising.append(rising[-1] * x)
    for x in left[:0:-1]:
        falling.append(falling[-1] * x)
    return rising, falling[::-1]


def place_body(info, vox, line, grid, *, width):
    h, t, _ = info
    channels, planes, rows, _ = vox.shape
    count = width // LANES
    base, side, source = window_parts(h, width)
    turn = beside_shift(source, h)

    for k in range(planes):
        for c in range(channels):
            tiles = [vox[c, k, :, pl.ds(base + j * LANES, LANES)] for j in range(count)]
            beside = pltpu.roll(vox[c, k, :, pl.ds(side, LANES)], turn, 1)
            for e, xs in enumerate(shifts(tiles, beside, h)):
                for j, x in enumerate(xs):
                    grid[e, c, k, SUB : SUB + rows, j * LANES : (j + 1) * LANES] = x
    beyond = pl.ds(pl.multiple_of(jnp.where(t == 0, SUB + rows, 0), SUB), SUB)
    for c in range(channels):
        tiles = [line[c, :, pl.ds(base + j * LANES, LANES)] for j in range(count)]
        beside = pltpu.roll(line[c, :, pl.ds(side, LANES)], turn, 1)
        for e, xs in enumerate(shifts(tiles, beside, h)):
            for j, x in enumerate(xs):
                for k in range(planes):
                    grid[e, c, k, beyond, j * LANES : (j + 1) * LANES] = jnp.broadcast_to(
                        x[k : k + 1], (SUB, LANES)
                    )


def inner_body(info, grid, own, other, vals, part, ends, inner, *, scale):
    t = info[1]
    _, rows, width = own.shape
    channels, planes = grid.shape[1:3]
    rays = (own, other)
    for row0, at, cols, yx, wz in ray_tiles(rays, rows, width, t):

        def channel(c, carry, row0=row0, at=at, cols=cols, yx=yx, wz=wz):
            old = [None, None]
            for p in range(planes):
                new = bilinear(yx, grid, c, p, row0, cols)
                for q in range(2):
                    w = wz[q]
                    if p == 0:
                        ends[q, c, 0, at, cols] = w[2] * new[q]
                    elif p == 1:
                        part[q, c, 0, at, cols] = w[1] * old[1][q] + w[2] * new[q]
                    else:
                        vals[q, c, p - 2, at, cols] = (
                            w[0] * old[0][q] + w[1] * old[1][q] + w[2] * new[q]
                        )
                    if p == planes - 1:
                        part[q, c, 1, at, cols] = w[0] * old[1][q] + w[1] * new[q]
                        ends[q, c, 1, at, cols] = w[0] * new[q]
                old = [old[1], new]
            return carry

        lax.fori_loop(0, channels, channel, 0)

    for q in range(2):

        def shade(row, col, q=q):
            ahead = rays[q][1, row, col] == 0.0
            sigma = [log_soft(vals[q, 0, k, row, col]) * scale for k in range(planes - 2)]
            left = [jnp.exp(-x) for x in sigma]
            rising, falling = products(left)
            light = [None] * (channels - 1)
            for k in range(planes - 2):
                glow = jnp.where(ahead, rising[k], falling[k]) * (1.0 - left[k])
                for c in range(channels - 1):
                    term = glow * logistic(vals[q, c + 1, k, row, col])
                    light[c] = term if k == 0 else light[c] + term
            inner[0, q, row, col] = total_of(sigma)
            for c in range(channels - 1):
                inner[c + 1, q, row, col] = light[c]

        each_tile(rows, width, shade)


def chunk_mask(s, chunk):
    bit = (iota((SUB, LANES), 1) >> (chunk.bit_length() - 1)) & 1
    mine = s & 1
    return bit == mine, jnp.where(mine == 1, LANES - chunk, chunk)


def rim_body(info, near_a, near_b, own, other, part, ends, inner, pay, rim, ends_out, keep, send, grid, *, scale, chunk, slabs):
    t, s = (info[1], info[2])
    _, channels, _, rows, width = part.shape
    count = width // LANES
    even = s % 2 == 0
    rays = (own, other)
    inside = jnp.where((s == 0) | (s == slabs - 1), 0.0, 1.0)
    spread_message(near_a, grid, jnp.where(even, 1, 0), info, channels, rows, count, 1.0)
    spread_message(near_b, grid, jnp.where(even, 0, 1), info, channels, rows, count, inside)
    for row0, at, cols, yx, wz in ray_tiles(rays, rows, width, t):

        def channel(c, carry, row0=row0, at=at, cols=cols, yx=yx, wz=wz):
            for p in range(2):
                new = bilinear(yx, grid, c, p, row0, cols)
                for q in range(2):
                    rim[q, c, p, at, cols] = part[q, c, p, at, cols] + wz[q][2 * p] * new[q]
                    ends_out[q, c, p, at, cols] = ends[q, c, p, at, cols] + wz[q][1] * new[q]
            return carry

        lax.fori_loop(0, channels, channel, 0)
    kept, turn = chunk_mask(s, chunk)

    def shade(row, col):
        lights = []
        for q in range(2):
            ahead = rays[q][1, row, col] == 0.0
            sigma = [log_soft(rim[q, 0, p, row, col]) * scale for p in range(2)]
            left = [jnp.exp(-x) for x in sigma]
            middle = inner[0, q, row, col]
            through = jnp.exp(-middle)
            first = jnp.where(ahead, left[0], left[1])
            last = first * through
            pay[0, q, row, col] = sigma[0] + middle + sigma[1]
            low = jnp.where(ahead, 1.0, last) * (1.0 - left[0])
            high = jnp.where(ahead, last, 1.0) * (1.0 - left[1])
            light = [
                low * logistic(rim[q, c + 1, 0, row, col])
                + first * inner[c + 1, q, row, col]
                + high * logistic(rim[q, c + 1, 1, row, col])
                for c in range(channels - 1)
            ]
            pay[1, q, row, col] = total_of([rays[q][2 + c, row, col] * x for c, x in enumerate(light)])
            lights.append(light)
        for c, (a, b) in enumerate(zip(*lights)):
            keep[c, row, col] = jnp.where(kept, a, pltpu.roll(b, turn, 1))
            send[c, row, col] = jnp.where(kept, pltpu.roll(b, LANES - turn, 1), a)

    each_tile(rows, width, shade, unroll=True)


def column_body(info, own, other, vals, rim, ends, cols5, *, scale, slabs):
    s = info[2]
    _, channels, inside, rows, width = vals.shape
    planes = inside + 2
    rays = (own, other)
    live = {-1: jnp.where(s > 0, 1.0, 0.0), planes: jnp.where(s < slabs - 1, 1.0, 0.0)}
    for q in range(2):

        def shade(row, col, q=q):
            ahead = rays[q][1, row, col] == 0.0
            wz = three(split_code(rays[q][0, row, col])[0])
            pull = [rays[q][2 + c, row, col] for c in range(channels - 1)]

            def value(c, k):
                if k in live:
                    return ends[q, c, 1 if k > 0 else 0, row, col]
                if k == 0 or k == planes - 1:
                    return rim[q, c, 1 if k else 0, row, col]
                return vals[q, c, k - 1, row, col]

            ks = range(planes)
            every = range(-1, planes + 1)
            sigma = {k: log_soft(value(0, k)) * scale for k in every}
            slope = {k: logistic(value(0, k)) * scale for k in every}
            left = {k: jnp.exp(-sigma[k]) for k in every}
            rising, falling = products([left[k] for k in ks])
            through = rising[-1] * left[planes - 1]
            share, after = ({}, {})
            tint = [{} for _ in range(channels - 1)]
            for k in every:
                if k == -1:
                    reach = jnp.where(ahead, jnp.exp(sigma[k]), through)
                elif k == planes:
                    reach = jnp.where(ahead, through, jnp.exp(sigma[k]))
                else:
                    reach = jnp.where(ahead, rising[k], falling[k])
                glow = reach * (1.0 - left[k])
                if k in live:
                    glow = glow * live[k]
                    slope[k] = slope[k] * live[k]
                hue = []
                for c in range(channels - 1):
                    colour = logistic(value(c + 1, k))
                    hue.append(pull[c] * colour)
                    tint[c][k] = glow * hue[-1] * (1.0 - colour)
                hue = total_of(hue)
                share[k] = glow * hue
                after[k] = reach * left[k] * hue
            whole = total_of([share[k] for k in ks])
            run = -share[-1]
            pushed = {}
            for k in every:
                upto = run + share[k]
                pushed[k] = (after[k] + jnp.where(ahead, upto, whole - run)) * slope[k]
                run = upto
            for n, field in enumerate([pushed, slope] + tint):
                for p in ks:
                    cols5[n, q, p, row, col] = (
                        wz[1] * field[p] + wz[2] * field[p - 1] + wz[0] * field[p + 1]
                    )

        each_tile(rows, width, shade)


def ray_order(info, bit, heading):
    lower = ((info[2] >> bit) & 1) == 1
    return heading == jnp.where(lower, 0.0, 1.0)


def scan_body(info, own, other, block, theirs, *refs, bit, rounds, chunk, tile_bit):
    first = bit == 0
    last = bit == rounds - 1
    refs = list(refs)
    state = None if first else refs.pop(0)
    out_state = refs.pop(0)
    out_block = None if last else refs.pop(0)
    out_final = refs.pop(0) if bit == rounds - 2 else None
    mine_scale, their_scale = refs
    rays = (own, other)
    _, rows, width = own.shape
    kept, turn = chunk_mask(info[2], chunk)
    halved = tile_bit is not None and bit >= tile_bit
    my_tile = (info[2] >> (tile_bit or 0)) & 1

    def ray(row, col):
        scales = []
        for q in range(2):
            heading = rays[q][1, row, col]
            earlier = ray_order(info, bit, heading)
            depth = block[0, q, row, col]
            before = jnp.zeros_like(depth) if first else state[0, q, row, col]
            rest = block[1, q, row, col] if first else state[1, q, row, col]
            if last:
                their_depth = their_light = theirs[q, row, col]
            else:
                their_depth, their_light = (theirs[n, q, row, col] for n in range(2))
            fade = jnp.exp(-depth)
            their_fade = jnp.exp(-their_depth)
            later = fade if first else jnp.exp(before - depth)
            out_rest = rest + jnp.where(earlier, 0.0, later * their_light)
            out_before = before + jnp.where(earlier, their_depth, 0.0)
            if last:
                reach = jnp.exp(-out_before)
                out_state[0, q, row, col] = reach
                out_state[1, q, row, col] = reach * out_rest
            else:
                out_state[0, q, row, col] = out_before
                out_state[1, q, row, col] = out_rest
                light = block[1, q, row, col]
                out_depth = depth + their_depth
                out_light = jnp.where(
                    earlier, their_light + their_fade * light, light + fade * their_light
                )
                out_block[0, q, row, col] = out_depth
                out_block[1, q, row, col] = out_light
                if out_final is not None:
                    out_final[q, row, col] = jnp.where(
                        ray_order(info, bit + 1, heading), out_light, out_depth
                    )
            scales.append((jnp.where(earlier, their_fade, 1.0), jnp.where(earlier, 1.0, fade)))
        return [jnp.where(kept, a, pltpu.roll(b, turn, 1)) for a, b in zip(*scales)]

    for i in range(rows // SUB):
        row = pl.ds(i * SUB, SUB)
        packed = [ray(row, pl.ds(j, LANES)) for j in range(0, width, LANES)]
        for n, out in enumerate((mine_scale, their_scale)):
            if halved:
                out[row, :] = jnp.where(my_tile == 0, packed[0][n], packed[1][n])
                continue
            for j, x in enumerate(packed):
                out[row, j * LANES : (j + 1) * LANES] = x[n]


def light_body(info, keep, got, mine_scale, their_scale, *outs, tile_bit):
    mine, theirs = (mine_scale[...], their_scale[...])
    if tile_bit is None:
        for c in range(keep.shape[0]):
            outs[0][c] = mine * keep[c] + theirs * got[c]
        return
    tile = (info[2] >> tile_bit) & 1
    for c in range(keep.shape[0]):
        both = mine * keep[c] + theirs * got[c]
        low, high = (both[:, :LANES], both[:, LANES:])
        outs[0][c] = jnp.where(tile == 0, low, high)
        outs[1][c] = jnp.where(tile == 0, high, low)


def corner_body(info, edge, line, out):
    rows = edge.shape[0]
    body = line.shape[0] - SUB
    border = iota((rows, LANES), 0) == jnp.where(info[1] == 0, rows - 1, 0)
    out[...] = edge[...] + jnp.where(border, line[body : body + 1, :LANES], 0.0)


def gather_body(info, keep, got, mine_scale, their_scale, mine, sent, *, chunk, half, halved):
    s = info[2]
    start = lax.rem(s, half) * chunk
    base = 0 if halved else (start // LANES) * LANES
    cols = pl.ds(pl.multiple_of(base, LANES), LANES)
    start = lax.rem(start, LANES)
    there = jnp.where(lax.rem(s, 2) == 1, start - chunk, start + chunk)
    for c in range(keep.shape[0]):
        both = mine_scale[:, cols] * keep[c, :, cols] + their_scale[:, cols] * got[c, :, cols]
        mine[c] = pltpu.roll(both, lax.rem(LANES - start, LANES), 1)[:, :chunk]
        sent[c] = pltpu.roll(both, lax.rem(LANES - there, LANES), 1)[:, :chunk]


def choose_body(info, mine, theirs, image, *, half):
    image[0] = jnp.where(info[2] // half == info[0], mine[...], theirs[...])


def strips_body(info, cols5, own, other, rows5, packs, down, across):
    h, t, _ = info
    fields, _, planes, rows, width = cols5.shape
    last = LANES - 1
    side = pl.ds(pl.multiple_of(jnp.where(h == 0, width - LANES, 0), LANES), LANES)
    source = jnp.where(h == 0, last, 0)
    lane = iota((rows, LANES), 1)
    for q, r in enumerate((own, other)):
        code = jnp.where(t == 0, r[0, rows - 1 : rows, :], r[0, :1, :])
        _, wy, wx = [three(x) for x in split_code(jnp.broadcast_to(code, (planes, width)))]
        y = jnp.where(t == 0, wy[2], wy[0])
        for e in range(3):
            down[q, e] = y * wx[e]
        code = pltpu.roll(r[0, :, side], lax.rem(LANES - source, LANES), 1)
        _, wy, wx = [three(x) for x in split_code(jnp.broadcast_to(code[:, :1], (rows, LANES)))]
        x = jnp.where(h == 0, wx[2], wx[0])
        for b in range(3):
            across[q, b] = wy[b] * x
        both = [jnp.zeros((rows, LANES), F32) for _ in range(2)]
        for n in range(fields):
            for p in range(planes):
                rows5[q, n, p : p + 1, :] = jnp.where(
                    t == 0, cols5[n, q, p, rows - 1 : rows, :], cols5[n, q, p, :1, :]
                )
                at = p if n < 2 else (n - 1) * planes + p
                turn = lax.rem(at - source + LANES, LANES)
                k = 1 if n == 1 else 0
                both[k] = jnp.where(
                    lane == at, pltpu.roll(cols5[n, q, p, :, side], turn, 1), both[k]
                )
        for k in range(2):
            packs[q, k] = both[k]


def border_body(info, reach_rest, rows5, packs, down, across, line, edge):
    h, t, _ = info
    _, fields, planes, width = rows5.shape
    rows = edge.shape[0]
    last = LANES - 1
    lane = iota((planes, width), 1)
    row = iota((rows, LANES), 0)

    def at_row(n, q):
        x = jnp.where(t == 0, reach_rest[n, q, rows - 1 : rows, :], reach_rest[n, q, :1, :])
        return jnp.broadcast_to(x, (planes, width))

    near = [at_row(0, q) for q in range(2)]
    far = [at_row(1, q) for q in range(2)]
    for c in range(fields - 1):
        strip = [near[q] * rows5[q, c + 1 if c else 0] for q in range(2)]
        if c == 0:
            strip = [strip[q] - far[q] * rows5[q, 1] for q in range(2)]
        minus, same, plus = [
            down[0, e] * strip[0] + down[1, e] * strip[1] for e in range(3)
        ]
        plus = jnp.where(lane == 0, 0.0, pltpu.roll(plus, 1, 1))
        minus = jnp.where(lane == width - 1, 0.0, pltpu.roll(minus, width - 1, 1))
        line[c * planes : (c + 1) * planes, :] = same + plus + minus

    side = pl.ds(pl.multiple_of(jnp.where(h == 0, width - LANES, 0), LANES), LANES)
    turn = lax.rem(LANES - jnp.where(h == 0, last, 0), LANES)

    def at_column(n, q):
        x = pltpu.roll(reach_rest[n, q, :, side], turn, 1)
        return jnp.broadcast_to(x[:, :1], (rows, LANES))

    packed = [
        at_column(0, q) * packs[q, 0] - at_column(1, q) * packs[q, 1] for q in range(2)
    ]
    part = [across[0, b] * packed[0] + across[1, b] * packed[1] for b in range(3)]
    lower = pltpu.roll(part[2], 1, 0)
    upper = pltpu.roll(part[0], rows - 1, 0)
    edge[...] = (
        part[1] + jnp.where(row == 0, 0.0, lower) + jnp.where(row == rows - 1, 0.0, upper)
    )
    line[(fields - 1) * planes :, :LANES] = jnp.where(
        t == 0, lower[:SUB], pltpu.roll(upper[rows - SUB :], 1, 0)
    )


def scatter_body(_, reach_rest, cols5, own, other, grad, weights):
    fields, _, planes, rows, width = cols5.shape
    channels = fields - 1
    lane = iota((rows, width), 1)
    row = iota((rows, width), 0)
    for q, r in enumerate((own, other)):
        _, wy, wx = [three(x) for x in split_code(r[0])]
        for b in range(3):
            for e in range(3):
                weights[q, b * 3 + e] = wy[b] * wx[e]

    def plane(p, carry):
        for c in range(channels):
            col = [reach_rest[0, q] * cols5[c + 1 if c else 0, q, p] for q in range(2)]
            if c == 0:
                col = [col[q] - reach_rest[1, q] * cols5[1, q, p] for q in range(2)]
            summed = []
            for e in range(3):
                part = [
                    weights[0, b * 3 + e] * col[0] + weights[1, b * 3 + e] * col[1]
                    for b in range(3)
                ]
                down = pltpu.roll(part[2], 1, 0)
                up = pltpu.roll(part[0], rows - 1, 0)
                summed.append(
                    part[1] + jnp.where(row == 0, 0.0, down) + jnp.where(row == rows - 1, 0.0, up)
                )
            right = pltpu.roll(summed[2], 1, 1)
            left = pltpu.roll(summed[0], width - 1, 1)
            grad[c, p] = (
                summed[1]
                + jnp.where(lane == 0, 0.0, right)
                + jnp.where(lane == width - 1, 0.0, left)
            )
        return carry

    lax.fori_loop(0, planes, plane, 0)


def finish_body(info, grad_in, line, edge, grad, buffer, sems):
    h, t, _ = info
    channels, planes, rows, width = buffer.shape
    source = jnp.where(h == 0, LANES - 1, 0)
    side = pl.ds(pl.multiple_of(jnp.where(h == 0, width - LANES, 0), LANES), LANES)
    last = jnp.where(t == 0, rows - 1, 0)
    at_row = iota((rows, width), 0) == last
    at_lane = iota((rows, LANES), 1) == source
    packed = edge[...]
    copies = []
    for c in range(channels):
        for p in range(planes):
            at = c * planes + p
            buffer[c, p] = grad_in[c, p] + jnp.where(at_row, line[at : at + 1, :], 0.0)
            turn = lax.rem(source - at + LANES, LANES)
            buffer[c, p, :, side] += jnp.where(at_lane, pltpu.roll(packed, turn, 1), 0.0)
        copies.append(pltpu.make_async_copy(buffer.at[c], grad.at[c], sems.at[c]))
        copies[-1].start()
    for copy in copies:
        copy.wait()


def per_device(voxels, offsets, heading, cotangent):
    channels, planes, rows, total = voxels.shape
    dirs, slabs, cores = (lax.axis_size(a) for a in ("dir", "slab", "tile"))
    if dirs != 2 or cores != 2 or slabs & (slabs - 1) or 2 * total > slabs * LANES:
        raise ValueError("mesh")
    if 2 * channels > SUB:
        raise ValueError("channels")
    width = total // dirs
    depth = planes * slabs
    scale = 2.0 / depth
    swap = [(0, 1), (1, 0)]
    count = width // LANES
    grid = lambda n: pltpu.VMEM((3, channels, n, rows + 2 * SUB, width), F32)
    colours = channels - 1
    half = slabs // dirs
    chunk = total // slabs
    rounds = slabs.bit_length() - 1
    tile_bit = (LANES // chunk).bit_length() - 1
    tile_bit = tile_bit if 0 < tile_bit < rounds - 1 else None

    pairs_a = [(i, i ^ 1) for i in range(slabs)]
    pairs_b = [(i, i + 1) for i in range(1, slabs - 1, 2)]
    pairs_b = [(a * cores + i, b * cores + i) for a, b in pairs_b for i in range(cores)]
    pairs_b = pairs_b + [(b, a) for a, b in pairs_b]
    pairs_b = pairs_b + [
        (a * cores + i, a * cores + 1 - i) for a in (0, slabs - 1) for i in range(cores)
    ]

    hbm = pl.BlockSpec(memory_space=pltpu.HBM)
    ray = shape(channels + 1, rows, width)
    own, sent, line = call(
        first_body,
        [ray, ray, shape(channels, planes, total)],
        tuple(
            pltpu.with_memory_space_constraint(x, pltpu.HBM)
            for x in (offsets, heading, cotangent, voxels)
        ),
        specs=[hbm] * 4,
        scratch=[
            pltpu.VMEM(offsets.shape, jnp.int32),
            pltpu.VMEM(heading.shape, jnp.int32),
            pltpu.VMEM(cotangent.shape, F32),
            pltpu.VMEM((channels, planes, SUB, total), F32),
            pltpu.SemaphoreType.DMA((4,)),
        ],
        limit=8,
        width=width,
        depth=depth,
    )
    line = lax.ppermute(line, "tile", swap)
    other = lax.ppermute(sent, "dir", swap)

    def block(k):
        return pl.BlockSpec((channels, 1, rows, total), lambda i: (0, k, 0, 0))

    near = call(
        pack_body,
        [shape(message_rows(channels, rows, count)[2], LANES)] * 2,
        (voxels, voxels, line),
        specs=[block(0), block(planes - 1), VMEM],
        width=width,
    )
    near = list(near)
    near[0] = lax.ppermute(near[0], "slab", pairs_a)
    near[1] = lax.ppermute(near[1], ("slab", "tile"), pairs_b)

    two = shape(2, channels, 2, rows, width)
    pair = shape(2, 2, rows, width)
    placed = call(
        place_body, shape(3, channels, planes, rows + 2 * SUB, width), (voxels, line), width=width
    )
    vals, part, ends, inner = call(
        inner_body,
        [shape(2, channels, planes - 2, rows, width), two, two, shape(channels, 2, rows, width)],
        (placed, own, other),
        scale=scale,
    )
    light = shape(colours, rows, width)
    pay, rim, ends, keep, send = call(
        rim_body,
        [pair, two, two, light, light],
        (*near, own, other, part, ends, inner),
        scratch=[grid(2)],
        scale=scale,
        chunk=chunk,
        slabs=slabs,
    )
    cols5 = call(
        column_body,
        shape(channels + 1, 2, planes, rows, width),
        (own, other, vals, rim, ends),
        scale=scale,
        slabs=slabs,
    )

    strips = call(
        strips_body,
        [
            shape(2, channels + 1, planes, width),
            shape(2, 2, rows, LANES),
            shape(2, 3, planes, width),
            shape(2, 3, rows, LANES),
        ],
        (cols5, own, other),
    )

    message, state = (pay, ())
    for bit in range(rounds):
        pairs = [(i, i ^ (1 << bit)) for i in range(slabs)]
        last = bit == rounds - 1
        theirs = lax.ppermute(message, "slab", pairs)
        got = lax.ppermute(send, "slab", pairs)
        halved = tile_bit is not None and bit >= tile_bit
        factor = shape(rows, LANES if halved else width)
        outs = [pair] + ([] if last else [pair])
        outs = outs + ([shape(2, rows, width)] if bit == rounds - 2 else []) + [factor] * 2
        state, *others, mine_scale, their_scale = call(
            scan_body,
            outs,
            (own, other, pay, theirs) + tuple(state),
            bit=bit,
            rounds=rounds,
            chunk=chunk,
            tile_bit=tile_bit,
        )
        if not last:
            pay, message = (others[0], others[-1])
            state = (state,)
        if last:
            break
        split = tile_bit if bit + 1 == tile_bit else None
        kept = shape(colours, rows, LANES) if split is not None else shape(*keep.shape)
        pieces = call(
            light_body,
            [kept] * (1 if split is None else 2),
            (keep, got, mine_scale, their_scale),
            tile_bit=split,
        )
        keep, send = (pieces[0], pieces[-1])

    line, edge = call(
        border_body, [shape(channels * planes + SUB, width), shape(rows, LANES)], (state, *strips)
    )
    line = lax.ppermute(line, "tile", swap)
    edge = call(corner_body, shape(rows, LANES), (edge, line))
    edge = lax.ppermute(edge, "dir", swap)
    piece = shape(colours, rows, chunk)
    mine, sent = call(
        gather_body,
        [piece, piece],
        (keep, got, mine_scale, their_scale),
        chunk=chunk,
        half=half,
        halved=tile_bit is not None,
    )
    theirs = lax.ppermute(sent, "dir", swap)
    grad_shape = (channels, planes, rows, width)
    grad = call(
        scatter_body,
        shape(*grad_shape),
        (state, cols5, own, other),
        scratch=[pltpu.VMEM((2, 9, rows, width), F32)],
    )
    voxel_grad = call(
        finish_body,
        shape(*grad_shape),
        (grad, line, edge),
        scratch=[pltpu.VMEM(grad_shape, F32), pltpu.SemaphoreType.DMA((channels,))],
        out_specs=hbm,
    )
    image = call(choose_body, shape(1, colours, rows, chunk), (mine, theirs), half=half)
    return (image, voxel_grad)


def solution(mesh):
    return jax.shard_map(
        per_device,
        mesh=mesh,
        in_specs=(
            P(None, "slab", "tile", None),
            P("dir", "tile", None),
            P("dir", "tile", None),
            P("dir", None, "tile", None),
        ),
        out_specs=(P("dir", None, "tile", "slab"), P(None, "slab", "tile", "dir")),
        check_vma=False,
    )
```
